32 devices in a mesh: edge: 8 (over z, y), grp: 4 (over x, core).
Axes of the slice: x: 2, y: 2, z: 4, core: 2. Of those that a mesh axis runs over, the one named last changes fastest.
Arguments:
- edge_lat: bfloat16 [4, 8192, 512], P('grp', 'edge'), may hold values from -6 to 6
- node_lat: bfloat16 [4, 512, 512], P('grp', 'edge'), may hold values from -6 to 6
- edge_cot: bfloat16 [4, 8192, 512], P('grp', 'edge'), may hold values from -3 to 3
- node_cot: bfloat16 [4, 512, 512], P('grp', 'edge'), may hold values from -9 to 9
- senders: int32 [4, 8192], P('grp', 'edge'), may hold values from 0 to 511
- receivers: int32 [4, 8192], P('grp', 'edge'), may hold values from 0 to 511
- edge_count: int32 [4, 8], P('grp', 'edge'), may hold values from 512 to 1024, as said below
- w_edge_in: float32 [1536, 512], P(('edge', 'grp')), may hold values from -0.15625 to 0.15625
- w_edge_out: float32 [512, 512], P(('edge', 'grp')), may hold values from -0.25 to 0.25
- w_node_in: float32 [1024, 512], P(('edge', 'grp'))
- w_node_out: float32 [512, 512], P(('edge', 'grp')), may hold values from -0.25 to 0.25
- small_params: float32 [8, 512], P(None, ('edge', 'grp'))
- first_edge_in: float32 [1536, 512], P(('edge', 'grp'))
- first_edge_out: float32 [512, 512], P(('edge', 'grp'))
- first_node_in: float32 [1024, 512], P(('edge', 'grp'))
- first_node_out: float32 [512, 512], P(('edge', 'grp'))
- first_small: float32 [8, 512], P(None, ('edge', 'grp'))
- second_edge_in: float32 [1536, 512], P(('edge', 'grp')), as said below
- second_edge_out: float32 [512, 512], P(('edge', 'grp'))
- second_node_in: float32 [1024, 512], P(('edge', 'grp'))
- second_node_out: float32 [512, 512], P(('edge', 'grp'))
- second_small: float32 [8, 512], P(None, ('edge', 'grp'))
Outputs:
- edge_new: bfloat16 [4, 8192, 512], P('grp', 'edge')
- node_new: bfloat16 [4, 512, 512], P('grp', 'edge')
- edge_grad: bfloat16 [4, 8192, 512], P('grp', 'edge')
- node_grad: bfloat16 [4, 512, 512], P('grp', 'edge')
- grad_edge_in: float32 [1536, 512], P(('edge', 'grp'))
- grad_edge_out: float32 [512, 512], P(('edge', 'grp'))
- grad_node_in: float32 [1024, 512], P(('edge', 'grp'))
- grad_node_out: float32 [512, 512], P(('edge', 'grp'))
- grad_small: float32 [8, 512], P(None, ('edge', 'grp'))
- second_edge_in_new: float32 [1536, 512], P(('edge', 'grp'))
- second_edge_out_new: float32 [512, 512], P(('edge', 'grp'))
- second_node_in_new: float32 [1024, 512], P(('edge', 'grp'))
- second_node_out_new: float32 [512, 512], P(('edge', 'grp'))
- second_small_new: float32 [8, 512], P(None, ('edge', 'grp'))
- w_edge_in_new: float32 [1536, 512], P(('edge', 'grp'))
- w_edge_out_new: float32 [512, 512], P(('edge', 'grp'))
- w_node_in_new: float32 [1024, 512], P(('edge', 'grp'))
- w_node_out_new: float32 [512, 512], P(('edge', 'grp'))
- small_new: float32 [8, 512], P(None, ('edge', 'grp'))
The draws below stay inside these ranges and needn't reach their ends.
Inputs may be any that keep to these rules, and one draw needn't show every extreme that they name: `edge_count`: in each sample one shard has all 1024 slots live; live slots come first in a shard. `senders`: node index within the sample's multimesh, also in padded slots. `receivers`: node index within the sample's multimesh, also in padded slots. `second_edge_in`: Positive.
All inputs are finite; a program needn't handle non-finite values.
Results may differ from the reference program's by a relative error of at most 0.011.
Values may be sent and summed in bfloat16 or wider, within the bound.
A program may use at most 128 MiB of HBM per device.

```python
import jax
import jax.numpy as jnp
from jax import lax

D = 512
EDGE_DEV = 1024
GROUPS = 4
SHARDS = 8
EDGES = 8192
NODES = 512
LIVE_EDGES = 24576
ALL_NODES = 2048


def draw_edge_count(key, part):
    counts = jax.random.randint(jax.random.fold_in(key, 1), (GROUPS, SHARDS), EDGE_DEV // 2, EDGE_DEV + 1)
    full = jax.random.randint(jax.random.fold_in(key, 2), (GROUPS,), 0, SHARDS)
    ranks = jnp.arange(SHARDS, dtype=jnp.int32)[None, :]
    return jnp.where(ranks == full[:, None], EDGE_DEV, counts).astype(jnp.int32)


def draw_small_params(key, part):
    gains = jax.random.uniform(jax.random.fold_in(key, 3), (8, D), jnp.float32, 0.5, 1.5)
    shifts = jax.random.uniform(jax.random.fold_in(key, 4), (8, D), jnp.float32, -0.5, 0.5)
    rows = jnp.arange(8)[:, None]
    return jnp.where((rows == 2) | (rows == 6), gains, shifts)


def draw_w_node_in(key, part):
    values = jax.random.normal(jax.random.fold_in(key, 9), (2 * D, D), jnp.float32)
    rows = jnp.where(jnp.arange(2 * D)[:, None] < D, 1.0, 1.0 / 6.0).astype(jnp.float32)
    return values * rows / jnp.sqrt(jnp.float32(2 * D))


def first_moment(key, shape, count, scale_rows):
    values = jax.random.normal(jax.random.fold_in(key, 5), shape, jnp.float32)
    return values * 0.11 * jnp.sqrt(jnp.float32(count)) * scale_rows


def second_moment(key, shape, count, scale_rows):
    spread = jax.random.uniform(jax.random.fold_in(key, 6), shape, jnp.float32, jnp.log(1.0), jnp.log(4.0))
    return 0.001 * jnp.float32(count) * jnp.exp(spread) * scale_rows * scale_rows


def node_rows_scale():
    return jnp.where(jnp.arange(2 * D)[:, None] < D, 1.4, 8.4).astype(jnp.float32)


def small_counts():
    return jnp.where(jnp.arange(8)[:, None] < 4, jnp.float32(LIVE_EDGES), jnp.float32(ALL_NODES))


def small_scales():
    table = jnp.array([0.45, 0.75, 0.5, 0.5, 1.4, 2.25, 1.5, 1.5], jnp.float32)
    return table[:, None]


def draw_first_edge_in(key, part):
    return first_moment(key, (3 * D, D), LIVE_EDGES, 0.45)


def draw_first_edge_out(key, part):
    return first_moment(key, (D, D), LIVE_EDGES, 0.45)


def draw_first_node_in(key, part):
    return first_moment(key, (2 * D, D), ALL_NODES, node_rows_scale())


def draw_first_node_out(key, part):
    return first_moment(key, (D, D), ALL_NODES, 1.35)


def draw_first_small(key, part):
    values = jax.random.normal(jax.random.fold_in(key, 7), (8, D), jnp.float32)
    return values * 0.11 * jnp.sqrt(small_counts()) * small_scales()


def draw_second_edge_in(key, part):
    return second_moment(key, (3 * D, D), LIVE_EDGES, 0.45)


def draw_second_edge_out(key, part):
    return second_moment(key, (D, D), LIVE_EDGES, 0.45)


def draw_second_node_in(key, part):
    return second_moment(key, (2 * D, D), ALL_NODES, node_rows_scale())


def draw_second_node_out(key, part):
    return second_moment(key, (D, D), ALL_NODES, 1.35)


def draw_second_small(key, part):
    spread = jax.random.uniform(jax.random.fold_in(key, 8), (8, D), jnp.float32, jnp.log(1.0), jnp.log(4.0))
    scales = small_scales()
    return 0.001 * small_counts() * jnp.exp(spread) * scales * scales


def touch_ends(values, key, smallest, largest):
    longest = values.shape.index(max(values.shape))
    spots = []
    for shift in (0, 1):
        where = [jax.random.randint(jax.random.fold_in(key, axis), (), 0, length) for axis, length in enumerate(values.shape)]
        where[longest] = (where[longest] + shift) % values.shape[longest]
        spots.append(tuple(where))
    return values.at[spots[0]].set(smallest).at[spots[1]].set(largest)


def block_levels(stream_key, dims, pieces, smallest, high):
    loudness = 1.0
    for dim, shards_of in pieces:
        draws = jax.random.uniform(jax.random.fold_in(jax.random.fold_in(stream_key, 6), dim), (shards_of,), jnp.float32, smallest / len(pieces), high / len(pieces))
        loudness = loudness * jnp.repeat(jnp.exp(draws), dims[dim] // shards_of).reshape((-1,) + (1,) * (len(dims) - 1 - dim))
    return loudness


def noise(key, shape, scale, bound, shards=(), held_as=jnp.bfloat16):
    entries = scale * jax.random.normal(key, shape, jnp.float32)
    if shards:
        entries = entries * block_levels(key, shape, shards, -0.22, 0.18)
    return jnp.clip(entries, -bound, bound).astype(held_as)


def setup_inputs(seed: int = 0) -> dict:
    streams_of = jax.random.split(jax.random.key(seed), 23)
    return {
        "edge_lat": noise(streams_of[0], (GROUPS, EDGES, D), 1.0, 6.0, ((0, 4), (1, 8))),
        "node_lat": noise(streams_of[1], (GROUPS, NODES, D), 1.0, 6.0, ((0, 4), (1, 8))),
        "edge_cot": noise(streams_of[2], (GROUPS, EDGES, D), 0.5, 3.0, ((0, 4), (1, 8))),
        "node_cot": noise(streams_of[3], (GROUPS, NODES, D), 1.5, 9.0, ((0, 4), (1, 8))),
        "senders": touch_ends(jax.random.randint(streams_of[4], (GROUPS, EDGES), 0, NODES), jax.random.fold_in(streams_of[4], 1), 0, NODES - 1).astype(jnp.int32),
        "receivers": touch_ends(jax.random.randint(streams_of[5], (GROUPS, EDGES), 0, NODES), jax.random.fold_in(streams_of[5], 1), 0, NODES - 1).astype(jnp.int32),
        "edge_count": draw_edge_count(jax.random.fold_in(streams_of[22], 71), 0),
        "w_edge_in": noise(streams_of[7], (3 * D, D), (3 * D) ** -0.5, 0.15625, ((0, 32),), jnp.float32),
        "w_edge_out": noise(streams_of[8], (D, D), D ** -0.5, 0.25, ((0, 32),), jnp.float32),
        "w_node_in": draw_w_node_in(jax.random.fold_in(streams_of[22], 71), 0),
        "w_node_out": noise(streams_of[10], (D, D), D ** -0.5, 0.25, ((0, 32),), jnp.float32),
        "small_params": draw_small_params(jax.random.fold_in(streams_of[22], 71), 0),
        "first_edge_in": draw_first_edge_in(jax.random.fold_in(streams_of[22], 71), 0),
        "first_edge_out": draw_first_edge_out(jax.random.fold_in(streams_of[22], 71), 0),
        "first_node_in": draw_first_node_in(jax.random.fold_in(streams_of[22], 71), 0),
        "first_node_out": draw_first_node_out(jax.random.fold_in(streams_of[22], 71), 0),
        "first_small": draw_first_small(jax.random.fold_in(streams_of[22], 71), 0),
        "second_edge_in": draw_second_edge_in(jax.random.fold_in(streams_of[22], 71), 0),
        "second_edge_out": draw_second_edge_out(jax.random.fold_in(streams_of[22], 71), 0),
        "second_node_in": draw_second_node_in(jax.random.fold_in(streams_of[22], 71), 0),
        "second_node_out": draw_second_node_out(jax.random.fold_in(streams_of[22], 71), 0),
        "second_small": draw_second_small(jax.random.fold_in(streams_of[22], 71), 0),
    }


@jax.custom_vjp
def low(v):
    return lax.optimization_barrier(v.astype(jnp.bfloat16)).astype(jnp.float32)

@jax.custom_vjp
def low_back(v):
    return v

def low_keep(v):
    return (low(v), None)

def low_pass(kept, grad):
    return (grad,)

def back_keep(v):
    return (v, None)

def back_low(kept, grad):
    return (low(grad),)
low.defvjp(low_keep, low_pass)
low_back.defvjp(back_keep, back_low)
step_count = 10.0

def matmul(left, right):
    return jnp.dot(left, right, precision=lax.Precision.HIGHEST, preferred_element_type=jnp.float32)

def layer_norm(values, gain, shift):
    mean = lax.optimization_barrier(jnp.mean(values, axis=-1, keepdims=True))
    centred = values - mean
    var = lax.optimization_barrier(jnp.mean(centred * centred, axis=-1, keepdims=True))
    return centred * lax.rsqrt(var + 1e-05) * gain + shift

def group_forward(edges, nodes, w1e, w2e, w1n, w2n, small, send, recv, maskf):
    nodes_low = low(nodes)
    w1e = low(w1e)
    w2e = low(w2e)
    w1n = low(w1n)
    w2n = low(w2n)
    small = low(small)

    def edge_block(inputs):
        e_blk, s_blk, r_blk, m_blk = inputs
        joined = jnp.concatenate([low(e_blk), nodes_low[s_blk], nodes_low[r_blk]], axis=1)
        pre = low_back(matmul(joined, w1e) + small[0])
        hidden = low(jax.nn.silu(pre))
        out = low_back(matmul(hidden, w2e) + small[1])
        return e_blk + m_blk[:, None] * layer_norm(out, small[2], small[3])
    edge_new = lax.map(jax.checkpoint(edge_block), (edges.reshape(SHARDS, EDGE_DEV, D), send.reshape(SHARDS, EDGE_DEV), recv.reshape(SHARDS, EDGE_DEV), maskf.reshape(SHARDS, EDGE_DEV))).reshape(EDGES, D)
    agg = low_back(jax.ops.segment_sum(maskf[:, None] * edge_new, recv, num_segments=NODES))
    node_in = jnp.concatenate([nodes_low, low(agg)], axis=1)
    pre_n = low_back(matmul(node_in, w1n) + small[4])
    hidden_n = low(jax.nn.silu(pre_n))
    out_n = low_back(matmul(hidden_n, w2n) + small[5])
    node_new = nodes + layer_norm(out_n, small[6], small[7])
    return (edge_new, node_new)

def adamw(weight, grad, first, second, rate):
    first_new = 0.9 * first + 0.1 * grad
    second_new = 0.999 * second + 0.001 * grad * grad
    mhat = first_new / (1.0 - 0.9 ** step_count)
    vhat = second_new / (1.0 - 0.999 ** step_count)
    return (weight - rate * (mhat / (jnp.sqrt(vhat) + 1e-08) + 0.1 * weight), second_new)

def reference(edge_lat, node_lat, edge_cot, node_cot, senders, receivers, edge_count, w_edge_in, w_edge_out, w_node_in, w_node_out, small_params, first_edge_in, first_edge_out, first_node_in, first_node_out, first_small, second_edge_in, second_edge_out, second_node_in, second_node_out, second_small):
    weights = (w_edge_in, w_edge_out, w_node_in, w_node_out, small_params)
    totals = [jnp.zeros_like(w) for w in weights]
    position = jnp.arange(EDGES, dtype=jnp.int32)
    local = position % EDGE_DEV
    shard = position // EDGE_DEV
    edge_outs, node_outs, edge_grads, node_grads = ([], [], [], [])
    for group in range(GROUPS):
        maskf = (local < edge_count[group][shard]).astype(jnp.float32)
        send = senders[group]
        recv = receivers[group]

        def run(edges, nodes, w1e, w2e, w1n, w2n, small):
            return group_forward(edges, nodes, w1e, w2e, w1n, w2n, small, send, recv, maskf)
        outputs, pull = jax.vjp(run, edge_lat[group].astype(jnp.float32), node_lat[group].astype(jnp.float32), *weights)
        grads = pull((edge_cot[group].astype(jnp.float32), node_cot[group].astype(jnp.float32)))
        edge_outs.append(outputs[0].astype(jnp.bfloat16))
        node_outs.append(outputs[1].astype(jnp.bfloat16))
        edge_grads.append(grads[0].astype(jnp.bfloat16))
        node_grads.append(grads[1].astype(jnp.bfloat16))
        totals = [t + g for t, g in zip(totals, grads[2:])]
    firsts = (first_edge_in, first_edge_out, first_node_in, first_node_out, first_small)
    seconds = (second_edge_in, second_edge_out, second_node_in, second_node_out, second_small)
    rates = (0.03, 0.03, 0.03, 0.03, 0.2)
    updated = [adamw(w, g, m, v, r) for w, g, m, v, r in zip(weights, totals, firsts, seconds, rates)]
    return (jnp.stack(edge_outs), jnp.stack(node_outs), jnp.stack(edge_grads), jnp.stack(node_grads), totals[0], totals[1], totals[2], totals[3], totals[4], updated[0][1], updated[1][1], updated[2][1], updated[3][1], updated[4][1], updated[0][0], updated[1][0], updated[2][0], updated[3][0], updated[4][0])
```

```python
import functools

import jax
import jax.numpy as jnp
from jax import lax
from jax.experimental import pallas as pl
from jax.experimental.pallas import tpu as pltpu
from jax.sharding import PartitionSpec as P

step_count = 10.0


def inner(left, right):
    return lax.dot_general(
        left, right, (((0,), (0,)), ((), ())), preferred_element_type=jnp.float32
    )


def times_t(left, right):
    return lax.dot_general(
        left, right, (((1,), (1,)), ((), ())), preferred_element_type=jnp.float32
    )


def norm_stats(values):
    mean = jnp.mean(values, axis=-1, keepdims=True)
    centred = values - mean
    var = jnp.mean(centred * centred, axis=-1, keepdims=True)
    rstd = lax.rsqrt(var + 1e-05)
    return (centred * rstd, rstd)


def norm_back(grad_out, normed, rstd, gain):
    scaled = grad_out * gain
    return rstd * (
        scaled
        - jnp.mean(scaled, axis=-1, keepdims=True)
        - normed * jnp.mean(scaled * normed, axis=-1, keepdims=True)
    )


def silu_slope(values):
    sig = jax.nn.sigmoid(values)
    return sig * (1.0 + values * (1.0 - sig))


def adamw(weight, grad, first, second, rate):
    first_new = 0.9 * first + 0.1 * grad
    second_new = 0.999 * second + 0.001 * grad * grad
    mhat = first_new / (1.0 - 0.9**step_count)
    vhat = second_new / (1.0 - 0.999**step_count)
    return (weight - rate * (mhat / (jnp.sqrt(vhat) + 1e-08) + 0.1 * weight), second_new)


def native(
    edge_lat,
    node_lat,
    edge_cot,
    node_cot,
    senders,
    receivers,
    edge_count,
    w_edge_in,
    w_edge_out,
    w_node_in,
    w_node_out,
    small_params,
    first_edge_in,
    first_edge_out,
    first_node_in,
    first_node_out,
    first_small,
    second_edge_in,
    second_edge_out,
    second_node_in,
    second_node_out,
    second_small,
):
    bf = jnp.bfloat16
    edges = edge_lat[0]
    nodes = node_lat[0]
    send = senders[0]
    recv = receivers[0]
    rows = edges.shape[0]
    width = edges.shape[1]
    maskf = (jnp.arange(rows, dtype=jnp.int32) < edge_count[0, 0]).astype(jnp.float32)[:, None]
    w1e, w2e, w1n, w2n, small = (
        lax.all_gather(w_edge_in.astype(bf), ("edge", "grp"), axis=0, tiled=True),
        lax.all_gather(w_edge_out.astype(bf), ("edge", "grp"), axis=0, tiled=True),
        lax.all_gather(w_node_in.astype(bf), ("edge", "grp"), axis=0, tiled=True),
        lax.all_gather(w_node_out.astype(bf), ("edge", "grp"), axis=0, tiled=True),
        lax.all_gather(small_params.astype(bf), ("edge", "grp"), axis=1, tiled=True),
    )
    params = small.astype(jnp.float32)
    whole = lax.all_gather(nodes, "edge", axis=0, tiled=True)
    node_total = whole.shape[0]
    joined = jnp.concatenate([edges, whole[send], whole[recv]], axis=1)
    pre = jnp.dot(joined, w1e, preferred_element_type=jnp.float32) + params[0]
    hidden = jax.nn.silu(pre).astype(bf)
    out = jnp.dot(hidden, w2e, preferred_element_type=jnp.float32) + params[1]
    normed, rstd = norm_stats(out)
    edge_new = edges.astype(jnp.float32) + maskf * (normed * params[2] + params[3])
    dense = jnp.zeros((node_total, width), jnp.float32).at[recv].add(maskf * edge_new)
    agg = lax.psum_scatter(dense, "edge", scatter_dimension=0, tiled=True)
    node_in = jnp.concatenate([nodes, agg.astype(bf)], axis=1)
    pre_n = jnp.dot(node_in, w1n, preferred_element_type=jnp.float32) + params[4]
    hidden_n = jax.nn.silu(pre_n).astype(bf)
    out_n = jnp.dot(hidden_n, w2n, preferred_element_type=jnp.float32) + params[5]
    normed_n, rstd_n = norm_stats(out_n)
    node_new = nodes.astype(jnp.float32) + normed_n * params[6] + params[7]
    grad_node_out_f = node_cot[0].astype(jnp.float32)
    d_out_n = norm_back(grad_node_out_f, normed_n, rstd_n, params[6]).astype(bf)
    gain_n = jnp.sum(grad_node_out_f * normed_n, axis=0)
    shift_n = jnp.sum(grad_node_out_f, axis=0)
    g_w2n = inner(hidden_n, d_out_n)
    g_b2n = jnp.sum(d_out_n.astype(jnp.float32), axis=0)
    d_pre_n = (times_t(d_out_n, w2n) * silu_slope(pre_n)).astype(bf)
    g_w1n = inner(node_in, d_pre_n)
    g_b1n = jnp.sum(d_pre_n.astype(jnp.float32), axis=0)
    d_node_in = times_t(d_pre_n, w1n)
    node_part = grad_node_out_f + d_node_in[:, :width]
    d_agg = d_node_in[:, width:].astype(bf)
    agg_rows = lax.all_gather(d_agg, "edge", axis=0, tiled=True)
    d_edge = edge_cot[0].astype(jnp.float32) + maskf * agg_rows[recv].astype(jnp.float32)
    masked = maskf * d_edge
    d_out = norm_back(masked, normed, rstd, params[2]).astype(bf)
    gain_e = jnp.sum(masked * normed, axis=0)
    shift_e = jnp.sum(masked, axis=0)
    g_w2e = inner(hidden, d_out)
    g_b2e = jnp.sum(d_out.astype(jnp.float32), axis=0)
    d_pre = (times_t(d_out, w2e) * silu_slope(pre)).astype(bf)
    g_w1e = inner(joined, d_pre)
    g_b1e = jnp.sum(d_pre.astype(jnp.float32), axis=0)
    d_joined = times_t(d_pre, w1e)
    edge_grad = (d_edge + d_joined[:, :width]).astype(bf)
    dense_grad = jnp.zeros((node_total, width), jnp.float32)
    dense_grad = (
        dense_grad.at[send]
        .add(d_joined[:, width : 2 * width])
        .at[recv]
        .add(d_joined[:, 2 * width :])
    )
    node_sum = lax.psum_scatter(dense_grad, "edge", scatter_dimension=0, tiled=True)
    node_grad = (node_part + node_sum).astype(bf)
    g_small = jnp.stack([g_b1e, g_b2e, gain_e, shift_e, g_b1n, g_b2n, gain_n, shift_n])
    grads = (
        lax.psum_scatter(g_w1e, ("edge", "grp"), scatter_dimension=0, tiled=True),
        lax.psum_scatter(g_w2e, ("edge", "grp"), scatter_dimension=0, tiled=True),
        lax.psum_scatter(g_w1n, ("edge", "grp"), scatter_dimension=0, tiled=True),
        lax.psum_scatter(g_w2n, ("edge", "grp"), scatter_dimension=0, tiled=True),
        lax.psum_scatter(g_small, ("edge", "grp"), scatter_dimension=1, tiled=True),
    )
    weights = (w_edge_in, w_edge_out, w_node_in, w_node_out, small_params)
    firsts = (first_edge_in, first_edge_out, first_node_in, first_node_out, first_small)
    seconds = (second_edge_in, second_edge_out, second_node_in, second_node_out, second_small)
    rates = (0.03, 0.03, 0.03, 0.03, 0.2)
    updated = [
        adamw(w, g, m, v, r) for w, g, m, v, r in zip(weights, grads, firsts, seconds, rates)
    ]
    return (
        edge_new.astype(bf)[None],
        node_new.astype(bf)[None],
        edge_grad[None],
        node_grad[None],
        grads[0],
        grads[1],
        grads[2],
        grads[3],
        grads[4],
        updated[0][1],
        updated[1][1],
        updated[2][1],
        updated[3][1],
        updated[4][1],
        updated[0][0],
        updated[1][0],
        updated[2][0],
        updated[3][0],
        updated[4][0],
    )


bf16 = jnp.bfloat16
f32 = jnp.float32
MESH = pl.DeviceIdType.MESH


def mm(left, right):
    return jnp.dot(left, right, preferred_element_type=f32)


def fold_rows(values):
    count, width = values.shape
    return jnp.sum(values.reshape(count // 8, 8, width), axis=0)


def layer_kernel(geo, *refs):
    Z, Y, X, C = geo["dims"]
    n_sem = geo["n_sem"]
    (
        edges_hbm,
        cot_hbm,
        nodes_in,
        ncot_in,
        send_in,
        recv_in,
        count_in,
        w1_in,
        w2_in,
        w3_in,
        w4_in,
        small_in,
        enew_out,
        egrad_out,
        nnew_out,
        ngrad_out,
        g1_out,
        g2_out,
        g3_out,
        g4_out,
        gs_out,
        edges,
        cot,
        nbuf,
        dbuf,
        w1,
        w2,
        w3,
        w4,
        w2v,
        w3v,
        w4v,
        pick,
        spread,
        proj,
        slope,
        hidden,
        normed,
        rstd,
        term,
        enew,
        dedge,
        dout,
        dpre,
        egrad,
        sums,
        pf,
        pb_a,
        pb_n,
        yr_a,
        yr_n,
        zs_a,
        zs_n,
        zr_a,
        zr_n,
        seg,
        sm_src,
        sm_rcv,
        gm_src,
        gm_rcv,
        gsm,
        *grad_refs,
    ) = refs
    local_sem, ssem, rsem = grad_refs[-3:]
    grad_refs = grad_refs[:-3]
    rows, D = edges.shape
    n = nodes_in.shape[0]
    N = Z * Y * n
    R = geo["chunk"]

    e_id = lax.axis_index("edge")
    g_id = lax.axis_index("grp")
    z = e_id // Y
    y = e_id % Y
    x = g_id // C
    c = g_id % C
    yp, xp, cp = 1 - y, 1 - x, 1 - c
    me = e_id * (X * C) + g_id
    y_dev = (z * Y + yp, g_id)
    x_dev = (e_id, xp * C + c)
    c_dev = (e_id, x * C + cp)

    def z_at(o):
        return lax.rem(z + o, Z)

    def z_dev(o):
        return (z_at(o) * Y + y, g_id)

    started = []

    def push(src, dst, dev):
        k = len(started)
        assert k < n_sem
        copy = pltpu.make_async_remote_copy(
            src_ref=src,
            dst_ref=dst,
            send_sem=ssem.at[k],
            recv_sem=rsem.at[k],
            device_id=dev,
            device_id_type=MESH,
        )
        copy.start()
        started.append(copy)
        return copy

    edges_copy = pltpu.make_async_copy(edges_hbm, edges, local_sem.at[0])
    cot_copy = pltpu.make_async_copy(cot_hbm, cot, local_sem.at[1])
    edges_copy.start()
    cot_copy.start()
    barrier = pltpu.get_barrier_semaphore()
    peers = [z_dev(o) for o in range(1, Z)] + [y_dev, x_dev, c_dev]
    for dev in peers:
        pl.semaphore_signal(barrier, inc=1, device_id=dev, device_id_type=MESH)

    nbuf[z, y] = nodes_in[...]
    r1 = w1_in.shape[0]
    w1[pl.ds(pl.multiple_of(me * r1, 16), r1), :] = w1_in[...].astype(bf16)
    for v, own in ((w2v, w2_in), (w3v, w3_in), (w4v, w4_in)):
        v[z, y, x, c] = own[...].astype(bf16)
    ws = small_in.shape[1]
    place = (
        lax.broadcasted_iota(jnp.int32, (ws, D), 1)
        == lax.broadcasted_iota(jnp.int32, (ws, D), 0) + me * ws
    )
    sm_src[0] = mm(small_in[...].astype(bf16), jnp.where(place, 1.0, 0.0).astype(bf16))
    pl.semaphore_wait(barrier, len(peers))

    own_n = nbuf.at[z, y]
    n_z = [push(own_n, own_n, z_dev(o)) for o in range(1, Z)]
    n_y = [push(own_n, own_n, y_dev)]

    def slot(zz, yy, xx):
        at = (((zz * Y + yy) * X + xx) * C + c) * r1
        return w1.at[pl.ds(pl.multiple_of(at, 16), r1), :]

    s = slot(z, y, x)
    w1_z = [push(s, s, z_dev(o)) for o in range(1, Z)]
    w1_y = [push(s, s, y_dev)]
    w1_x = [push(s, s, x_dev)]
    w1_c = [push(s, s, c_dev)]
    sm_z = [push(sm_src.at[0], sm_rcv.at[o - 1], z_dev(o)) for o in range(1, Z)]

    class Lines:
        def __init__(self, v):
            self.v = v
            s = v.at[z, y, x, c]
            self.z = [push(s, s, z_dev(o)) for o in range(1, Z)]

        def line(self):
            for copy in self.z:
                copy.wait_recv()
            s = self.v.at[:, y, x, c]
            self.y = push(s, s, y_dev)
            self.x = [push(s, s, x_dev)]

        def cross(self):
            self.y.wait_recv()
            s = self.v.at[:, yp, x, c]
            self.x.append(push(s, s, x_dev))

        def pair(self):
            for copy in self.x:
                copy.wait_recv()
            s = self.v.at[:, :, :, c]
            self.c = push(s, s, c_dev)

        def done(self, whole):
            self.c.wait_recv()
            whole[...] = self.v[...].reshape(whole.shape)

    w2_lines = Lines(w2v)
    w3_lines = Lines(w3v)
    w4_lines = Lines(w4v)

    lane = lax.broadcasted_iota(jnp.int32, (128, N), 1)
    sub = lax.broadcasted_iota(jnp.int32, (N, 128), 0)

    @pl.loop(0, rows // 128)
    def _(k):
        at = pl.ds(pl.multiple_of(k * 128, 128), 128)
        for half, ids in enumerate((send_in, recv_in)):
            row = jnp.broadcast_to(ids[0:1, at], (128, 128))
            col = jnp.tile(row.T, (1, N // 128))
            pick[at, half * N : (half + 1) * N] = jnp.where(lane == col, 1.0, 0.0).astype(bf16)
            wide = jnp.broadcast_to(ids[0:1, at], (N, 128))
            spread[half * N : (half + 1) * N, at] = jnp.where(sub == wide, 1.0, 0.0).astype(bf16)

    for o in range(1, Z):
        n_z[o - 1].wait_recv()
        s = nbuf.at[z_at(Z - o), y]
        n_y.append(push(s, s, y_dev))
    for o in range(1, Z):
        w1_z[o - 1].wait_recv()
        s = slot(z_at(Z - o), y, x)
        w1_y.append(push(s, s, y_dev))
        w1_x.append(push(s, s, x_dev))
        w1_c.append(push(s, s, c_dev))
    w2_lines.line()

    def small_sum(src, rcv, stage, copies):
        total = src[stage]
        for copy, k in copies:
            copy.wait_recv()
            total = total + rcv[k]
        src[stage + 1] = total

    small_sum(sm_src, sm_rcv, 0, [(copy, k) for k, copy in enumerate(sm_z)])
    sm_y = push(sm_src.at[1], sm_rcv.at[Z - 1], y_dev)
    for o in range(Z):
        w1_y[o].wait_recv()
        s = slot(z_at(Z - o), yp, x)
        w1_x.append(push(s, s, x_dev))
        w1_c.append(push(s, s, c_dev))
    w2_lines.cross()
    small_sum(sm_src, sm_rcv, 1, [(sm_y, Z - 1)])
    sm_x = push(sm_src.at[2], sm_rcv.at[Z], x_dev)
    for k in range(Y * Z):
        w1_x[k].wait_recv()
        s = slot(z_at(Z - k % Z), y if k < Z else yp, xp)
        w1_c.append(push(s, s, c_dev))
    w2_lines.pair()
    small_sum(sm_src, sm_rcv, 2, [(sm_x, Z)])
    sm_c = push(sm_src.at[3], sm_rcv.at[Z + 1], c_dev)
    w3_lines.line()
    w4_lines.line()
    for copy in n_y:
        copy.wait_recv()
    edges_copy.wait()
    for copy in w1_c:
        copy.wait_recv()
    w2_lines.done(w2)
    small_sum(sm_src, sm_rcv, 3, [(sm_c, Z + 1)])

    nodes_all = nbuf[...].reshape(N, D)
    proj[0:N, :] = mm(nodes_all, w1[D : 2 * D, :]).astype(bf16)
    proj[N : 2 * N, :] = mm(nodes_all, w1[2 * D : 3 * D, :]).astype(bf16)
    count = count_in[0, 0]
    row_id = lax.broadcasted_iota(jnp.int32, (R, D), 0)

    @pl.loop(0, rows // R)
    def _(i):
        at = pl.ds(pl.multiple_of(i * R, R), R)
        live = row_id < count - i * R
        own = edges[at, :]
        pre = mm(own, w1[0:D, :]) + mm(pick[at, :], proj[...]) + sm_src[4, 0:1, :]
        sig = jax.nn.sigmoid(pre)
        act = (pre * sig).astype(bf16)
        hidden[at, :] = act
        slope[at, :] = sig * (1.0 + pre * (1.0 - sig))
        out = mm(act, w2[...]) + sm_src[4, 1:2, :]
        norm, inv = norm_stats(out)
        normed[at, :] = norm
        rstd[at, :] = jnp.broadcast_to(inv, (R, 128))
        new = own.astype(f32) + jnp.where(live, norm * sm_src[4, 2:3, :] + sm_src[4, 3:4, :], 0.0)
        enew[at, :] = new.astype(bf16)
        term[at, :] = jnp.where(live, new, 0.0).astype(bf16)

    enew_copy = pltpu.make_async_copy(enew, enew_out, local_sem.at[2])
    enew_copy.start()
    w3_lines.cross()
    w4_lines.cross()

    class NodeSum:
        def __init__(self, total, pb, yr, zs, zr):
            self.zs, self.zr = zs, zr
            pf[...] = total.reshape(Z, Y, n, D)
            pb[...] = total.astype(bf16).reshape(Z, Y, n, D)
            self.yr = yr
            self.y = [push(pb.at[z_at(o), yp], yr.at[o], y_dev) for o in (*range(1, Z), 0)]

        def turn(self):
            self.z = []
            for k, o in enumerate((*range(1, Z), 0)):
                self.y[k].wait_recv()
                part = pf[z_at(o), y] + self.yr[o].astype(f32)
                if o == 0:
                    self.kept = part
                else:
                    self.zs[o - 1] = part.astype(bf16)
                    self.z.append(push(self.zs.at[o - 1], self.zr.at[o - 1], z_dev(o)))

        def total(self):
            result = self.kept
            for o in range(1, Z):
                self.z[o - 1].wait_recv()
                result = result + self.zr[o - 1].astype(f32)
            return result

    agg_sum = NodeSum(mm(spread[N : 2 * N, :], term[...]), pb_a, yr_a, zs_a, zr_a)
    w3_lines.pair()
    w4_lines.pair()
    agg_sum.turn()
    w3_lines.done(w3)
    w4_lines.done(w4)
    agg = agg_sum.total()

    def par(k):
        return sm_src[4, k : k + 1, :]

    own_nodes = nodes_in[...]
    agg_low = agg.astype(bf16)
    pre_n = mm(own_nodes, w3[0:D, :]) + mm(agg_low, w3[D : 2 * D, :]) + par(4)
    sig_n = jax.nn.sigmoid(pre_n)
    hidden_n = (pre_n * sig_n).astype(bf16)
    out_n = mm(hidden_n, w4[...]) + par(5)
    normed_n, rstd_n = norm_stats(out_n)
    ncot = ncot_in[...].astype(f32)
    d_out_n = norm_back(ncot, normed_n, rstd_n, par(6)).astype(bf16)
    slope_n = sig_n * (1.0 + pre_n * (1.0 - sig_n))
    d_pre_n = (times_t(d_out_n, w4[...]) * slope_n).astype(bf16)
    dbuf[z, y] = times_t(d_pre_n, w3[D : 2 * D, :]).astype(bf16)
    own_d = dbuf.at[z, y]
    d_z = [push(own_d, own_d, z_dev(o)) for o in range(1, Z)]
    d_y = [push(own_d, own_d, y_dev)]

    class WeightSum:
        def __init__(self, grad, crecv, xs, xrecv, ks, ys, yrecv, zs, zrecv):
            self.grad, self.crecv, self.xs, self.xrecv, self.ks = grad, crecv, xs, xrecv, ks
            self.ys, self.yrecv, self.zs, self.zrecv = ys, yrecv, zs, zrecv

        def put(self, first, values):
            low, r = values.astype(bf16), self.grad.shape[4]
            row = 0
            while row < values.shape[0]:
                k, off = divmod(first + row, r)
                size = min(r - off, values.shape[0] - row)
                at = (k // (Y * X * C), k // (X * C) % Y, k // C % X, k % C)
                self.grad[(*at, slice(off, off + size))] = low[row : row + size]
                row += size

        def rows_of(self, zz, yy, xx):
            return self.grad[zz, yy, xx, c].astype(f32)

        def start(self):
            self.c = [
                push(self.grad.at[:, :, xx, cp], self.crecv.at[h], c_dev)
                for h, xx in enumerate((xp, x))
            ]

        def cross_x(self):
            self.c[0].wait_recv()
            self.x = []
            for h, yy in enumerate((yp, y)):
                for zz in range(Z):
                    part = self.rows_of(zz, yy, xp) + self.crecv[0, zz, yy].astype(f32)
                    self.xs[h, zz] = part.astype(bf16)
                self.x.append(push(self.xs.at[h], self.xrecv.at[h], x_dev))
            self.c[1].wait_recv()
            for h, yy in enumerate((yp, y)):
                for zz in range(Z):
                    self.ks[h, zz] = self.rows_of(zz, yy, x) + self.crecv[1, zz, yy].astype(f32)

        def cross_y(self):
            self.x[0].wait_recv()
            self.ys[...] = (self.ks[0] + self.xrecv[0].astype(f32)).astype(bf16)
            self.y = push(self.ys, self.yrecv, y_dev)
            self.x[1].wait_recv()
            self.ks[1] = self.ks[1] + self.xrecv[1].astype(f32)

        def cross_z(self):
            self.y.wait_recv()
            self.z = []
            for o in range(1, Z):
                zz = z_at(o)
                self.zs[o - 1] = (self.ks[1, zz] + self.yrecv[zz].astype(f32)).astype(bf16)
                self.z.append(push(self.zs.at[o - 1], self.zrecv.at[o - 1], z_dev(o)))

        def total(self):
            result = self.ks[1, z] + self.yrecv[z].astype(f32)
            for o in range(1, Z):
                self.z[o - 1].wait_recv()
                result = result + self.zrecv[o - 1].astype(f32)
            return result

    per = len(grad_refs) // 4
    sum1, sum2, sum3, sum4 = [WeightSum(*grad_refs[k * per : (k + 1) * per]) for k in range(4)]

    sum3.put(0, inner(own_nodes, d_pre_n))
    sum3.put(D, inner(agg_low, d_pre_n))
    sum4.put(0, inner(hidden_n, d_out_n))
    sum3.start()
    sum4.start()
    nnew_out[...] = (own_nodes.astype(f32) + normed_n * par(6) + par(7)).astype(bf16)
    node_part = ncot + times_t(d_pre_n, w3[0:D, :])
    gsm[4:5, :] = jnp.sum(d_pre_n.astype(f32), axis=0, keepdims=True)
    gsm[5:6, :] = jnp.sum(d_out_n.astype(f32), axis=0, keepdims=True)
    gsm[6:7, :] = jnp.sum(ncot * normed_n, axis=0, keepdims=True)
    gsm[7:8, :] = jnp.sum(ncot, axis=0, keepdims=True)
    for o in range(1, Z):
        d_z[o - 1].wait_recv()
        s = dbuf.at[z_at(Z - o), y]
        d_y.append(push(s, s, y_dev))
    sum3.cross_x()
    sum4.cross_x()
    cot_copy.wait()
    for copy in d_y:
        copy.wait_recv()

    sums[...] = jnp.zeros_like(sums)
    d_all = dbuf[...].reshape(N, D)

    @pl.loop(0, rows // R)
    def _(i):
        at = pl.ds(pl.multiple_of(i * R, R), R)
        live = row_id < count - i * R
        d_edge = cot[at, :].astype(f32) + jnp.where(live, mm(pick[at, N : 2 * N], d_all), 0.0)
        dedge[at, :] = d_edge
        masked = jnp.where(live, d_edge, 0.0)
        norm = normed[at, :]
        inv = rstd[at, 0:1]
        weighted = masked * norm
        sums[2] += fold_rows(weighted)
        sums[3] += fold_rows(masked)
        d_out = norm_back(masked, norm, inv, par(2)).astype(bf16)
        dout[at, :] = d_out
        sums[1] += fold_rows(d_out.astype(f32))
        d_pre = (times_t(d_out, w2[...]) * slope[at, :]).astype(bf16)
        dpre[at, :] = d_pre
        sums[0] += fold_rows(d_pre.astype(f32))

    sum3.cross_y()
    sum4.cross_y()
    d_pre = dpre[...]
    seg[0:N, :] = mm(spread[0:N, :], d_pre).astype(bf16)
    seg[N : 2 * N, :] = mm(spread[N : 2 * N, :], d_pre).astype(bf16)
    node_sum = NodeSum(
        times_t(seg[0:N, :], w1[D : 2 * D, :]) + times_t(seg[N : 2 * N, :], w1[2 * D : 3 * D, :]),
        pb_n,
        yr_n,
        zs_n,
        zr_n,
    )
    sum2.put(0, inner(hidden[...], dout[...]))
    sum2.start()
    sum1.put(D, inner(nodes_all, seg[0:N, :]))
    sum1.put(2 * D, inner(nodes_all, seg[N : 2 * N, :]))
    sum1.put(0, inner(edges[...], d_pre))
    sum1.start()
    for k in range(4):
        gsm[k : k + 1, :] = jnp.sum(sums[k], axis=0, keepdims=True)
    gm_src[0] = gsm[...]
    gm_c = push(gm_src.at[0], gm_rcv.at[0], c_dev)
    node_sum.turn()
    sum3.cross_z()
    sum4.cross_z()
    sum2.cross_x()
    sum1.cross_x()
    small_sum(gm_src, gm_rcv, 0, [(gm_c, 0)])
    gm_x = push(gm_src.at[1], gm_rcv.at[1], x_dev)

    @pl.loop(0, rows // R)
    def _(i):
        at = pl.ds(pl.multiple_of(i * R, R), R)
        egrad[at, :] = (dedge[at, :] + times_t(dpre[at, :], w1[0:D, :])).astype(bf16)

    egrad_copy = pltpu.make_async_copy(egrad, egrad_out, local_sem.at[3])
    egrad_copy.start()
    sum2.cross_y()
    sum1.cross_y()
    small_sum(gm_src, gm_rcv, 1, [(gm_x, 1)])
    gm_y = push(gm_src.at[2], gm_rcv.at[2], y_dev)
    ngrad_out[...] = (node_part + node_sum.total()).astype(bf16)
    g3_out[...] = sum3.total()
    g4_out[...] = sum4.total()
    sum2.cross_z()
    sum1.cross_z()
    small_sum(gm_src, gm_rcv, 2, [(gm_y, 2)])
    gm_z = [push(gm_src.at[3], gm_rcv.at[2 + o], z_dev(o)) for o in range(1, Z)]
    g2_out[...] = sum2.total()
    g1_out[...] = sum1.total()
    small_sum(gm_src, gm_rcv, 3, [(copy, 3 + k) for k, copy in enumerate(gm_z)])
    take = (
        lax.broadcasted_iota(jnp.int32, (D, ws), 0)
        == lax.broadcasted_iota(jnp.int32, (D, ws), 1) + me * ws
    )
    gs_out[...] = jnp.dot(
        gm_src[4],
        jnp.where(take, 1.0, 0.0),
        preferred_element_type=f32,
        precision=lax.Precision.HIGHEST,
    )
    for copy in started:
        copy.wait_send()
    enew_copy.wait()
    egrad_copy.wait()


def update_kernel(*refs):
    (
        enew,
        egrad,
        nnew,
        ngrad,
        *rest,
    ) = refs[:24]
    outs = refs[24:]
    for src, dst in zip((enew, nnew, egrad, ngrad), outs[:4]):
        dst[0] = src[...]
    grads, weights, firsts, seconds = rest[0:5], rest[5:10], rest[10:15], rest[15:20]
    rates = (0.03, 0.03, 0.03, 0.03, 0.2)
    for k in range(5):
        grad = grads[k][...]
        new_w, new_v = adamw(weights[k][...], grad, firsts[k][...], seconds[k][...], rates[k])
        outs[4 + k][...] = grad
        outs[9 + k][...] = new_v
        outs[14 + k][...] = new_w


def on_device(n_edge, n_grp, *args):
    (
        edge_lat,
        node_lat,
        edge_cot,
        node_cot,
        senders,
        receivers,
        edge_count,
        *state,
    ) = args
    weights, firsts, seconds = state[0:5], state[5:10], state[10:15]
    rows, D = edge_lat.shape[1:]
    n = node_lat.shape[1]
    N = n * n_edge
    n_dev = n_edge * n_grp
    shards = [w.shape[0] for w in weights[:4]]
    fits = (
        n_edge % 2 == 0
        and n_grp == 4
        and all(r % 16 == 0 for r in shards)
        and D % 128 == 0
        and N % 128 == 0
        and rows % 256 == 0
        and rows * N <= 1024 * 1024
    )
    if not fits:
        return native(*args)
    Z, Y, X, C = n_edge // 2, 2, 2, 2
    n_sem = 160

    def vm(shape, dtype=bf16):
        return pltpu.VMEM(shape, dtype)

    scratch = [
        vm((rows, D)),
        vm((rows, D)),
        vm((Z, Y, n, D)),
        vm((Z, Y, n, D)),
        *[vm((r * n_dev, D)) for r in shards],
        *[vm((Z, Y, X, C, r, D)) for r in shards[1:]],
        vm((rows, 2 * N)),
        vm((2 * N, rows)),
        vm((2 * N, D)),
        vm((rows, D), f32),
        vm((rows, D)),
        vm((rows, D), f32),
        vm((rows, 128), f32),
        vm((rows, D)),
        vm((rows, D)),
        vm((rows, D), f32),
        vm((rows, D)),
        vm((rows, D)),
        vm((rows, D)),
        vm((4, 8, D), f32),
        vm((Z, Y, n, D), f32),
        vm((Z, Y, n, D)),
        vm((Z, Y, n, D)),
        vm((Z, n, D)),
        vm((Z, n, D)),
        vm((Z - 1, n, D)),
        vm((Z - 1, n, D)),
        vm((Z - 1, n, D)),
        vm((Z - 1, n, D)),
        vm((2 * N, D)),
        vm((5, 8, D), f32),
        vm((Z + 2, 8, D), f32),
        vm((5, 8, D), f32),
        vm((Z + 2, 8, D), f32),
        vm((8, D), f32),
    ]
    for r in shards:
        scratch += [
            vm((Z, Y, X, C, r, D)),
            vm((2, Z, Y, r, D)),
            vm((2, Z, r, D)),
            vm((2, Z, r, D)),
            vm((2, Z, r, D), f32),
            vm((Z, r, D)),
            vm((Z, r, D)),
            vm((Z - 1, r, D)),
            vm((Z - 1, r, D)),
        ]
    scratch += [
        pltpu.SemaphoreType.DMA((4,)),
        pltpu.SemaphoreType.DMA((n_sem,)),
        pltpu.SemaphoreType.DMA((n_sem,)),
    ]
    sds = jax.ShapeDtypeStruct
    anyspace = pl.BlockSpec(memory_space=pl.ANY)
    vmem = pl.BlockSpec(memory_space=pltpu.VMEM)
    smem = pl.BlockSpec(memory_space=pltpu.SMEM)
    big = [sds((rows, D), bf16)] * 2 + [sds((n, D), bf16)] * 2
    grads = [sds(w.shape, f32) for w in weights]
    results = pl.pallas_call(
        functools.partial(layer_kernel, {"dims": (Z, Y, X, C), "n_sem": n_sem, "chunk": 256}),
        out_shape=big + grads,
        in_specs=[anyspace, anyspace] + [vmem] * 4 + [smem] + [vmem] * 5,
        out_specs=[anyspace, anyspace] + [vmem] * 7,
        scratch_shapes=scratch,
        compiler_params=pltpu.CompilerParams(
            collective_id=0, has_side_effects=True, vmem_limit_bytes=56 * 1024 * 1024
        ),
        name="layer",
    )(
        edge_lat[0],
        edge_cot[0],
        node_lat[0],
        node_cot[0],
        senders,
        receivers,
        edge_count,
        *weights,
    )
    state_out = [sds(w.shape, f32) for w in weights]
    return tuple(
        pl.pallas_call(
            update_kernel,
            out_shape=[
                sds((1, rows, D), bf16),
                sds((1, n, D), bf16),
                sds((1, rows, D), bf16),
                sds((1, n, D), bf16),
                *state_out,
                *state_out,
                *state_out,
            ],
            in_specs=[vmem] * 24,
            out_specs=[vmem] * 19,
            compiler_params=pltpu.CompilerParams(vmem_limit_bytes=32 * 1024 * 1024),
            name="update",
        )(*results, *weights, *firsts, *seconds)
    )


def solution(mesh):
    in_specs = (
        P("grp", "edge", None),
        P("grp", "edge", None),
        P("grp", "edge", None),
        P("grp", "edge", None),
        P("grp", "edge"),
        P("grp", "edge"),
        P("grp", "edge"),
        P(("edge", "grp"), None),
        P(("edge", "grp"), None),
        P(("edge", "grp"), None),
        P(("edge", "grp"), None),
        P(None, ("edge", "grp")),
        P(("edge", "grp"), None),
        P(("edge", "grp"), None),
        P(("edge", "grp"), None),
        P(("edge", "grp"), None),
        P(None, ("edge", "grp")),
        P(("edge", "grp"), None),
        P(("edge", "grp"), None),
        P(("edge", "grp"), None),
        P(("edge", "grp"), None),
        P(None, ("edge", "grp")),
    )
    out_specs = (
        P("grp", "edge", None),
        P("grp", "edge", None),
        P("grp", "edge", None),
        P("grp", "edge", None),
        P(("edge", "grp"), None),
        P(("edge", "grp"), None),
        P(("edge", "grp"), None),
        P(("edge", "grp"), None),
        P(None, ("edge", "grp")),
        P(("edge", "grp"), None),
        P(("edge", "grp"), None),
        P(("edge", "grp"), None),
        P(("edge", "grp"), None),
        P(None, ("edge", "grp")),
        P(("edge", "grp"), None),
        P(("edge", "grp"), None),
        P(("edge", "grp"), None),
        P(("edge", "grp"), None),
        P(None, ("edge", "grp")),
    )
    return jax.shard_map(
        functools.partial(on_device, mesh.shape["edge"], mesh.shape["grp"]),
        mesh=mesh, in_specs=in_specs, out_specs=out_specs, check_vma=False
    )
```

```python
import functools

import jax
import jax.numpy as jnp
from jax import lax
from jax.experimental import pallas as pl
from jax.experimental.pallas import tpu as pltpu
from jax.sharding import PartitionSpec as P

step_count = 10.0


def inner(left, right):
    return lax.dot_general(
        left, right, (((0,), (0,)), ((), ())), preferred_element_type=jnp.float32
    )


def times_t(left, right):
    return lax.dot_general(
        left, right, (((1,), (1,)), ((), ())), preferred_element_type=jnp.float32
    )


def norm_stats(values):
    mean = jnp.mean(values, axis=-1, keepdims=True)
    centred = values - mean
    var = jnp.mean(centred * centred, axis=-1, keepdims=True)
    rstd = lax.rsqrt(var + 1e-05)
    return (centred * rstd, rstd)


def norm_back(grad_out, normed, rstd, gain):
    scaled = grad_out * gain
    return rstd * (
        scaled
        - jnp.mean(scaled, axis=-1, keepdims=True)
        - normed * jnp.mean(scaled * normed, axis=-1, keepdims=True)
    )


def silu_slope(values):
    sig = jax.nn.sigmoid(values)
    return sig * (1.0 + values * (1.0 - sig))


def adamw(weight, grad, first, second, rate):
    first_new = 0.9 * first + 0.1 * grad
    second_new = 0.999 * second + 0.001 * grad * grad
    mhat = first_new / (1.0 - 0.9**step_count)
    vhat = second_new / (1.0 - 0.999**step_count)
    return (weight - rate * (mhat / (jnp.sqrt(vhat) + 1e-08) + 0.1 * weight), second_new)


def native(
    edge_lat,
    node_lat,
    edge_cot,
    node_cot,
    senders,
    receivers,
    edge_count,
    w_edge_in,
    w_edge_out,
    w_node_in,
    w_node_out,
    small_params,
    first_edge_in,
    first_edge_out,
    first_node_in,
    first_node_out,
    first_small,
    second_edge_in,
    second_edge_out,
    second_node_in,
    second_node_out,
    second_small,
):
    bf = jnp.bfloat16
    edges = edge_lat[0]
    nodes = node_lat[0]
    send = senders[0]
    recv = receivers[0]
    rows = edges.shape[0]
    width = edges.shape[1]
    maskf = (jnp.arange(rows, dtype=jnp.int32) < edge_count[0, 0]).astype(jnp.float32)[:, None]
    w1e, w2e, w1n, w2n, small = (
        lax.all_gather(w_edge_in.astype(bf), ("edge", "grp"), axis=0, tiled=True),
        lax.all_gather(w_edge_out.astype(bf), ("edge", "grp"), axis=0, tiled=True),
        lax.all_gather(w_node_in.astype(bf), ("edge", "grp"), axis=0, tiled=True),
        lax.all_gather(w_node_out.astype(bf), ("edge", "grp"), axis=0, tiled=True),
        lax.all_gather(small_params.astype(bf), ("edge", "grp"), axis=1, tiled=True),
    )
    params = small.astype(jnp.float32)
    whole = lax.all_gather(nodes, "edge", axis=0, tiled=True)
    node_total = whole.shape[0]
    joined = jnp.concatenate([edges, whole[send], whole[recv]], axis=1)
    pre = jnp.dot(joined, w1e, preferred_element_type=jnp.float32) + params[0]
    hidden = jax.nn.silu(pre).astype(bf)
    out = jnp.dot(hidden, w2e, preferred_element_type=jnp.float32) + params[1]
    normed, rstd = norm_stats(out)
    edge_new = edges.astype(jnp.float32) + maskf * (normed * params[2] + params[3])
    dense = jnp.zeros((node_total, width), jnp.float32).at[recv].add(maskf * edge_new)
    agg = lax.psum_scatter(dense, "edge", scatter_dimension=0, tiled=True)
    node_in = jnp.concatenate([nodes, agg.astype(bf)], axis=1)
    pre_n = jnp.dot(node_in, w1n, preferred_element_type=jnp.float32) + params[4]
    hidden_n = jax.nn.silu(pre_n).astype(bf)
    out_n = jnp.dot(hidden_n, w2n, preferred_element_type=jnp.float32) + params[5]
    normed_n, rstd_n = norm_stats(out_n)
    node_new = nodes.astype(jnp.float32) + normed_n * params[6] + params[7]
    grad_node_out_f = node_cot[0].astype(jnp.float32)
    d_out_n = norm_back(grad_node_out_f, normed_n, rstd_n, params[6]).astype(bf)
    gain_n = jnp.sum(grad_node_out_f * normed_n, axis=0)
    shift_n = jnp.sum(grad_node_out_f, axis=0)
    g_w2n = inner(hidden_n, d_out_n)
    g_b2n = jnp.sum(d_out_n.astype(jnp.float32), axis=0)
    d_pre_n = (times_t(d_out_n, w2n) * silu_slope(pre_n)).astype(bf)
    g_w1n = inner(node_in, d_pre_n)
    g_b1n = jnp.sum(d_pre_n.astype(jnp.float32), axis=0)
    d_node_in = times_t(d_pre_n, w1n)
    node_part = grad_node_out_f + d_node_in[:, :width]
    d_agg = d_node_in[:, width:].astype(bf)
    agg_rows = lax.all_gather(d_agg, "edge", axis=0, tiled=True)
    d_edge = edge_cot[0].astype(jnp.float32) + maskf * agg_rows[recv].astype(jnp.float32)
    masked = maskf * d_edge
    d_out = norm_back(masked, normed, rstd, params[2]).astype(bf)
    gain_e = jnp.sum(masked * normed, axis=0)
    shift_e = jnp.sum(masked, axis=0)
    g_w2e = inner(hidden, d_out)
    g_b2e = jnp.sum(d_out.astype(jnp.float32), axis=0)
    d_pre = (times_t(d_out, w2e) * silu_slope(pre)).astype(bf)
    g_w1e = inner(joined, d_pre)
    g_b1e = jnp.sum(d_pre.astype(jnp.float32), axis=0)
    d_joined = times_t(d_pre, w1e)
    edge_grad = (d_edge + d_joined[:, :width]).astype(bf)
    dense_grad = jnp.zeros((node_total, width), jnp.float32)
    dense_grad = (
        dense_grad.at[send]
        .add(d_joined[:, width : 2 * width])
        .at[recv]
        .add(d_joined[:, 2 * width :])
    )
    node_sum = lax.psum_scatter(dense_grad, "edge", scatter_dimension=0, tiled=True)
    node_grad = (node_part + node_sum).astype(bf)
    g_small = jnp.stack([g_b1e, g_b2e, gain_e, shift_e, g_b1n, g_b2n, gain_n, shift_n])
    grads = (
        lax.psum_scatter(g_w1e, ("edge", "grp"), scatter_dimension=0, tiled=True),
        lax.psum_scatter(g_w2e, ("edge", "grp"), scatter_dimension=0, tiled=True),
        lax.psum_scatter(g_w1n, ("edge", "grp"), scatter_dimension=0, tiled=True),
        lax.psum_scatter(g_w2n, ("edge", "grp"), scatter_dimension=0, tiled=True),
        lax.psum_scatter(g_small, ("edge", "grp"), scatter_dimension=1, tiled=True),
    )
    weights = (w_edge_in, w_edge_out, w_node_in, w_node_out, small_params)
    firsts = (first_edge_in, first_edge_out, first_node_in, first_node_out, first_small)
    seconds = (second_edge_in, second_edge_out, second_node_in, second_node_out, second_small)
    rates = (0.03, 0.03, 0.03, 0.03, 0.2)
    updated = [
        adamw(w, g, m, v, r) for w, g, m, v, r in zip(weights, grads, firsts, seconds, rates)
    ]
    return (
        edge_new.astype(bf)[None],
        node_new.astype(bf)[None],
        edge_grad[None],
        node_grad[None],
        grads[0],
        grads[1],
        grads[2],
        grads[3],
        grads[4],
        updated[0][1],
        updated[1][1],
        updated[2][1],
        updated[3][1],
        updated[4][1],
        updated[0][0],
        updated[1][0],
        updated[2][0],
        updated[3][0],
        updated[4][0],
    )


bf16 = jnp.bfloat16
f32 = jnp.float32
MESH = pl.DeviceIdType.MESH


def mm(left, right):
    return jnp.dot(left, right, preferred_element_type=f32)


def fold_rows(values):
    count, width = values.shape
    return jnp.sum(values.reshape(count // 8, 8, width), axis=0)


def layer_kernel(geo, *refs):
    Z, Y, X, C = geo["dims"]
    n_sem = geo["n_sem"]
    (
        edges_hbm,
        cot_hbm,
        nodes_in,
        ncot_in,
        send_in,
        recv_in,
        count_in,
        w1_in,
        w2_in,
        w3_in,
        w4_in,
        small_in,
        enew_out,
        egrad_out,
        nnew_out,
        ngrad_out,
        g1_out,
        g2_out,
        g3_out,
        g4_out,
        gs_out,
        edges,
        cot,
        nbuf,
        dbuf,
        w1,
        w2,
        w3,
        w4,
        wa,
        wb,
        pick,
        spread,
        proj,
        slope,
        hidden,
        normed,
        rstd,
        term,
        enew,
        dedge,
        dout,
        dpre,
        egrad,
        sums,
        pf,
        pb_a,
        pb_n,
        yr_a,
        yr_n,
        zs_a,
        zs_n,
        zr_a,
        zr_n,
        seg,
        sm_src,
        sm_rcv,
        gm_src,
        gm_rcv,
        gsm,
        *grad_refs,
    ) = refs
    local_sem, ssem, rsem = grad_refs[-3:]
    grad_refs = grad_refs[:-3]
    rows, D = edges.shape
    n = nodes_in.shape[0]
    N = Z * Y * n
    R = geo["chunk"]

    e_id = lax.axis_index("edge")
    g_id = lax.axis_index("grp")
    z = e_id // Y
    y = e_id % Y
    x = g_id // C
    c = g_id % C
    yp, xp, cp = 1 - y, 1 - x, 1 - c
    me = e_id * (X * C) + g_id
    y_dev = (z * Y + yp, g_id)
    x_dev = (e_id, xp * C + c)
    c_dev = (e_id, x * C + cp)

    def z_at(o):
        return lax.rem(z + o, Z)

    def z_dev(o):
        return (z_at(o) * Y + y, g_id)

    started = []

    def push(src, dst, dev):
        k = len(started)
        assert k < n_sem
        copy = pltpu.make_async_remote_copy(
            src_ref=src,
            dst_ref=dst,
            send_sem=ssem.at[k],
            recv_sem=rsem.at[k],
            device_id=dev,
            device_id_type=MESH,
        )
        copy.start()
        started.append(copy)
        return copy

    edges_copy = pltpu.make_async_copy(edges_hbm, edges, local_sem.at[0])
    cot_copy = pltpu.make_async_copy(cot_hbm, cot, local_sem.at[1])
    edges_copy.start()
    cot_copy.start()
    barrier = pltpu.get_barrier_semaphore()
    peers = [z_dev(o) for o in range(1, Z)] + [y_dev, x_dev, c_dev]
    for dev in peers:
        pl.semaphore_signal(barrier, inc=1, device_id=dev, device_id_type=MESH)

    nbuf[z, y] = nodes_in[...]
    r1, r2, r3, r4 = (own.shape[0] for own in (w1_in, w2_in, w3_in, w4_in))
    wa[z, y, x, c, 0:r1, :] = w1_in[...].astype(bf16)
    wa[z, y, x, c, r1 : r1 + r2, :] = w2_in[...].astype(bf16)
    wb[z, y, x, c, 0:r3, :] = w3_in[...].astype(bf16)
    wb[z, y, x, c, r3 : r3 + r4, :] = w4_in[...].astype(bf16)
    ws = small_in.shape[1]
    place = (
        lax.broadcasted_iota(jnp.int32, (ws, D), 1)
        == lax.broadcasted_iota(jnp.int32, (ws, D), 0) + me * ws
    )
    sm_src[0] = mm(small_in[...].astype(bf16), jnp.where(place, 1.0, 0.0).astype(bf16))
    pl.semaphore_wait(barrier, len(peers))

    sm_z = [push(sm_src.at[0], sm_rcv.at[o - 1], z_dev(o)) for o in range(1, Z)]
    s = wa.at[z, y, x, c]
    a_z = [push(s, s, z_dev(o)) for o in range(1, Z)]
    a_y = [push(s, s, y_dev)]
    a_x = [push(s, s, x_dev)]
    a_c = [push(s, s, c_dev)]
    own_n = nbuf.at[z, y]
    n_y = [push(own_n, own_n, y_dev)]
    n_z = [push(own_n, own_n, z_dev(o)) for o in range(1, Z)]
    s = wb.at[z, y, x, c]
    b_z = [push(s, s, z_dev(o)) for o in range(1, Z)]

    lane = lax.broadcasted_iota(jnp.int32, (128, N), 1)
    sub = lax.broadcasted_iota(jnp.int32, (N, 128), 0)

    @pl.loop(0, rows // 128)
    def _(k):
        at = pl.ds(pl.multiple_of(k * 128, 128), 128)
        for half, ids in enumerate((send_in, recv_in)):
            row = jnp.broadcast_to(ids[0:1, at], (128, 128))
            col = jnp.tile(row.T, (1, N // 128))
            pick[at, half * N : (half + 1) * N] = jnp.where(lane == col, 1.0, 0.0).astype(bf16)
            wide = jnp.broadcast_to(ids[0:1, at], (N, 128))
            spread[half * N : (half + 1) * N, at] = jnp.where(sub == wide, 1.0, 0.0).astype(bf16)

    def settle(zz, yy, xx, cc):
        k = ((zz * Y + yy) * X + xx) * C + cc
        w1[pl.ds(pl.multiple_of(k * r1, 16), r1), :] = wa[zz, yy, xx, cc, 0:r1, :]
        w2[pl.ds(pl.multiple_of(k * r2, 16), r2), :] = wa[zz, yy, xx, cc, r1 : r1 + r2, :]

    def small_sum(src, rcv, stage, copies):
        total = src[stage]
        for copy, k in copies:
            copy.wait_recv()
            total = total + rcv[k]
        src[stage + 1] = total

    def on_z(o):
        a_z[o - 1].wait_recv()
        s = wa.at[z_at(Z - o), y, x, c]
        a_y.append(push(s, s, y_dev))
        a_x.append(push(s, s, x_dev))
        a_c.append(push(s, s, c_dev))
        settle(z_at(Z - o), y, x, c)

    def on_y(o):
        a_y[o].wait_recv()
        s = wa.at[z_at(Z - o), yp, x, c]
        a_x.append(push(s, s, x_dev))
        a_c.append(push(s, s, c_dev))
        settle(z_at(Z - o), yp, x, c)

    x_order = [(0, 0)]
    settle(z, y, x, c)
    for o in range(1, Z):
        on_z(o)
        x_order.append((o, 0))
        on_y(o - 1)
        x_order.append((o - 1, 1))
    small_sum(sm_src, sm_rcv, 0, [(copy, k) for k, copy in enumerate(sm_z)])
    sm_y = push(sm_src.at[1], sm_rcv.at[Z - 1], y_dev)

    def on_n(o):
        n_z[o - 1].wait_recv()
        s = nbuf.at[z_at(Z - o), y]
        n_y.append(push(s, s, y_dev))

    on_n(1)
    on_y(Z - 1)
    x_order.append((Z - 1, 1))
    for o in range(2, Z):
        on_n(o)
    small_sum(sm_src, sm_rcv, 1, [(sm_y, Z - 1)])
    sm_x = push(sm_src.at[2], sm_rcv.at[Z], x_dev)
    for copy, (o, flip) in zip(list(a_x), x_order):
        copy.wait_recv()
        yy = yp if flip else y
        s = wa.at[z_at(Z - o), yy, xp, c]
        a_c.append(push(s, s, c_dev))
        settle(z_at(Z - o), yy, xp, c)
    small_sum(sm_src, sm_rcv, 2, [(sm_x, Z)])
    sm_c = push(sm_src.at[3], sm_rcv.at[Z + 1], c_dev)
    for copy in b_z:
        copy.wait_recv()
    s = wb.at[:, y, x, c]
    b_y = push(s, s, y_dev)
    b_x = [push(s, s, x_dev)]
    for copy in n_y:
        copy.wait_recv()
    edges_copy.wait()
    for copy in a_c:
        copy.wait_recv()
    for zz in range(Z):
        for yy in range(Y):
            for xx in range(X):
                settle(zz, yy, xx, cp)
    small_sum(sm_src, sm_rcv, 3, [(sm_c, Z + 1)])

    nodes_all = nbuf[...].reshape(N, D)
    proj[0:N, :] = mm(nodes_all, w1[D : 2 * D, :]).astype(bf16)
    proj[N : 2 * N, :] = mm(nodes_all, w1[2 * D : 3 * D, :]).astype(bf16)
    count = count_in[0, 0]
    row_id = lax.broadcasted_iota(jnp.int32, (R, D), 0)

    @pl.loop(0, rows // R)
    def _(i):
        at = pl.ds(pl.multiple_of(i * R, R), R)
        live = row_id < count - i * R
        own = edges[at, :]
        pre = mm(own, w1[0:D, :]) + mm(pick[at, :], proj[...]) + sm_src[4, 0:1, :]
        sig = jax.nn.sigmoid(pre)
        act = (pre * sig).astype(bf16)
        hidden[at, :] = act
        slope[at, :] = sig * (1.0 + pre * (1.0 - sig))
        out = mm(act, w2[...]) + sm_src[4, 1:2, :]
        norm, inv = norm_stats(out)
        normed[at, :] = norm
        rstd[at, :] = jnp.broadcast_to(inv, (R, 128))
        new = own.astype(f32) + jnp.where(live, norm * sm_src[4, 2:3, :] + sm_src[4, 3:4, :], 0.0)
        enew[at, :] = new.astype(bf16)
        term[at, :] = jnp.where(live, new, 0.0).astype(bf16)

    enew_copy = pltpu.make_async_copy(enew, enew_out, local_sem.at[2])
    enew_copy.start()
    b_y.wait_recv()
    s = wb.at[:, yp, x, c]
    b_x.append(push(s, s, x_dev))

    order = (*range(1, Z), 0)

    class NodeSum:
        def __init__(self, total, pb, yr, zs, zr):
            self.zs, self.zr = zs, zr
            pf[...] = total.reshape(Z, Y, n, D)
            pb[...] = total.astype(bf16).reshape(Z, Y, n, D)
            self.yr = yr
            self.y = [push(pb.at[z_at(o), yp], yr.at[o], y_dev) for o in order]

        def turn(self):
            self.z = []
            for k, o in enumerate(order):
                self.y[k].wait_recv()
                part = pf[z_at(o), y] + self.yr[o].astype(f32)
                if o == 0:
                    self.kept = part
                else:
                    self.zs[o - 1] = part.astype(bf16)
                    self.z.append(push(self.zs.at[o - 1], self.zr.at[o - 1], z_dev(o)))

        def total(self):
            result = self.kept
            for o in range(1, Z):
                self.z[o - 1].wait_recv()
                result = result + self.zr[o - 1].astype(f32)
            return result

    agg_sum = NodeSum(mm(spread[N : 2 * N, :], term[...]), pb_a, yr_a, zs_a, zr_a)
    for copy in b_x:
        copy.wait_recv()
    s = wb.at[:, :, :, c]
    b_c = push(s, s, c_dev)
    agg_sum.turn()
    b_c.wait_recv()
    w3[...] = wb[:, :, :, :, 0:r3, :].reshape(w3.shape)
    w4[...] = wb[:, :, :, :, r3 : r3 + r4, :].reshape(w4.shape)
    own_nodes = nodes_in[...]
    pre_own = mm(own_nodes, w3[0:D, :])
    agg = agg_sum.total()

    def par(k):
        return sm_src[4, k : k + 1, :]

    agg_low = agg.astype(bf16)
    pre_n = pre_own + mm(agg_low, w3[D : 2 * D, :]) + par(4)
    sig_n = jax.nn.sigmoid(pre_n)
    hidden_n = (pre_n * sig_n).astype(bf16)
    out_n = mm(hidden_n, w4[...]) + par(5)
    normed_n, rstd_n = norm_stats(out_n)
    ncot = ncot_in[...].astype(f32)
    d_out_n = norm_back(ncot, normed_n, rstd_n, par(6)).astype(bf16)
    slope_n = sig_n * (1.0 + pre_n * (1.0 - sig_n))
    d_pre_n = (times_t(d_out_n, w4[...]) * slope_n).astype(bf16)
    dbuf[z, y] = times_t(d_pre_n, w3[D : 2 * D, :]).astype(bf16)
    own_d = dbuf.at[z, y]
    d_z = [push(own_d, own_d, z_dev(o)) for o in range(1, Z)]
    d_y = [push(own_d, own_d, y_dev)]

    class WeightSum:
        def __init__(self, grad, crecv, xs, xrecv, ks, ys, yrecv, zs, zrecv):
            self.grad, self.crecv, self.xs, self.xrecv, self.ks = grad, crecv, xs, xrecv, ks
            self.ys, self.yrecv, self.zs, self.zrecv = ys, yrecv, zs, zrecv

        def put(self, first, values, lane_rows=None, base=0):
            low, r = values.astype(bf16), lane_rows or self.grad.shape[4]
            row = 0
            while row < values.shape[0]:
                k, off = divmod(first + row, r)
                size = min(r - off, values.shape[0] - row)
                at = (k // (Y * X * C), k // (X * C) % Y, k // C % X, k % C)
                self.grad[(*at, slice(base + off, base + off + size))] = low[row : row + size]
                row += size

        def start(self):
            self.c = [
                push(self.grad.at[:, yy, xx, cp], self.crecv.at[k], c_dev)
                for k, (yy, xx) in enumerate(((yp, xp), (y, xp), (yp, x), (y, x)))
            ]

        def cross_x(self):
            self.x = []
            for k, yy in enumerate((yp, y)):
                self.c[k].wait_recv()
                for o in order:
                    zz = z_at(o)
                    part = self.grad[zz, yy, xp, c].astype(f32) + self.crecv[k, zz].astype(f32)
                    self.xs[k, o] = part.astype(bf16)
                    self.x.append(push(self.xs.at[k, o], self.xrecv.at[k, o], x_dev))
            for k, yy in enumerate((yp, y)):
                self.c[2 + k].wait_recv()
                for o in order:
                    zz = z_at(o)
                    self.ks[k, o] = self.grad[zz, yy, x, c].astype(f32) + self.crecv[2 + k, zz].astype(f32)

        def cross_y(self):
            self.y = []
            for k, o in enumerate(order):
                self.x[k].wait_recv()
                self.ys[o] = (self.ks[0, o] + self.xrecv[0, o].astype(f32)).astype(bf16)
                self.y.append(push(self.ys.at[o], self.yrecv.at[o], y_dev))

        def gather(self, k, o):
            self.x[Z + k].wait_recv()
            self.y[k].wait_recv()
            return self.ks[1, o] + self.xrecv[1, o].astype(f32) + self.yrecv[o].astype(f32)

        def cross_z(self):
            self.z = []
            for k, o in enumerate(order[:-1]):
                self.zs[o - 1] = self.gather(k, o).astype(bf16)
                self.z.append(push(self.zs.at[o - 1], self.zrecv.at[o - 1], z_dev(o)))
            self.kept = self.gather(Z - 1, 0)

        def total(self):
            result = self.kept
            for o in range(1, Z):
                self.z[o - 1].wait_recv()
                result = result + self.zrecv[o - 1].astype(f32)
            return result

    per = len(grad_refs) // 3
    sum1, sum2, sum_n = [WeightSum(*grad_refs[k * per : (k + 1) * per]) for k in range(3)]

    sum_n.put(0, inner(own_nodes, d_pre_n), r3)
    sum_n.put(D, inner(agg_low, d_pre_n), r3)
    sum_n.put(0, inner(hidden_n, d_out_n), r4, r3)
    sum_n.start()
    nnew_out[...] = (own_nodes.astype(f32) + normed_n * par(6) + par(7)).astype(bf16)
    node_part = ncot + times_t(d_pre_n, w3[0:D, :])
    gsm[4:5, :] = jnp.sum(d_pre_n.astype(f32), axis=0, keepdims=True)
    gsm[5:6, :] = jnp.sum(d_out_n.astype(f32), axis=0, keepdims=True)
    gsm[6:7, :] = jnp.sum(ncot * normed_n, axis=0, keepdims=True)
    gsm[7:8, :] = jnp.sum(ncot, axis=0, keepdims=True)
    for o in range(1, Z):
        d_z[o - 1].wait_recv()
        s = dbuf.at[z_at(Z - o), y]
        d_y.append(push(s, s, y_dev))
    sum_n.cross_x()
    cot_copy.wait()
    for copy in d_y:
        copy.wait_recv()

    sums[...] = jnp.zeros_like(sums)
    d_all = dbuf[...].reshape(N, D)

    def edge_back(i):
        at = pl.ds(pl.multiple_of(i * R, R), R)
        live = row_id < count - i * R
        d_edge = cot[at, :].astype(f32) + jnp.where(live, mm(pick[at, N : 2 * N], d_all), 0.0)
        dedge[at, :] = d_edge
        masked = jnp.where(live, d_edge, 0.0)
        norm = normed[at, :]
        inv = rstd[at, 0:1]
        weighted = masked * norm
        sums[2] += fold_rows(weighted)
        sums[3] += fold_rows(masked)
        d_out = norm_back(masked, norm, inv, par(2)).astype(bf16)
        dout[at, :] = d_out
        sums[1] += fold_rows(d_out.astype(f32))
        d_pre = (times_t(d_out, w2[...]) * slope[at, :]).astype(bf16)
        dpre[at, :] = d_pre
        sums[0] += fold_rows(d_pre.astype(f32))

    half = rows // R // 2
    pl.loop(0, half)(edge_back)
    sum_n.cross_y()
    pl.loop(half, rows // R)(edge_back)
    sum2.put(0, inner(hidden[...], dout[...]))
    sum2.start()
    for k in range(4):
        gsm[k : k + 1, :] = jnp.sum(sums[k], axis=0, keepdims=True)
    gm_src[0] = gsm[...]
    gm_c = push(gm_src.at[0], gm_rcv.at[0], c_dev)
    sum_n.cross_z()
    d_pre = dpre[...]
    sum1.put(0, inner(edges[...], d_pre))
    sum2.cross_x()
    small_sum(gm_src, gm_rcv, 0, [(gm_c, 0)])
    gm_x = push(gm_src.at[1], gm_rcv.at[1], x_dev)
    seg[0:N, :] = mm(spread[0:N, :], d_pre).astype(bf16)
    seg[N : 2 * N, :] = mm(spread[N : 2 * N, :], d_pre).astype(bf16)
    sum1.put(D, inner(nodes_all, seg[0:N, :]))
    sum1.put(2 * D, inner(nodes_all, seg[N : 2 * N, :]))
    sum1.start()
    node_sum = NodeSum(
        times_t(seg[0:N, :], w1[D : 2 * D, :]) + times_t(seg[N : 2 * N, :], w1[2 * D : 3 * D, :]),
        pb_n,
        yr_n,
        zs_n,
        zr_n,
    )
    sum1.cross_x()
    small_sum(gm_src, gm_rcv, 1, [(gm_x, 1)])
    gm_y = push(gm_src.at[2], gm_rcv.at[2], y_dev)
    sum2.cross_y()
    node_sum.turn()
    sum2.cross_z()
    small_sum(gm_src, gm_rcv, 2, [(gm_y, 2)])
    gm_z = [push(gm_src.at[3], gm_rcv.at[2 + o], z_dev(o)) for o in range(1, Z)]

    @pl.loop(0, rows // R)
    def _(i):
        at = pl.ds(pl.multiple_of(i * R, R), R)
        egrad[at, :] = (dedge[at, :] + times_t(dpre[at, :], w1[0:D, :])).astype(bf16)

    egrad_copy = pltpu.make_async_copy(egrad, egrad_out, local_sem.at[3])
    egrad_copy.start()
    sum1.cross_y()
    ngrad_out[...] = (node_part + node_sum.total()).astype(bf16)
    total_n = sum_n.total()
    g3_out[...] = total_n[0:r3]
    g4_out[...] = total_n[r3 : r3 + r4]
    g2_out[...] = sum2.total()
    small_sum(gm_src, gm_rcv, 3, [(copy, 3 + k) for k, copy in enumerate(gm_z)])
    take = (
        lax.broadcasted_iota(jnp.int32, (D, ws), 0)
        == lax.broadcasted_iota(jnp.int32, (D, ws), 1) + me * ws
    )
    gs_out[...] = jnp.dot(
        gm_src[4],
        jnp.where(take, 1.0, 0.0),
        preferred_element_type=f32,
        precision=lax.Precision.HIGHEST,
    )
    sum1.cross_z()
    g1_out[...] = sum1.total()
    for copy in started:
        copy.wait_send()
    enew_copy.wait()
    egrad_copy.wait()


def update_kernel(*refs):
    (
        enew,
        egrad,
        nnew,
        ngrad,
        *rest,
    ) = refs[:24]
    outs = refs[24:]
    for src, dst in zip((enew, nnew, egrad, ngrad), outs[:4]):
        dst[0] = src[...]
    grads, weights, firsts, seconds = rest[0:5], rest[5:10], rest[10:15], rest[15:20]
    rates = (0.03, 0.03, 0.03, 0.03, 0.2)
    for k in range(5):
        grad = grads[k][...]
        new_w, new_v = adamw(weights[k][...], grad, firsts[k][...], seconds[k][...], rates[k])
        outs[4 + k][...] = grad
        outs[9 + k][...] = new_v
        outs[14 + k][...] = new_w


def on_device(n_edge, n_grp, *args):
    (
        edge_lat,
        node_lat,
        edge_cot,
        node_cot,
        senders,
        receivers,
        edge_count,
        *state,
    ) = args
    weights, firsts, seconds = state[0:5], state[5:10], state[10:15]
    rows, D = edge_lat.shape[1:]
    n = node_lat.shape[1]
    N = n * n_edge
    n_dev = n_edge * n_grp
    shards = [w.shape[0] for w in weights[:4]]
    fits = (
        n_edge % 2 == 0
        and n_grp == 4
        and all(r % 16 == 0 for r in shards)
        and D % 128 == 0
        and N % 128 == 0
        and rows % 256 == 0
        and rows * N <= 1024 * 1024
    )
    if not fits:
        return native(*args)
    Z, Y, X, C = n_edge // 2, 2, 2, 2
    n_sem = 200

    def vm(shape, dtype=bf16):
        return pltpu.VMEM(shape, dtype)

    scratch = [
        vm((rows, D)),
        vm((rows, D)),
        vm((Z, Y, n, D)),
        vm((Z, Y, n, D)),
        *[vm((r * n_dev, D)) for r in shards],
        vm((Z, Y, X, C, shards[0] + shards[1], D)),
        vm((Z, Y, X, C, shards[2] + shards[3], D)),
        vm((rows, 2 * N)),
        vm((2 * N, rows)),
        vm((2 * N, D)),
        vm((rows, D), f32),
        vm((rows, D)),
        vm((rows, D), f32),
        vm((rows, 128), f32),
        vm((rows, D)),
        vm((rows, D)),
        vm((rows, D), f32),
        vm((rows, D)),
        vm((rows, D)),
        vm((rows, D)),
        vm((4, 8, D), f32),
        vm((Z, Y, n, D), f32),
        vm((Z, Y, n, D)),
        vm((Z, Y, n, D)),
        vm((Z, n, D)),
        vm((Z, n, D)),
        vm((Z - 1, n, D)),
        vm((Z - 1, n, D)),
        vm((Z - 1, n, D)),
        vm((Z - 1, n, D)),
        vm((2 * N, D)),
        vm((5, 8, D), f32),
        vm((Z + 2, 8, D), f32),
        vm((5, 8, D), f32),
        vm((Z + 2, 8, D), f32),
        vm((8, D), f32),
    ]
    for r in (shards[0], shards[1], shards[2] + shards[3]):
        scratch += [
            vm((Z, Y, X, C, r, D)),
            vm((4, Z, r, D)),
            vm((2, Z, r, D)),
            vm((2, Z, r, D)),
            vm((2, Z, r, D), f32),
            vm((Z, r, D)),
            vm((Z, r, D)),
            vm((Z - 1, r, D)),
            vm((Z - 1, r, D)),
        ]
    scratch += [
        pltpu.SemaphoreType.DMA((4,)),
        pltpu.SemaphoreType.DMA((n_sem,)),
        pltpu.SemaphoreType.DMA((n_sem,)),
    ]
    sds = jax.ShapeDtypeStruct
    anyspace = pl.BlockSpec(memory_space=pl.ANY)
    vmem = pl.BlockSpec(memory_space=pltpu.VMEM)
    smem = pl.BlockSpec(memory_space=pltpu.SMEM)
    big = [sds((rows, D), bf16)] * 2 + [sds((n, D), bf16)] * 2
    grads = [sds(w.shape, f32) for w in weights]
    results = pl.pallas_call(
        functools.partial(layer_kernel, {"dims": (Z, Y, X, C), "n_sem": n_sem, "chunk": 256}),
        out_shape=big + grads,
        in_specs=[anyspace, anyspace] + [vmem] * 4 + [smem] + [vmem] * 5,
        out_specs=[anyspace, anyspace] + [vmem] * 7,
        scratch_shapes=scratch,
        compiler_params=pltpu.CompilerParams(
            collective_id=0, has_side_effects=True, vmem_limit_bytes=56 * 1024 * 1024
        ),
        name="layer",
    )(
        edge_lat[0],
        edge_cot[0],
        node_lat[0],
        node_cot[0],
        senders,
        receivers,
        edge_count,
        *weights,
    )
    state_out = [sds(w.shape, f32) for w in weights]
    return tuple(
        pl.pallas_call(
            update_kernel,
            out_shape=[
                sds((1, rows, D), bf16),
                sds((1, n, D), bf16),
                sds((1, rows, D), bf16),
                sds((1, n, D), bf16),
                *state_out,
                *state_out,
                *state_out,
            ],
            in_specs=[vmem] * 24,
            out_specs=[vmem] * 19,
            compiler_params=pltpu.CompilerParams(vmem_limit_bytes=60 * 1024 * 1024),
            name="update",
        )(*results, *weights, *firsts, *seconds)
    )


def solution(mesh):
    in_specs = (
        P("grp", "edge", None),
        P("grp", "edge", None),
        P("grp", "edge", None),
        P("grp", "edge", None),
        P("grp", "edge"),
        P("grp", "edge"),
        P("grp", "edge"),
        P(("edge", "grp"), None),
        P(("edge", "grp"), None),
        P(("edge", "grp"), None),
        P(("edge", "grp"), None),
        P(None, ("edge", "grp")),
        P(("edge", "grp"), None),
        P(("edge", "grp"), None),
        P(("edge", "grp"), None),
        P(("edge", "grp"), None),
        P(None, ("edge", "grp")),
        P(("edge", "grp"), None),
        P(("edge", "grp"), None),
        P(("edge", "grp"), None),
        P(("edge", "grp"), None),
        P(None, ("edge", "grp")),
    )
    out_specs = (
        P("grp", "edge", None),
        P("grp", "edge", None),
        P("grp", "edge", None),
        P("grp", "edge", None),
        P(("edge", "grp"), None),
        P(("edge", "grp"), None),
        P(("edge", "grp"), None),
        P(("edge", "grp"), None),
        P(None, ("edge", "grp")),
        P(("edge", "grp"), None),
        P(("edge", "grp"), None),
        P(("edge", "grp"), None),
        P(("edge", "grp"), None),
        P(None, ("edge", "grp")),
        P(("edge", "grp"), None),
        P(("edge", "grp"), None),
        P(("edge", "grp"), None),
        P(("edge", "grp"), None),
        P(None, ("edge", "grp")),
    )
    return jax.shard_map(
        functools.partial(on_device, mesh.shape["edge"], mesh.shape["grp"]),
        mesh=mesh, in_specs=in_specs, out_specs=out_specs, check_vma=False
    )
```

```python
import functools

import jax
import jax.numpy as jnp
from jax import lax
from jax.experimental import pallas as pl
from jax.experimental.pallas import tpu as pltpu
from jax.sharding import PartitionSpec as P

step_count = 10.0


def inner(left, right):
    return lax.dot_general(
        left, right, (((0,), (0,)), ((), ())), preferred_element_type=jnp.float32
    )


def times_t(left, right):
    return lax.dot_general(
        left, right, (((1,), (1,)), ((), ())), preferred_element_type=jnp.float32
    )


def norm_stats(values):
    mean = jnp.mean(values, axis=-1, keepdims=True)
    centred = values - mean
    var = jnp.mean(centred * centred, axis=-1, keepdims=True)
    rstd = lax.rsqrt(var + 1e-05)
    return (centred * rstd, rstd)


def norm_back(grad_out, normed, rstd, gain):
    scaled = grad_out * gain
    return rstd * (
        scaled
        - jnp.mean(scaled, axis=-1, keepdims=True)
        - normed * jnp.mean(scaled * normed, axis=-1, keepdims=True)
    )


def silu_slope(values):
    sig = jax.nn.sigmoid(values)
    return sig * (1.0 + values * (1.0 - sig))


def adamw(weight, grad, first, second, rate):
    first_new = 0.9 * first + 0.1 * grad
    second_new = 0.999 * second + 0.001 * grad * grad
    mhat = first_new / (1.0 - 0.9**step_count)
    vhat = second_new / (1.0 - 0.999**step_count)
    return (weight - rate * (mhat / (jnp.sqrt(vhat) + 1e-08) + 0.1 * weight), second_new)


def native(
    edge_lat,
    node_lat,
    edge_cot,
    node_cot,
    senders,
    receivers,
    edge_count,
    w_edge_in,
    w_edge_out,
    w_node_in,
    w_node_out,
    small_params,
    first_edge_in,
    first_edge_out,
    first_node_in,
    first_node_out,
    first_small,
    second_edge_in,
    second_edge_out,
    second_node_in,
    second_node_out,
    second_small,
):
    bf = jnp.bfloat16
    edges = edge_lat[0]
    nodes = node_lat[0]
    send = senders[0]
    recv = receivers[0]
    rows = edges.shape[0]
    width = edges.shape[1]
    maskf = (jnp.arange(rows, dtype=jnp.int32) < edge_count[0, 0]).astype(jnp.float32)[:, None]
    w1e, w2e, w1n, w2n, small = (
        lax.all_gather(w_edge_in.astype(bf), ("edge", "grp"), axis=0, tiled=True),
        lax.all_gather(w_edge_out.astype(bf), ("edge", "grp"), axis=0, tiled=True),
        lax.all_gather(w_node_in.astype(bf), ("edge", "grp"), axis=0, tiled=True),
        lax.all_gather(w_node_out.astype(bf), ("edge", "grp"), axis=0, tiled=True),
        lax.all_gather(small_params.astype(bf), ("edge", "grp"), axis=1, tiled=True),
    )
    params = small.astype(jnp.float32)
    whole = lax.all_gather(nodes, "edge", axis=0, tiled=True)
    node_total = whole.shape[0]
    joined = jnp.concatenate([edges, whole[send], whole[recv]], axis=1)
    pre = jnp.dot(joined, w1e, preferred_element_type=jnp.float32) + params[0]
    hidden = jax.nn.silu(pre).astype(bf)
    out = jnp.dot(hidden, w2e, preferred_element_type=jnp.float32) + params[1]
    normed, rstd = norm_stats(out)
    edge_new = edges.astype(jnp.float32) + maskf * (normed * params[2] + params[3])
    dense = jnp.zeros((node_total, width), jnp.float32).at[recv].add(maskf * edge_new)
    agg = lax.psum_scatter(dense, "edge", scatter_dimension=0, tiled=True)
    node_in = jnp.concatenate([nodes, agg.astype(bf)], axis=1)
    pre_n = jnp.dot(node_in, w1n, preferred_element_type=jnp.float32) + params[4]
    hidden_n = jax.nn.silu(pre_n).astype(bf)
    out_n = jnp.dot(hidden_n, w2n, preferred_element_type=jnp.float32) + params[5]
    normed_n, rstd_n = norm_stats(out_n)
    node_new = nodes.astype(jnp.float32) + normed_n * params[6] + params[7]
    grad_node_out_f = node_cot[0].astype(jnp.float32)
    d_out_n = norm_back(grad_node_out_f, normed_n, rstd_n, params[6]).astype(bf)
    gain_n = jnp.sum(grad_node_out_f * normed_n, axis=0)
    shift_n = jnp.sum(grad_node_out_f, axis=0)
    g_w2n = inner(hidden_n, d_out_n)
    g_b2n = jnp.sum(d_out_n.astype(jnp.float32), axis=0)
    d_pre_n = (times_t(d_out_n, w2n) * silu_slope(pre_n)).astype(bf)
    g_w1n = inner(node_in, d_pre_n)
    g_b1n = jnp.sum(d_pre_n.astype(jnp.float32), axis=0)
    d_node_in = times_t(d_pre_n, w1n)
    node_part = grad_node_out_f + d_node_in[:, :width]
    d_agg = d_node_in[:, width:].astype(bf)
    agg_rows = lax.all_gather(d_agg, "edge", axis=0, tiled=True)
    d_edge = edge_cot[0].astype(jnp.float32) + maskf * agg_rows[recv].astype(jnp.float32)
    masked = maskf * d_edge
    d_out = norm_back(masked, normed, rstd, params[2]).astype(bf)
    gain_e = jnp.sum(masked * normed, axis=0)
    shift_e = jnp.sum(masked, axis=0)
    g_w2e = inner(hidden, d_out)
    g_b2e = jnp.sum(d_out.astype(jnp.float32), axis=0)
    d_pre = (times_t(d_out, w2e) * silu_slope(pre)).astype(bf)
    g_w1e = inner(joined, d_pre)
    g_b1e = jnp.sum(d_pre.astype(jnp.float32), axis=0)
    d_joined = times_t(d_pre, w1e)
    edge_grad = (d_edge + d_joined[:, :width]).astype(bf)
    dense_grad = jnp.zeros((node_total, width), jnp.float32)
    dense_grad = (
        dense_grad.at[send]
        .add(d_joined[:, width : 2 * width])
        .at[recv]
        .add(d_joined[:, 2 * width :])
    )
    node_sum = lax.psum_scatter(dense_grad, "edge", scatter_dimension=0, tiled=True)
    node_grad = (node_part + node_sum).astype(bf)
    g_small = jnp.stack([g_b1e, g_b2e, gain_e, shift_e, g_b1n, g_b2n, gain_n, shift_n])
    grads = (
        lax.psum_scatter(g_w1e, ("edge", "grp"), scatter_dimension=0, tiled=True),
        lax.psum_scatter(g_w2e, ("edge", "grp"), scatter_dimension=0, tiled=True),
        lax.psum_scatter(g_w1n, ("edge", "grp"), scatter_dimension=0, tiled=True),
        lax.psum_scatter(g_w2n, ("edge", "grp"), scatter_dimension=0, tiled=True),
        lax.psum_scatter(g_small, ("edge", "grp"), scatter_dimension=1, tiled=True),
    )
    weights = (w_edge_in, w_edge_out, w_node_in, w_node_out, small_params)
    firsts = (first_edge_in, first_edge_out, first_node_in, first_node_out, first_small)
    seconds = (second_edge_in, second_edge_out, second_node_in, second_node_out, second_small)
    rates = (0.03, 0.03, 0.03, 0.03, 0.2)
    updated = [
        adamw(w, g, m, v, r) for w, g, m, v, r in zip(weights, grads, firsts, seconds, rates)
    ]
    return (
        edge_new.astype(bf)[None],
        node_new.astype(bf)[None],
        edge_grad[None],
        node_grad[None],
        grads[0],
        grads[1],
        grads[2],
        grads[3],
        grads[4],
        updated[0][1],
        updated[1][1],
        updated[2][1],
        updated[3][1],
        updated[4][1],
        updated[0][0],
        updated[1][0],
        updated[2][0],
        updated[3][0],
        updated[4][0],
    )


bf16 = jnp.bfloat16
f32 = jnp.float32
MESH = pl.DeviceIdType.MESH


def mm(left, right):
    return jnp.dot(left, right, preferred_element_type=f32)


def fold_rows(values):
    count, width = values.shape
    return jnp.sum(values.reshape(count // 8, 8, width), axis=0)


GEO = {
    "chunk": 256,
    "gather": (
        "n0", "y0.0", "y0.1", "z1.0", "z2.0", "z1.1", "z2.1", "y1.0", "y2.0", "s0", "z3.0", "s1",
        "y2.1", "z3.1", "y1.1", "n1", "n2", "b0", "y3.0", "n3", "s2", "y3.1"
    ),
    "late": (
        "b1", "b2", "l0", "l1", "l2"
    ),
    "mid": (
        "b3", "l3"
    ),
    "tail": (
        "wa", "zn3", "wb", "xa0", "zn2", "ns", "xb0", "g_0", "xb1", "zn1", "xb3", "wc", "ng3",
        "xa2", "xa1", "ng2", "ya3", "nh2", "nh3", "xa3", "ng1", "ya2", "xb2", "g_1", "ya1", "nh1",
        "xc0", "ng0", "yb3", "xc1", "za3", "ya0", "zn0", "yb1", "za2", "yb2", "xc3", "g_2", "za1",
        "yb0", "xc2", "yc3", "zb3", "e", "yc1", "zb1", "yc2", "zb2", "zb0", "za0", "nh0", "tn",
        "g_3", "zc3", "zc1", "g_4", "zc2", "yc0", "zc0", "tb", "ta", "tN", "tc"
    ),
}


def layer_kernel(geo, *refs):
    Z, Y, X, C = geo["dims"]
    n_sem = geo["n_sem"]
    (
        edges_hbm,
        cot_hbm,
        nodes_hbm,
        ncot_hbm,
        send_hbm,
        recv_hbm,
        count_in,
        w1_hbm,
        w2_hbm,
        w3_hbm,
        w4_hbm,
        small_hbm,
        enew,
        egrad,
        nnew_out,
        ngrad_out,
        g1_out,
        g2_out,
        g3_out,
        g4_out,
        gs_out,
        edges,
        cot,
        nodes_in,
        ncot_in,
        send_in,
        recv_in,
        w1_in,
        w2_in,
        w3_in,
        w4_in,
        small_in,
        nbuf,
        dbuf,
        w1,
        w2,
        w3,
        w4,
        wa,
        wb,
        pick,
        spread,
        proj,
        slope,
        hidden,
        normed,
        rstd,
        term,
        dedge,
        dout,
        dpre,
        sums,
        pf,
        pb_a,
        pb_n,
        yr_a,
        yr_n,
        zs_a,
        zs_n,
        zr_a,
        zr_n,
        seg,
        sm_src,
        sm_rcv,
        sm_tile,
        par_all,
        gm_src,
        gm_rcv,
        gm_tile,
        gsm,
        *grad_refs,
    ) = refs
    local_sem, ssem, rsem = grad_refs[-3:]
    grad_refs = grad_refs[:-3]
    rows, D = edges.shape
    n = nodes_in.shape[0]
    N = Z * Y * n
    R = geo["chunk"]

    e_id = lax.axis_index("edge")
    g_id = lax.axis_index("grp")
    z = e_id // Y
    y = e_id % Y
    x = g_id // C
    c = g_id % C
    yp, xp, cp = 1 - y, 1 - x, 1 - c
    me = e_id * (X * C) + g_id
    y_dev = (z * Y + yp, g_id)
    x_dev = (e_id, xp * C + c)
    c_dev = (e_id, x * C + cp)

    def zx(m):
        place = z
        for j in range(m.bit_length()):
            if m >> j & 1:
                place = place + (1 << j) - (2 << j) * (z // (1 << j) % 2)
        return place

    def z_dev(m):
        return (zx(m) * Y + y, g_id)

    started = []

    def push(src, dst, dev):
        k = len(started)
        assert k < n_sem
        copy = pltpu.make_async_remote_copy(
            src_ref=src,
            dst_ref=dst,
            send_sem=ssem.at[k],
            recv_sem=rsem.at[k],
            device_id=dev,
            device_id_type=MESH,
        )
        copy.start()
        started.append(copy)
        return copy

    barrier = pltpu.get_barrier_semaphore()
    peers = [z_dev(m) for m in range(1, Z)] + [y_dev, x_dev, c_dev]
    for dev in peers:
        pl.semaphore_signal(barrier, inc=1, device_id=dev, device_id_type=MESH)
    loads = [
        (w1_hbm, w1_in),
        (w2_hbm, w2_in),
        (w3_hbm, w3_in),
        (w4_hbm, w4_in),
        (small_hbm, small_in),
        (nodes_hbm, nodes_in),
        (send_hbm, send_in),
        (recv_hbm, recv_in),
        (ncot_hbm, ncot_in),
        (edges_hbm, edges),
        (cot_hbm, cot),
    ]
    loads = [pltpu.make_async_copy(*pair, local_sem.at[k]) for k, pair in enumerate(loads)]
    for load in loads:
        load.start()
    for load in loads[0:6]:
        load.wait()
    r1, r2, r3, r4 = (own.shape[0] for own in (w1_in, w2_in, w3_in, w4_in))
    ra = r1 + r2
    wa[z, y, x, c, 0:r1, :] = w1_in[...].astype(bf16)
    wa[z, y, x, c, r1:ra, :] = w2_in[...].astype(bf16)
    wb[z, y, x, c, 0:r3, :] = w3_in[...].astype(bf16)
    wb[z, y, x, c, r3 : r3 + r4, :] = w4_in[...].astype(bf16)
    nbuf[z, y] = nodes_in[...]
    ws = small_in.shape[1]
    wide = ws * Y * X * C
    first = me % (Y * X * C) * ws
    place = (
        lax.broadcasted_iota(jnp.int32, (ws, wide), 1)
        == lax.broadcasted_iota(jnp.int32, (ws, wide), 0) + first
    )
    sm_src[0] = mm(small_in[...].astype(bf16), jnp.where(place, 1.0, 0.0).astype(bf16))

    for load in loads[6:9]:
        load.wait()
    lane = lax.broadcasted_iota(jnp.int32, (128, N), 1)
    sub = lax.broadcasted_iota(jnp.int32, (N, 128), 0)

    @pl.loop(0, rows // 128)
    def _(k):
        at = pl.ds(pl.multiple_of(k * 128, 128), 128)
        for half, ids in enumerate((send_in, recv_in)):
            row = jnp.broadcast_to(ids[0:1, at], (128, 128))
            col = jnp.tile(row.T, (1, N // 128))
            pick[at, half * N : (half + 1) * N] = jnp.where(lane == col, 1.0, 0.0).astype(bf16)
            flat = jnp.broadcast_to(ids[0:1, at], (N, 128))
            spread[half * N : (half + 1) * N, at] = jnp.where(sub == flat, 1.0, 0.0).astype(bf16)

    pl.semaphore_wait(barrier, len(peers))

    def along_z(own):
        return {1 << j: push(own, own, z_dev(1 << j)) for j in reversed(range((Z - 1).bit_length()))}

    def arrive_z(copies, m, block):
        copies[m].wait_recv()
        j = 0
        while not m >> j & 1:
            copies[m | 1 << j] = push(block, block, z_dev(1 << j))
            j += 1

    halves = ra // 2

    def part(zz, yy, xx, h):
        return wa.at[zz, yy, xx, c, h * halves : (h + 1) * halves, :]

    def send(block, dev):
        return push(block, block, dev)

    def settle(zz, yy, xx, cc):
        k = ((zz * Y + yy) * X + xx) * C + cc
        w1[pl.ds(pl.multiple_of(k * r1, 16), r1), :] = wa[zz, yy, xx, cc, 0:r1, :]
        w2[pl.ds(pl.multiple_of(k * r2, 16), r2), :] = wa[zz, yy, xx, cc, r1:ra, :]

    def small_sum(src, rcv, stage, copy):
        copy.wait_recv()
        src[stage + 1] = src[stage] + rcv[stage]

    small = [push(sm_src.at[0], sm_rcv.at[0], c_dev)]
    a_z, a_y, a_x, a_c, x_order = ({}, {}), {}, [], [], []
    n_z, n_y, b_z, b_y, b_x = {}, [], {}, [], []
    for h in range(2):
        own = part(z, y, x, h)
        a_z[h].update(along_z(own))
        a_y[0, h] = send(own, y_dev)
        a_x.append(send(own, x_dev))
        x_order.append((0, 0, h))
    a_c.append(send(wa.at[z, y, x, c], c_dev))

    def across(m, flip, h):
        yy = yp if flip else y
        a_x.append(send(part(zx(m), yy, x, h), x_dev))
        x_order.append((m, flip, h))
        if h == 1:
            a_c.append(send(wa.at[zx(m), yy, x, c], c_dev))
            settle(zx(m), yy, x, c)

    def on_z(m, h):
        block = part(zx(m), y, x, h)
        arrive_z(a_z[h], m, block)
        a_y[m, h] = send(block, y_dev)
        across(m, 0, h)

    def on_y(m, h):
        a_y[m, h].wait_recv()
        across(m, 1, h)

    def on_n(m, _):
        block = nbuf.at[zx(m), y]
        if m == 0:
            n_z.update(along_z(block))
        else:
            arrive_z(n_z, m, block)
        n_y.append(send(block, y_dev))

    def on_b(m, _):
        block = wb.at[zx(m), y, x, c]
        if m == 0:
            b_z.update(along_z(block))
        else:
            arrive_z(b_z, m, block)

    def line_b(m, _):
        block = wb.at[zx(m), y, x, c]
        b_y.append(send(block, y_dev))
        b_x.append(send(block, x_dev))

    def on_x(first, last):
        for k in range(first, last):
            m, flip, h = x_order[k]
            a_x[k].wait_recv()
            if h == 1:
                yy = yp if flip else y
                a_c.append(send(wa.at[zx(m), yy, xp, c], c_dev))
                settle(zx(m), yy, xp, c)

    def on_small(k, _):
        small_sum(sm_src, sm_rcv, k, small[k])
        if k < 2:
            small.append(push(sm_src.at[k + 1], sm_rcv.at[k + 1], (y_dev, x_dev)[k]))
        else:
            sm_tile[z] = sm_src[3]
            small.extend(push(sm_src.at[3], sm_tile.at[z], z_dev(m)) for m in range(1, Z))

    settle(z, y, x, c)
    steps = {"z": on_z, "y": on_y, "n": on_n, "b": on_b, "l": line_b, "x": on_x, "s": on_small}
    for step in geo["gather"]:
        kind, (m, h) = step[0], ([int(v) for v in step[1:].split(".")] + [0])[:2]
        if kind in "xs" or m < Z:
            steps[kind](m, h)
    on_x(0, len(x_order))
    for copy in n_y:
        copy.wait_recv()
    loads[9].wait()
    for copy in a_c:
        copy.wait_recv()
    for step in geo["late"]:
        kind, m = step[0], int(step[1:])
        if m < Z:
            steps[kind](m, 0)
    for zz in range(Z):
        for yy in range(Y):
            for xx in range(X):
                settle(zz, yy, xx, cp)
    for copy in small[3:]:
        copy.wait_recv()
    for zz in range(Z):
        par_all[:, zz * wide : (zz + 1) * wide] = sm_tile[zz]

    nodes_all = nbuf[...].reshape(N, D)
    proj[0:N, :] = mm(nodes_all, w1[D : 2 * D, :]).astype(bf16)
    proj[N : 2 * N, :] = mm(nodes_all, w1[2 * D : 3 * D, :]).astype(bf16)
    count = count_in[0, 0]
    row_id = lax.broadcasted_iota(jnp.int32, (R, D), 0)

    def edge_forward(i):
        at = pl.ds(pl.multiple_of(i * R, R), R)
        live = row_id < count - i * R
        own = edges[at, :]
        pre = mm(own, w1[0:D, :]) + mm(pick[at, :], proj[...]) + par_all[0:1, :]
        sig = jax.nn.sigmoid(pre)
        act = (pre * sig).astype(bf16)
        hidden[at, :] = act
        slope[at, :] = sig * (1.0 + pre * (1.0 - sig))
        out = mm(act, w2[...]) + par_all[1:2, :]
        norm, inv = norm_stats(out)
        normed[at, :] = norm
        rstd[at, :] = jnp.broadcast_to(inv, (R, 128))
        new = own.astype(f32) + jnp.where(live, norm * par_all[2:3, :] + par_all[3:4, :], 0.0)
        enew[at, :] = new.astype(bf16)
        term[at, :] = jnp.where(live, new, 0.0).astype(bf16)

    half = rows // R // 2
    pl.loop(0, half)(edge_forward)
    for step in geo["mid"]:
        kind, m = step[0], int(step[1:])
        if m < Z:
            steps[kind](m, 0)
    pl.loop(half, rows // R)(edge_forward)

    order = tuple(reversed(range(Z)))

    class NodeSum:
        def __init__(self, total, pb, yr, zs, zr):
            self.yr, self.zs, self.zr = yr, zs, zr
            pf[...] = total.reshape(Z, Y, 2, n // 2, D)
            pb[...] = total.astype(bf16).reshape(Z, Y, 2, n // 2, D)
            self.y = {
                (m, h): push(pb.at[zx(m), yp, h], yr.at[m, h], y_dev) for m in order for h in range(2)
            }

            self.z = {}

        def turn(self, m, h):
            self.y[m, h].wait_recv()
            part = pf[zx(m), y, h] + self.yr[m, h].astype(f32)
            if m == 0:
                pf[z, y, h] = part
            else:
                self.zs[m - 1, h] = part.astype(bf16)
                self.z[m, h] = push(self.zs.at[m - 1, h], self.zr.at[m - 1, h], z_dev(m))

        def total(self):
            sums = []
            for h in range(2):
                part = pf[z, y, h]
                for m in range(1, Z):
                    self.z[m, h].wait_recv()
                    part = part + self.zr[m - 1, h].astype(f32)
                sums.append(part)
            return jnp.concatenate(sums, axis=0)

    agg_sum = NodeSum(mm(spread[N : 2 * N, :], term[...]), pb_a, yr_a, zs_a, zr_a)
    for copy in b_y:
        copy.wait_recv()
    b_x.append(send(wb.at[:, yp, x, c], x_dev))
    b_c = [send(wb.at[:, yy, x, c], c_dev) for yy in (y, yp)]
    for m in order:
        for h in range(2):
            agg_sum.turn(m, h)
    for copy in b_x[:-1]:
        copy.wait_recv()
    b_c.append(send(wb.at[:, y, xp, c], c_dev))
    b_x[-1].wait_recv()
    b_c.append(send(wb.at[:, yp, xp, c], c_dev))
    for copy in b_c:
        copy.wait_recv()
    w3[...] = wb[:, :, :, :, 0:r3, :].reshape(w3.shape)
    w4[...] = wb[:, :, :, :, r3 : r3 + r4, :].reshape(w4.shape)
    own_nodes = nodes_in[...]
    pre_own = mm(own_nodes, w3[0:D, :])
    agg = agg_sum.total()

    def par(k):
        return par_all[k : k + 1, :]

    agg_low = agg.astype(bf16)
    pre_n = pre_own + mm(agg_low, w3[D : 2 * D, :]) + par(4)
    sig_n = jax.nn.sigmoid(pre_n)
    hidden_n = (pre_n * sig_n).astype(bf16)
    out_n = mm(hidden_n, w4[...]) + par(5)
    normed_n, rstd_n = norm_stats(out_n)
    ncot = ncot_in[...].astype(f32)
    d_out_n = norm_back(ncot, normed_n, rstd_n, par(6)).astype(bf16)
    slope_n = sig_n * (1.0 + pre_n * (1.0 - sig_n))
    d_pre_n = (times_t(d_out_n, w4[...]) * slope_n).astype(bf16)
    dbuf[z, y] = times_t(d_pre_n, w3[D : 2 * D, :]).astype(bf16)
    d_z, d_y = {}, []

    def d_part(m, h):
        return dbuf.at[zx(m), y, h * (n // 2) : (h + 1) * (n // 2), :]

    for h in range(2):
        for m in order[:-1]:
            d_z[m, h] = send(d_part(0, h), z_dev(m))
        d_y.append(send(d_part(0, h), y_dev))

    class WeightSum:
        def __init__(self, grad, crecv, xs, xrecv, ks, ys, yrecv, zs, zrecv):
            self.grad, self.crecv, self.xs, self.xrecv, self.ks = grad, crecv, xs, xrecv, ks
            self.ys, self.yrecv, self.zs, self.zrecv = ys, yrecv, zs, zrecv

        def put(self, first, values, lane_rows=None, base=0):
            low, r = values.astype(bf16), lane_rows or self.grad.shape[4]
            row = 0
            while row < values.shape[0]:
                k, off = divmod(first + row, r)
                size = min(r - off, values.shape[0] - row)
                at = (k // (Y * X * C), k // (X * C) % Y, k // C % X, k % C)
                self.grad[(*at, slice(base + off, base + off + size))] = low[row : row + size]
                row += size

        def start(self):
            self.c = [
                push(self.grad.at[:, yy, xx, cp], self.crecv.at[k], c_dev)
                for k, (yy, xx) in enumerate(((yp, xp), (y, xp), (yp, x), (y, x)))
            ]

            self.x, self.y, self.z = {}, {}, {}

        def cross_x(self, k):
            self.c[k].wait_recv()
            for m in order:
                part = self.grad[zx(m), (yp, y)[k % 2], (xp, x)[k // 2], c].astype(f32)
                part = part + self.crecv[k, zx(m)].astype(f32)
                if k < 2:
                    self.xs[k, m] = part.astype(bf16)
                    self.x[k, m] = push(self.xs.at[k, m], self.xrecv.at[k, m], x_dev)
                else:
                    self.ks[k - 2, m] = part

        def cross_y(self, m):
            self.x[0, m].wait_recv()
            self.ys[m] = (self.ks[0, m] + self.xrecv[0, m].astype(f32)).astype(bf16)
            self.y[m] = push(self.ys.at[m], self.yrecv.at[m], y_dev)

        def cross_z(self, m):
            self.x[1, m].wait_recv()
            self.y[m].wait_recv()
            part = self.ks[1, m] + self.xrecv[1, m].astype(f32) + self.yrecv[m].astype(f32)
            if m == 0:
                self.ks[1, 0] = part
            else:
                self.zs[m - 1] = part.astype(bf16)
                self.z[m] = push(self.zs.at[m - 1], self.zrecv.at[m - 1], z_dev(m))

        def total(self):
            result = self.ks[1, 0]
            for o in range(1, Z):
                self.z[o].wait_recv()
                result = result + self.zrecv[o - 1].astype(f32)
            return result

    per = len(grad_refs) // 4
    sum1a, sum1b, sum2, sum_n = [WeightSum(*grad_refs[k * per : (k + 1) * per]) for k in range(4)]

    sum_n.put(0, inner(own_nodes, d_pre_n), r3)
    sum_n.put(D, inner(agg_low, d_pre_n), r3)
    sum_n.put(0, inner(hidden_n, d_out_n), r4, r3)
    sum_n.start()
    nnew_out[...] = (own_nodes.astype(f32) + normed_n * par(6) + par(7)).astype(bf16)
    node_part = ncot + times_t(d_pre_n, w3[0:D, :])
    gsm[4:5, :] = jnp.sum(d_pre_n.astype(f32), axis=0, keepdims=True)
    gsm[5:6, :] = jnp.sum(d_out_n.astype(f32), axis=0, keepdims=True)
    gsm[6:7, :] = jnp.sum(ncot * normed_n, axis=0, keepdims=True)
    gsm[7:8, :] = jnp.sum(ncot, axis=0, keepdims=True)
    for h in range(2):
        for m in range(1, Z):
            d_z[m, h].wait_recv()
            d_y.append(send(d_part(m, h), y_dev))
    for k in range(4):
        sum_n.cross_x(k)
    loads[10].wait()
    for copy in d_y:
        copy.wait_recv()

    sums[...] = jnp.zeros_like(sums)
    d_all = dbuf[...].reshape(N, D)

    def edge_back(i):
        at = pl.ds(pl.multiple_of(i * R, R), R)
        live = row_id < count - i * R
        d_edge = cot[at, :].astype(f32) + jnp.where(live, mm(pick[at, N : 2 * N], d_all), 0.0)
        dedge[at, :] = d_edge
        masked = jnp.where(live, d_edge, 0.0)
        norm = normed[at, :]
        inv = rstd[at, 0:1]
        weighted = masked * norm
        sums[2] += fold_rows(weighted)
        sums[3] += fold_rows(masked)
        d_out = norm_back(masked, norm, inv, par(2)).astype(bf16)
        dout[at, :] = d_out
        sums[1] += fold_rows(d_out.astype(f32))
        d_pre = (times_t(d_out, w2[...]) * slope[at, :]).astype(bf16)
        dpre[at, :] = d_pre
        sums[0] += fold_rows(d_pre.astype(f32))

    pl.loop(0, half)(edge_back)
    for m in order:
        sum_n.cross_y(m)
    pl.loop(half, rows // R)(edge_back)
    edges_all = edges[...]

    def edge_grads(k, into):
        at = slice(k * (D // 2), (k + 1) * (D // 2))
        d_pre = dpre[:, at]
        into.put(0, inner(edges_all, d_pre))
        for half in range(2):
            nodes_at = slice(half * N, (half + 1) * N)
            seg[nodes_at, at] = mm(spread[nodes_at, :], d_pre).astype(bf16)
            into.put((1 + half) * D, inner(nodes_all, seg[nodes_at, at]))
        into.start()

    sums_w = {"a": sum1a, "b": sum1b, "c": sum2, "n": sum_n}
    gm = []
    later = {}

    def step_w(which, _):
        if which == "c":
            sum2.put(0, inner(hidden[...], dout[...]))
            sum2.start()
        else:
            edge_grads("ab".index(which), sums_w[which])

    def step_t(which, _):
        if which == "N":
            ngrad_out[...] = (node_part + later["N"].total()).astype(bf16)
            return
        result = sums_w[which].total()
        if which == "n":
            g3_out[...] = result[0:r3]
            g4_out[...] = result[r3 : r3 + r4]
        elif which == "c":
            g2_out[...] = result
        else:
            k = "ab".index(which)
            g1_out[:, k * (D // 2) : (k + 1) * (D // 2)] = result

    def step_n(which, k):
        if which == "s":
            later["N"] = NodeSum(
                times_t(seg[0:N, :], w1[D : 2 * D, :])
                + times_t(seg[N : 2 * N, :], w1[2 * D : 3 * D, :]),
                pb_n,
                yr_n,
                zs_n,
                zr_n,
            )
        else:
            later["N"].turn(k, "gh".index(which))

    def step_e(*_):
        @pl.loop(0, rows // R)
        def _(i):
            at = pl.ds(pl.multiple_of(i * R, R), R)
            egrad[at, :] = (dedge[at, :] + times_t(dpre[at, :], w1[0:D, :])).astype(bf16)

    def step_g(_, k):
        if k == 0:
            for row in range(4):
                gsm[row : row + 1, :] = jnp.sum(sums[row], axis=0, keepdims=True)
            for zz in range(Z):
                gm_tile[zz] = gsm[:, zz * wide : (zz + 1) * wide]
            gm.extend(
                push(gm_tile.at[zx(m)], gm_tile.at[Z + m - 1], z_dev(m)) for m in range(1, Z)
            )
        elif k == 1:
            tile = gm_tile[z]
            for m in range(1, Z):
                gm[m - 1].wait_recv()
                tile = tile + gm_tile[Z + m - 1]
            gm_src[0] = tile
            gm.append(push(gm_src.at[0], gm_rcv.at[0], y_dev))
        else:
            small_sum(gm_src, gm_rcv, k - 2, gm[-1])
            if k < 4:
                gm.append(push(gm_src.at[k - 1], gm_rcv.at[k - 1], (x_dev, c_dev)[k - 2]))
                return
            take = (
                lax.broadcasted_iota(jnp.int32, (wide, ws), 0)
                == lax.broadcasted_iota(jnp.int32, (wide, ws), 1) + first
            )
            gs_out[...] = jnp.dot(
                gm_src[3],
                jnp.where(take, 1.0, 0.0),
                preferred_element_type=f32,
                precision=lax.Precision.HIGHEST,
            )

    tail = {
        "w": step_w,
        "x": lambda which, k: sums_w[which].cross_x(k),
        "y": lambda which, m: sums_w[which].cross_y(m),
        "z": lambda which, m: sums_w[which].cross_z(m),
        "t": step_t,
        "n": step_n,
        "e": step_e,
        "g": step_g,
    }
    for step in geo["tail"]:
        kind, which, k = step[0], step[1:2], int(step[2:] or 0)
        if kind not in "yzn" or k < Z:
            tail[kind](which, k)
    for copy in started:
        copy.wait_send()


def update_kernel(*refs):
    passed, weights, firsts, seconds = refs[0:9], refs[9:14], refs[14:19], refs[19:24]
    outs, new_v, new_w, smalls, sem = refs[24:43], refs[43:47], refs[47:51], refs[51:54], refs[54]
    enew, egrad, nnew, ngrad, *grads = passed
    copies = []

    def put(src, dst):
        copies.append(pltpu.make_async_copy(src, dst, sem.at[len(copies)]))
        copies[-1].start()

    for src, dst in zip((weights[4], firsts[4], seconds[4]), smalls):
        put(src, dst)
    for src, dst in zip((enew, nnew, egrad, ngrad), outs[:4]):
        put(src, dst.at[0])
    for k in range(4):
        put(grads[k], outs[4 + k])
    outs[8][...] = grads[4][...]
    for k in range(4):
        new_w[k][...], new_v[k][...] = adamw(
            weights[k][...], grads[k][...], firsts[k][...], seconds[k][...], 0.03
        )
        put(new_v[k], outs[9 + k])
        put(new_w[k], outs[14 + k])
    for copy in copies[:3]:
        copy.wait()
    small, first, second = (ref[...] for ref in smalls)
    outs[18][...], outs[13][...] = adamw(small, grads[4][...], first, second, 0.2)
    for copy in copies[3:]:
        copy.wait()


def on_device(n_edge, n_grp, *args):
    (
        edge_lat,
        node_lat,
        edge_cot,
        node_cot,
        senders,
        receivers,
        edge_count,
        *state,
    ) = args
    weights, firsts, seconds = state[0:5], state[5:10], state[10:15]
    rows, D = edge_lat.shape[1:]
    n = node_lat.shape[1]
    N = n * n_edge
    n_dev = n_edge * n_grp
    shards = [w.shape[0] for w in weights[:4]]
    fits = (
        n_edge % 2 == 0
        and n_grp == 4
        and all(r % 16 == 0 for r in shards)
        and n_edge // 2 in (2, 4)
        and D % (128 * (n_edge // 2)) == 0
        and D % 256 == 0
        and N % 128 == 0
        and n % 32 == 0
        and (shards[0] + shards[1]) % 32 == 0
        and rows % 256 == 0
        and rows * N <= 1024 * 1024
    )
    if not fits:
        return native(*args)
    Z, Y, X, C = n_edge // 2, 2, 2, 2
    n_sem = 240

    def vm(shape, dtype=bf16):
        return pltpu.VMEM(shape, dtype)

    ins = [edge_lat[0], edge_cot[0], node_lat[0], node_cot[0], senders, receivers, edge_count, *weights]
    scratch = [
        *[vm(a.shape, a.dtype) for a in ins if a is not edge_count],
        vm((Z, Y, n, D)),
        vm((Z, Y, n, D)),
        *[vm((r * n_dev, D)) for r in shards],
        vm((Z, Y, X, C, shards[0] + shards[1], D)),
        vm((Z, Y, X, C, shards[2] + shards[3], D)),
        vm((rows, 2 * N)),
        vm((2 * N, rows)),
        vm((2 * N, D)),
        vm((rows, D), f32),
        vm((rows, D)),
        vm((rows, D), f32),
        vm((rows, 128), f32),
        vm((rows, D)),
        vm((rows, D), f32),
        vm((rows, D)),
        vm((rows, D)),
        vm((4, 8, D), f32),
        vm((Z, Y, 2, n // 2, D), f32),
        vm((Z, Y, 2, n // 2, D)),
        vm((Z, Y, 2, n // 2, D)),
        vm((Z, 2, n // 2, D)),
        vm((Z, 2, n // 2, D)),
        *[vm((Z - 1, 2, n // 2, D))] * 4,
        vm((2 * N, D)),
        vm((4, 8, D // Z), f32),
        vm((3, 8, D // Z), f32),
        vm((Z, 8, D // Z), f32),
        vm((8, D), f32),
        vm((4, 8, D // Z), f32),
        vm((3, 8, D // Z), f32),
        vm((2 * Z - 1, 8, D // Z), f32),
        vm((8, D), f32),
    ]
    blocks = ((shards[0], D // 2), (shards[0], D // 2), (shards[1], D), (shards[2] + shards[3], D))
    for r, cols in blocks:
        scratch += [
            vm((Z, Y, X, C, r, cols)),
            vm((4, Z, r, cols)),
            vm((2, Z, r, cols)),
            vm((2, Z, r, cols)),
            vm((2, Z, r, cols), f32),
            vm((Z, r, cols)),
            vm((Z, r, cols)),
            vm((Z - 1, r, cols)),
            vm((Z - 1, r, cols)),
        ]
    scratch += [
        pltpu.SemaphoreType.DMA((len(ins),)),
        pltpu.SemaphoreType.DMA((n_sem,)),
        pltpu.SemaphoreType.DMA((n_sem,)),
    ]
    hbm = pl.BlockSpec(memory_space=pltpu.HBM)
    anyspace = pl.BlockSpec(memory_space=pl.ANY)
    vmem = pl.BlockSpec(memory_space=pltpu.VMEM)
    results = pl.pallas_call(
        functools.partial(layer_kernel, dict(GEO, dims=(Z, Y, X, C), n_sem=n_sem)),
        out_shape=[vm((rows, D))] * 2 + [vm((n, D))] * 2 + [vm(w.shape, f32) for w in weights],
        in_specs=[hbm] * 6 + [pl.BlockSpec(memory_space=pltpu.SMEM)] + [hbm] * 5,
        out_specs=[vmem] * 9,
        scratch_shapes=scratch,
        compiler_params=pltpu.CompilerParams(
            collective_id=0, has_side_effects=True, vmem_limit_bytes=52 * 1024 * 1024
        ),
        name="layer",
    )(*ins)
    sds = jax.ShapeDtypeStruct
    state_out = [sds(w.shape, f32) for w in weights]
    kept = [vm(w.shape, f32) for w in weights[:4]]
    return tuple(
        pl.pallas_call(
            update_kernel,
            out_shape=[
                sds((1, rows, D), bf16),
                sds((1, n, D), bf16),
                sds((1, rows, D), bf16),
                sds((1, n, D), bf16),
                *state_out,
                *state_out,
                *state_out,
            ],
            in_specs=[vmem] * 9 + ([vmem] * 4 + [hbm]) * 3,
            out_specs=[anyspace] * 4 + ([anyspace] * 4 + [vmem]) * 3,
            scratch_shapes=[
                *kept,
                *kept,
                *[vm(weights[4].shape, f32)] * 3,
                pltpu.SemaphoreType.DMA((19,)),
            ],
            compiler_params=pltpu.CompilerParams(vmem_limit_bytes=8 * 1024 * 1024),
            name="update",
        )(*results, *weights, *firsts, *seconds)
    )


def solution(mesh):
    in_specs = (
        P("grp", "edge", None),
        P("grp", "edge", None),
        P("grp", "edge", None),
        P("grp", "edge", None),
        P("grp", "edge"),
        P("grp", "edge"),
        P("grp", "edge"),
        P(("edge", "grp"), None),
        P(("edge", "grp"), None),
        P(("edge", "grp"), None),
        P(("edge", "grp"), None),
        P(None, ("edge", "grp")),
        P(("edge", "grp"), None),
        P(("edge", "grp"), None),
        P(("edge", "grp"), None),
        P(("edge", "grp"), None),
        P(None, ("edge", "grp")),
        P(("edge", "grp"), None),
        P(("edge", "grp"), None),
        P(("edge", "grp"), None),
        P(("edge", "grp"), None),
        P(None, ("edge", "grp")),
    )
    out_specs = (
        P("grp", "edge", None),
        P("grp", "edge", None),
        P("grp", "edge", None),
        P("grp", "edge", None),
        P(("edge", "grp"), None),
        P(("edge", "grp"), None),
        P(("edge", "grp"), None),
        P(("edge", "grp"), None),
        P(None, ("edge", "grp")),
        P(("edge", "grp"), None),
        P(("edge", "grp"), None),
        P(("edge", "grp"), None),
        P(("edge", "grp"), None),
        P(None, ("edge", "grp")),
        P(("edge", "grp"), None),
        P(("edge", "grp"), None),
        P(("edge", "grp"), None),
        P(("edge", "grp"), None),
        P(None, ("edge", "grp")),
    )
    return jax.shard_map(
        functools.partial(on_device, mesh.shape["edge"], mesh.shape["grp"]),
        mesh=mesh, in_specs=in_specs, out_specs=out_specs, check_vma=False
    )
```

```python
import functools

import jax
import jax.numpy as jnp
from jax import lax
from jax.experimental import pallas as pl
from jax.experimental.pallas import tpu as pltpu
from jax.sharding import PartitionSpec as P

step_count = 10.0


def inner(left, right):
    return lax.dot_general(
        left, right, (((0,), (0,)), ((), ())), preferred_element_type=jnp.float32
    )


def times_t(left, right):
    return lax.dot_general(
        left, right, (((1,), (1,)), ((), ())), preferred_element_type=jnp.float32
    )


def norm_stats(values):
    mean = jnp.mean(values, axis=-1, keepdims=True)
    centred = values - mean
    var = jnp.mean(centred * centred, axis=-1, keepdims=True)
    rstd = lax.rsqrt(var + 1e-05)
    return (centred * rstd, rstd)


def norm_back(grad_out, normed, rstd, gain):
    scaled = grad_out * gain
    return rstd * (
        scaled
        - jnp.mean(scaled, axis=-1, keepdims=True)
        - normed * jnp.mean(scaled * normed, axis=-1, keepdims=True)
    )


def silu_slope(values):
    sig = jax.nn.sigmoid(values)
    return sig * (1.0 + values * (1.0 - sig))


def adamw(weight, grad, first, second, rate):
    first_new = 0.9 * first + 0.1 * grad
    second_new = 0.999 * second + 0.001 * grad * grad
    mhat = first_new / (1.0 - 0.9**step_count)
    vhat = second_new / (1.0 - 0.999**step_count)
    return (weight - rate * (mhat / (jnp.sqrt(vhat) + 1e-08) + 0.1 * weight), second_new)


def native(
    edge_lat,
    node_lat,
    edge_cot,
    node_cot,
    senders,
    receivers,
    edge_count,
    w_edge_in,
    w_edge_out,
    w_node_in,
    w_node_out,
    small_params,
    first_edge_in,
    first_edge_out,
    first_node_in,
    first_node_out,
    first_small,
    second_edge_in,
    second_edge_out,
    second_node_in,
    second_node_out,
    second_small,
):
    bf = jnp.bfloat16
    edges = edge_lat[0]
    nodes = node_lat[0]
    send = senders[0]
    recv = receivers[0]
    rows = edges.shape[0]
    width = edges.shape[1]
    maskf = (jnp.arange(rows, dtype=jnp.int32) < edge_count[0, 0]).astype(jnp.float32)[:, None]
    w1e, w2e, w1n, w2n, small = (
        lax.all_gather(w_edge_in.astype(bf), ("edge", "grp"), axis=0, tiled=True),
        lax.all_gather(w_edge_out.astype(bf), ("edge", "grp"), axis=0, tiled=True),
        lax.all_gather(w_node_in.astype(bf), ("edge", "grp"), axis=0, tiled=True),
        lax.all_gather(w_node_out.astype(bf), ("edge", "grp"), axis=0, tiled=True),
        lax.all_gather(small_params.astype(bf), ("edge", "grp"), axis=1, tiled=True),
    )
    params = small.astype(jnp.float32)
    whole = lax.all_gather(nodes, "edge", axis=0, tiled=True)
    node_total = whole.shape[0]
    joined = jnp.concatenate([edges, whole[send], whole[recv]], axis=1)
    pre = jnp.dot(joined, w1e, preferred_element_type=jnp.float32) + params[0]
    hidden = jax.nn.silu(pre).astype(bf)
    out = jnp.dot(hidden, w2e, preferred_element_type=jnp.float32) + params[1]
    normed, rstd = norm_stats(out)
    edge_new = edges.astype(jnp.float32) + maskf * (normed * params[2] + params[3])
    dense = jnp.zeros((node_total, width), jnp.float32).at[recv].add(maskf * edge_new)
    agg = lax.psum_scatter(dense, "edge", scatter_dimension=0, tiled=True)
    node_in = jnp.concatenate([nodes, agg.astype(bf)], axis=1)
    pre_n = jnp.dot(node_in, w1n, preferred_element_type=jnp.float32) + params[4]
    hidden_n = jax.nn.silu(pre_n).astype(bf)
    out_n = jnp.dot(hidden_n, w2n, preferred_element_type=jnp.float32) + params[5]
    normed_n, rstd_n = norm_stats(out_n)
    node_new = nodes.astype(jnp.float32) + normed_n * params[6] + params[7]
    grad_node_out_f = node_cot[0].astype(jnp.float32)
    d_out_n = norm_back(grad_node_out_f, normed_n, rstd_n, params[6]).astype(bf)
    gain_n = jnp.sum(grad_node_out_f * normed_n, axis=0)
    shift_n = jnp.sum(grad_node_out_f, axis=0)
    g_w2n = inner(hidden_n, d_out_n)
    g_b2n = jnp.sum(d_out_n.astype(jnp.float32), axis=0)
    d_pre_n = (times_t(d_out_n, w2n) * silu_slope(pre_n)).astype(bf)
    g_w1n = inner(node_in, d_pre_n)
    g_b1n = jnp.sum(d_pre_n.astype(jnp.float32), axis=0)
    d_node_in = times_t(d_pre_n, w1n)
    node_part = grad_node_out_f + d_node_in[:, :width]
    d_agg = d_node_in[:, width:].astype(bf)
    agg_rows = lax.all_gather(d_agg, "edge", axis=0, tiled=True)
    d_edge = edge_cot[0].astype(jnp.float32) + maskf * agg_rows[recv].astype(jnp.float32)
    masked = maskf * d_edge
    d_out = norm_back(masked, normed, rstd, params[2]).astype(bf)
    gain_e = jnp.sum(masked * normed, axis=0)
    shift_e = jnp.sum(masked, axis=0)
    g_w2e = inner(hidden, d_out)
    g_b2e = jnp.sum(d_out.astype(jnp.float32), axis=0)
    d_pre = (times_t(d_out, w2e) * silu_slope(pre)).astype(bf)
    g_w1e = inner(joined, d_pre)
    g_b1e = jnp.sum(d_pre.astype(jnp.float32), axis=0)
    d_joined = times_t(d_pre, w1e)
    edge_grad = (d_edge + d_joined[:, :width]).astype(bf)
    dense_grad = jnp.zeros((node_total, width), jnp.float32)
    dense_grad = (
        dense_grad.at[send]
        .add(d_joined[:, width : 2 * width])
        .at[recv]
        .add(d_joined[:, 2 * width :])
    )
    node_sum = lax.psum_scatter(dense_grad, "edge", scatter_dimension=0, tiled=True)
    node_grad = (node_part + node_sum).astype(bf)
    g_small = jnp.stack([g_b1e, g_b2e, gain_e, shift_e, g_b1n, g_b2n, gain_n, shift_n])
    grads = (
        lax.psum_scatter(g_w1e, ("edge", "grp"), scatter_dimension=0, tiled=True),
        lax.psum_scatter(g_w2e, ("edge", "grp"), scatter_dimension=0, tiled=True),
        lax.psum_scatter(g_w1n, ("edge", "grp"), scatter_dimension=0, tiled=True),
        lax.psum_scatter(g_w2n, ("edge", "grp"), scatter_dimension=0, tiled=True),
        lax.psum_scatter(g_small, ("edge", "grp"), scatter_dimension=1, tiled=True),
    )
    weights = (w_edge_in, w_edge_out, w_node_in, w_node_out, small_params)
    firsts = (first_edge_in, first_edge_out, first_node_in, first_node_out, first_small)
    seconds = (second_edge_in, second_edge_out, second_node_in, second_node_out, second_small)
    rates = (0.03, 0.03, 0.03, 0.03, 0.2)
    updated = [
        adamw(w, g, m, v, r) for w, g, m, v, r in zip(weights, grads, firsts, seconds, rates)
    ]
    return (
        edge_new.astype(bf)[None],
        node_new.astype(bf)[None],
        edge_grad[None],
        node_grad[None],
        grads[0],
        grads[1],
        grads[2],
        grads[3],
        grads[4],
        updated[0][1],
        updated[1][1],
        updated[2][1],
        updated[3][1],
        updated[4][1],
        updated[0][0],
        updated[1][0],
        updated[2][0],
        updated[3][0],
        updated[4][0],
    )


bf16 = jnp.bfloat16
f32 = jnp.float32
MESH = pl.DeviceIdType.MESH


def mm(left, right):
    return jnp.dot(left, right, preferred_element_type=f32)


def fold_rows(values):
    count, width = values.shape
    return jnp.sum(values.reshape(count // 8, 8, width), axis=0)


GEO = {
    "gather": (
        "n0", "y0.0", "y0.1", "z1.0", "z2.0", "z1.1", "z2.1", "y1.0", "y2.0", "s0", "z3.0", "s1",
        "y2.1", "z3.1", "y1.1", "n1", "n2", "b0", "y3.0", "n3", "s2", "y3.1"
    ),
    "late": (
        "b1", "b2", "l0", "l1", "l2"
    ),
    "mid": (
        "b3", "l3"
    ),
    "agg": (
        "p3", "p2", "p1", "p0", "b0", "t3.0", "t3.1", "t2.0", "g2.0", "t2.1", "b1", "t1.0", "g2.1",
        "t1.1", "t0.0", "b2", "t0.1", "b3", "g0.0", "g0.1"
    ),
    "back": (
        "x0", "x1", "d1.0", "d2.0", "d1.1", "d2.1", "d3.0", "d3.1", "x2", "x3"
    ),
    "tail": (
        "wa", "wb", "xa0", "zn2", "ns", "xa2", "wc", "xb0", "xb2", "zn1", "xc0", "zn3", "g_0",
        "xa3", "xa1", "ya3", "ng3", "xb1", "ng2", "zn0", "ya1", "ya2", "nh3", "mn2", "yb3", "ng1",
        "mn0", "yb0", "nh2", "ng0", "nh1", "xc3", "g_1", "yb1", "xc1", "xc2", "za3", "e", "no2",
        "nm0", "za2", "yc3", "za1", "yb2", "ya0", "xb3", "yc2", "zb3", "ma2", "zb1", "nh0", "yc1",
        "g_2", "zc3", "tn", "nm2", "zb2", "zc2", "za0", "mb2", "mc2", "ma0", "g_3", "yc0", "zc1",
        "zb0", "mb0", "no0", "g_4", "zc0", "tb", "tN", "ta", "mc0", "tc"
    ),
}


def layer_kernel(geo, *refs):
    Z, Y, X, C = geo["dims"]
    n_sem = geo["n_sem"]
    (
        edges_hbm,
        cot_hbm,
        nodes_hbm,
        ncot_hbm,
        send_hbm,
        recv_hbm,
        count_in,
        w1_hbm,
        w2_hbm,
        w3_hbm,
        w4_hbm,
        small_hbm,
        enew,
        egrad,
        nnew_out,
        ngrad_out,
        g1_out,
        g2_out,
        g3_out,
        g4_out,
        gs_out,
        edges,
        cot,
        nodes_in,
        ncot_in,
        send_in,
        recv_in,
        w1_in,
        w2_in,
        w3_in,
        w4_in,
        small_in,
        nbuf,
        dbuf,
        w1,
        w2,
        w3,
        w4,
        wa,
        wb,
        pick,
        spread,
        proj,
        slope,
        hidden,
        normed,
        rstd,
        term,
        dedge,
        dout,
        dpre,
        sums,
        pf,
        pb_a,
        pb_n,
        yr_a,
        yr_n,
        zs_a,
        zs_n,
        zr_a,
        zr_n,
        seg,
        sm_src,
        sm_rcv,
        sm_tile,
        par_all,
        gm_src,
        gm_rcv,
        gm_tile,
        gsm,
        *grad_refs,
    ) = refs
    local_sem, ssem, rsem = grad_refs[-3:]
    grad_refs = grad_refs[:-3]
    rows, D = edges.shape
    n = nodes_in.shape[0]
    N = Z * Y * n
    R = rows // 2

    e_id = lax.axis_index("edge")
    g_id = lax.axis_index("grp")
    z = e_id // Y
    y = e_id % Y
    x = g_id // C
    c = g_id % C
    yp, xp, cp = 1 - y, 1 - x, 1 - c
    me = e_id * (X * C) + g_id
    y_dev = (z * Y + yp, g_id)
    x_dev = (e_id, xp * C + c)
    c_dev = (e_id, x * C + cp)

    def zx(m):
        place = z
        for j in range(m.bit_length()):
            if m >> j & 1:
                place = place + (1 << j) - (2 << j) * (z // (1 << j) % 2)
        return place

    def z_dev(m):
        return (zx(m) * Y + y, g_id)

    started = []

    def push(src, dst, dev):
        k = len(started)
        assert k < n_sem
        copy = pltpu.make_async_remote_copy(
            src_ref=src,
            dst_ref=dst,
            send_sem=ssem.at[k],
            recv_sem=rsem.at[k],
            device_id=dev,
            device_id_type=MESH,
        )
        copy.start()
        started.append(copy)
        return copy

    barrier = pltpu.get_barrier_semaphore()
    peers = [z_dev(m) for m in range(1, Z)] + [y_dev, x_dev, c_dev]
    for dev in peers:
        pl.semaphore_signal(barrier, inc=1, device_id=dev, device_id_type=MESH)
    loads = [
        (w1_hbm, w1_in),
        (w2_hbm, w2_in),
        (w3_hbm, w3_in),
        (w4_hbm, w4_in),
        (small_hbm, small_in),
        (nodes_hbm, nodes_in),
        (send_hbm, send_in),
        (recv_hbm, recv_in),
        (ncot_hbm, ncot_in),
        (edges_hbm, edges),
        (cot_hbm, cot),
    ]
    loads = [pltpu.make_async_copy(*pair, local_sem.at[k]) for k, pair in enumerate(loads)]
    for load in loads:
        load.start()
    for load in loads[0:6]:
        load.wait()
    r1, r2, r3, r4 = (own.shape[0] for own in (w1_in, w2_in, w3_in, w4_in))
    ra = r1 + r2
    wa[z, y, x, c, 0:r1, :] = w1_in[...].astype(bf16)
    wa[z, y, x, c, r1:ra, :] = w2_in[...].astype(bf16)
    wb[z, y, x, c, 0:r3, :] = w3_in[...].astype(bf16)
    wb[z, y, x, c, r3 : r3 + r4, :] = w4_in[...].astype(bf16)
    nbuf[z, y] = nodes_in[...]
    ws = small_in.shape[1]
    wide = ws * Y * X * C
    first = me % (Y * X * C) * ws
    place = (
        lax.broadcasted_iota(jnp.int32, (ws, wide), 1)
        == lax.broadcasted_iota(jnp.int32, (ws, wide), 0) + first
    )
    sm_src[0] = mm(small_in[...].astype(bf16), jnp.where(place, 1.0, 0.0).astype(bf16))

    for load in loads[6:9]:
        load.wait()
    lane = lax.broadcasted_iota(jnp.int32, (128, N), 1)
    sub = lax.broadcasted_iota(jnp.int32, (N, 128), 0)

    @pl.loop(0, rows // 128)
    def _(k):
        at = pl.ds(pl.multiple_of(k * 128, 128), 128)
        for half, ids in enumerate((send_in, recv_in)):
            row = jnp.broadcast_to(ids[0:1, at], (128, 128))
            col = jnp.tile(row.T, (1, N // 128))
            pick[at, half * N : (half + 1) * N] = jnp.where(lane == col, 1.0, 0.0).astype(bf16)
            flat = jnp.broadcast_to(ids[0:1, at], (N, 128))
            spread[half * N : (half + 1) * N, at] = jnp.where(sub == flat, 1.0, 0.0).astype(bf16)

    pl.semaphore_wait(barrier, len(peers))

    def along_z(own):
        return {1 << j: push(own, own, z_dev(1 << j)) for j in reversed(range((Z - 1).bit_length()))}

    def arrive_z(copies, m, block):
        copies[m].wait_recv()
        j = 0
        while not m >> j & 1:
            copies[m | 1 << j] = push(block, block, z_dev(1 << j))
            j += 1

    halves = ra // 2

    def part(zz, yy, xx, h):
        return wa.at[zz, yy, xx, c, h * halves : (h + 1) * halves, :]

    def send(block, dev):
        return push(block, block, dev)

    def settle(zz, yy, xx, cc):
        k = ((zz * Y + yy) * X + xx) * C + cc
        w1[pl.ds(pl.multiple_of(k * r1, 16), r1), :] = wa[zz, yy, xx, cc, 0:r1, :]
        w2[pl.ds(pl.multiple_of(k * r2, 16), r2), :] = wa[zz, yy, xx, cc, r1:ra, :]

    def small_sum(src, rcv, stage, copy):
        copy.wait_recv()
        src[stage + 1] = src[stage] + rcv[stage]

    small = [push(sm_src.at[0], sm_rcv.at[0], c_dev)]
    a_z, a_y, a_x, a_c, x_order = ({}, {}), {}, [], [], []
    n_z, n_y, b_z, b_y, b_x = {}, [], {}, [], []
    for h in range(2):
        own = part(z, y, x, h)
        a_z[h].update(along_z(own))
        a_y[0, h] = send(own, y_dev)
        a_x.append(send(own, x_dev))
        x_order.append((0, 0, h))
    a_c.append(send(wa.at[z, y, x, c], c_dev))

    def across(m, flip, h):
        yy = yp if flip else y
        a_x.append(send(part(zx(m), yy, x, h), x_dev))
        x_order.append((m, flip, h))
        if h == 1:
            a_c.append(send(wa.at[zx(m), yy, x, c], c_dev))
            settle(zx(m), yy, x, c)

    def on_z(m, h):
        block = part(zx(m), y, x, h)
        arrive_z(a_z[h], m, block)
        a_y[m, h] = send(block, y_dev)
        across(m, 0, h)

    def on_y(m, h):
        a_y[m, h].wait_recv()
        across(m, 1, h)

    def on_n(m, _):
        block = nbuf.at[zx(m), y]
        if m == 0:
            n_z.update(along_z(block))
        else:
            arrive_z(n_z, m, block)
        n_y.append(send(block, y_dev))

    def on_b(m, _):
        block = wb.at[zx(m), y, x, c]
        if m == 0:
            b_z.update(along_z(block))
        else:
            arrive_z(b_z, m, block)

    def line_b(m, _):
        block = wb.at[zx(m), y, x, c]
        b_y.append(send(block, y_dev))
        b_x.append(send(block, x_dev))

    def on_x(first, last):
        for k in range(first, last):
            m, flip, h = x_order[k]
            a_x[k].wait_recv()
            if h == 1:
                yy = yp if flip else y
                a_c.append(send(wa.at[zx(m), yy, xp, c], c_dev))
                settle(zx(m), yy, xp, c)

    def on_small(k, _):
        small_sum(sm_src, sm_rcv, k, small[k])
        if k < 2:
            small.append(push(sm_src.at[k + 1], sm_rcv.at[k + 1], (y_dev, x_dev)[k]))
        else:
            sm_tile[z] = sm_src[3]
            small.extend(push(sm_src.at[3], sm_tile.at[z], z_dev(m)) for m in range(1, Z))

    settle(z, y, x, c)
    steps = {"z": on_z, "y": on_y, "n": on_n, "b": on_b, "l": line_b, "x": on_x, "s": on_small}
    for step in geo["gather"]:
        kind, (m, h) = step[0], ([int(v) for v in step[1:].split(".")] + [0])[:2]
        if kind in "xs" or m < Z:
            steps[kind](m, h)
    on_x(0, len(x_order))
    for copy in n_y:
        copy.wait_recv()
    loads[9].wait()
    for copy in a_c:
        copy.wait_recv()
    for step in geo["late"]:
        kind, m = step[0], int(step[1:])
        if m < Z:
            steps[kind](m, 0)
    for zz in range(Z):
        for yy in range(Y):
            for xx in range(X):
                settle(zz, yy, xx, cp)
    for copy in small[3:]:
        copy.wait_recv()
    for zz in range(Z):
        par_all[:, zz * wide : (zz + 1) * wide] = sm_tile[zz]

    nodes_all = nbuf[...].reshape(N, D)
    proj[0:N, :] = mm(nodes_all, w1[D : 2 * D, :]).astype(bf16)
    proj[N : 2 * N, :] = mm(nodes_all, w1[2 * D : 3 * D, :]).astype(bf16)
    count = count_in[0, 0]
    row_id = lax.broadcasted_iota(jnp.int32, (R, D), 0)

    def edge_forward(i):
        at = slice(i * R, (i + 1) * R)
        live = row_id < count - i * R
        own = edges[at, :]
        pre = mm(own, w1[0:D, :]) + mm(pick[at, :], proj[...]) + par_all[0:1, :]
        sig = jax.nn.sigmoid(pre)
        act = (pre * sig).astype(bf16)
        hidden[at, :] = act
        slope[at, :] = sig * (1.0 + pre * (1.0 - sig))
        out = mm(act, w2[...]) + par_all[1:2, :]
        norm, inv = norm_stats(out)
        normed[at, :] = norm
        rstd[at, :] = jnp.broadcast_to(inv, (R, 128))
        new = own.astype(f32) + jnp.where(live, norm * par_all[2:3, :] + par_all[3:4, :], 0.0)
        enew[at, :] = new.astype(bf16)
        term[at, :] = jnp.where(live, new, 0.0).astype(bf16)

    edge_forward(0)
    for step in geo["mid"]:
        kind, m = step[0], int(step[1:])
        if m < Z:
            steps[kind](m, 0)
    edge_forward(1)

    order = tuple(reversed(range(Z)))

    class NodeSum:
        def __init__(self, pb, yr, zs, zr):
            self.pb, self.yr, self.zs, self.zr = pb, yr, zs, zr
            self.y, self.z = {}, {}

        def put(self, m, values):
            pf[zx(m)] = values.reshape(Y, 2, n // 2, D)
            self.pb[zx(m)] = values.astype(bf16).reshape(Y, 2, n // 2, D)
            for h in range(2):
                self.y[m, h] = push(self.pb.at[zx(m), yp, h], self.yr.at[m, h], y_dev)

        def over(self, m, h, low):
            self.zs[m - 1, h] = pf[zx(m), y, h].astype(bf16)
            self.z[m, h] = push(self.zs.at[m - 1, h], self.zr.at[m - 1, h], z_dev(low))

        def turn(self, m, h):
            self.y[m, h].wait_recv()
            pf[zx(m), y, h] = pf[zx(m), y, h] + self.yr[m, h].astype(f32)
            if m % 2:
                self.over(m, h, 1)

        def merge(self, m, h):
            self.z[m + 1, h].wait_recv()
            pf[zx(m), y, h] = pf[zx(m), y, h] + self.zr[m, h].astype(f32)
            if m:
                self.over(m, h, 2)

        def total(self):
            sums = []
            for h in range(2):
                part = pf[z, y, h]
                for m in range(2, Z, 2):
                    self.z[m, h].wait_recv()
                    part = part + self.zr[m - 1, h].astype(f32)
                sums.append(part)
            return jnp.concatenate(sums, axis=0)

    agg_sum = NodeSum(pb_a, yr_a, zs_a, zr_a)
    b_c, early = [], {}

    def step_p(m, _):
        first_row = pl.multiple_of(N + zx(m) * (Y * n), Y * n)
        agg_sum.put(m, mm(spread[pl.ds(first_row, Y * n), :], term[...]))

    def step_b(k, _):
        if k == 0:
            for copy in b_y:
                copy.wait_recv()
            b_x.append(send(wb.at[:, yp, x, c], x_dev))
            b_c.extend(send(wb.at[:, yy, x, c], c_dev) for yy in (y, yp))
        elif k == 1:
            for copy in b_x[:-1]:
                copy.wait_recv()
            b_c.append(send(wb.at[:, y, xp, c], c_dev))
        elif k == 2:
            b_x[-1].wait_recv()
            b_c.append(send(wb.at[:, yp, xp, c], c_dev))
        else:
            for copy in b_c:
                copy.wait_recv()
            w3[...] = wb[:, :, :, :, 0:r3, :].reshape(w3.shape)
            w4[...] = wb[:, :, :, :, r3 : r3 + r4, :].reshape(w4.shape)
            early["pre"] = mm(nodes_in[...], w3[0:D, :])

    sums_n = {"p": step_p, "b": step_b, "t": agg_sum.turn, "g": agg_sum.merge}
    for step in geo["agg"]:
        kind, (m, h) = step[0], ([int(v) for v in step[1:].split(".")] + [0])[:2]
        if kind == "b" or m < Z:
            sums_n[kind](m, h)
    own_nodes = nodes_in[...]
    agg = agg_sum.total()

    def par(k):
        return par_all[k : k + 1, :]

    agg_low = agg.astype(bf16)
    pre_n = early["pre"] + mm(agg_low, w3[D : 2 * D, :]) + par(4)
    sig_n = jax.nn.sigmoid(pre_n)
    hidden_n = (pre_n * sig_n).astype(bf16)
    out_n = mm(hidden_n, w4[...]) + par(5)
    normed_n, rstd_n = norm_stats(out_n)
    ncot = ncot_in[...].astype(f32)
    d_out_n = norm_back(ncot, normed_n, rstd_n, par(6)).astype(bf16)
    slope_n = sig_n * (1.0 + pre_n * (1.0 - sig_n))
    d_pre_n = (times_t(d_out_n, w4[...]) * slope_n).astype(bf16)
    dbuf[z, y] = times_t(d_pre_n, w3[D : 2 * D, :]).astype(bf16)
    d_z, d_y = {}, []

    def d_part(m, h):
        return dbuf.at[zx(m), y, h * (n // 2) : (h + 1) * (n // 2), :]

    def step_d(m, h):
        block = d_part(m, h)
        if m == 0:
            d_z[h] = along_z(block)
        else:
            arrive_z(d_z[h], m, block)
        d_y.append(send(block, y_dev))

    for h in range(2):
        step_d(0, h)
    class WeightSum:
        def __init__(self, grad, crecv, xs, xrecv, ks, ys, yrecv, zs, zrecv):
            self.grad, self.crecv, self.xs, self.xrecv, self.ks = grad, crecv, xs, xrecv, ks
            self.ys, self.yrecv, self.zs, self.zrecv = ys, yrecv, zs, zrecv

        def put(self, first, values, lane_rows=None, base=0):
            low, r = values.astype(bf16), lane_rows or self.grad.shape[4]
            row = 0
            while row < values.shape[0]:
                k, off = divmod(first + row, r)
                size = min(r - off, values.shape[0] - row)
                at = (k // (Y * X * C), k // (X * C) % Y, k // C % X, k % C)
                self.grad[(*at, slice(base + off, base + off + size))] = low[row : row + size]
                row += size

        def start(self):
            self.c = [
                push(self.grad.at[:, yy, xx, cp], self.crecv.at[k], c_dev)
                for k, (yy, xx) in enumerate(((yp, xp), (y, xp), (yp, x), (y, x)))
            ]

            self.x, self.y, self.z = {}, {}, {}

        def cross_x(self, k):
            self.c[k].wait_recv()
            for m in order:
                part = self.grad[zx(m), (yp, y)[k % 2], (xp, x)[k // 2], c].astype(f32)
                part = part + self.crecv[k, zx(m)].astype(f32)
                if k < 2:
                    self.xs[k, m] = part.astype(bf16)
                    self.x[k, m] = push(self.xs.at[k, m], self.xrecv.at[k, m], x_dev)
                else:
                    self.ks[k - 2, m] = part

        def cross_y(self, m):
            self.x[0, m].wait_recv()
            self.ys[m] = (self.ks[0, m] + self.xrecv[0, m].astype(f32)).astype(bf16)
            self.y[m] = push(self.ys.at[m], self.yrecv.at[m], y_dev)

        def cross_z(self, m):
            self.x[1, m].wait_recv()
            self.y[m].wait_recv()
            part = self.ks[1, m] + self.xrecv[1, m].astype(f32) + self.yrecv[m].astype(f32)
            if m % 2:
                self.over(part, m, 1)
            else:
                self.ks[1, m] = part

        def over(self, part, m, low):
            self.zs[m - 1] = part.astype(bf16)
            self.z[m] = push(self.zs.at[m - 1], self.zrecv.at[m - 1], z_dev(low))

        def merge(self, m):
            self.z[m + 1].wait_recv()
            part = self.ks[1, m] + self.zrecv[m].astype(f32)
            if m:
                self.over(part, m, 2)
            else:
                self.ks[1, 0] = part

        def total(self):
            result = self.ks[1, 0]
            for m in range(2, Z, 2):
                self.z[m].wait_recv()
                result = result + self.zrecv[m - 1].astype(f32)
            return result

    per = len(grad_refs) // 4
    sum1a, sum1b, sum2, sum_n = [WeightSum(*grad_refs[k * per : (k + 1) * per]) for k in range(4)]

    sum_n.put(0, inner(own_nodes, d_pre_n), r3)
    sum_n.put(D, inner(agg_low, d_pre_n), r3)
    sum_n.put(0, inner(hidden_n, d_out_n), r4, r3)
    sum_n.start()
    nnew_out[...] = (own_nodes.astype(f32) + normed_n * par(6) + par(7)).astype(bf16)
    node_part = ncot + times_t(d_pre_n, w3[0:D, :])
    gsm[4:5, :] = jnp.sum(d_pre_n.astype(f32), axis=0, keepdims=True)
    gsm[5:6, :] = jnp.sum(d_out_n.astype(f32), axis=0, keepdims=True)
    gsm[6:7, :] = jnp.sum(ncot * normed_n, axis=0, keepdims=True)
    gsm[7:8, :] = jnp.sum(ncot, axis=0, keepdims=True)
    parts_d = {"d": step_d, "x": lambda k, _: sum_n.cross_x(k)}
    for step in geo["back"]:
        kind, (m, h) = step[0], ([int(v) for v in step[1:].split(".")] + [0])[:2]
        if kind == "x" or m < Z:
            parts_d[kind](m, h)
    loads[10].wait()
    for copy in d_y:
        copy.wait_recv()

    sums[...] = jnp.zeros_like(sums)
    d_all = dbuf[...].reshape(N, D)

    def edge_back(i):
        at = slice(i * R, (i + 1) * R)
        live = row_id < count - i * R
        d_edge = cot[at, :].astype(f32) + jnp.where(live, mm(pick[at, N : 2 * N], d_all), 0.0)
        dedge[at, :] = d_edge
        masked = jnp.where(live, d_edge, 0.0)
        norm = normed[at, :]
        inv = rstd[at, 0:1]
        weighted = masked * norm
        sums[2] += fold_rows(weighted)
        sums[3] += fold_rows(masked)
        d_out = norm_back(masked, norm, inv, par(2)).astype(bf16)
        dout[at, :] = d_out
        sums[1] += fold_rows(d_out.astype(f32))
        d_pre = (times_t(d_out, w2[...]) * slope[at, :]).astype(bf16)
        dpre[at, :] = d_pre
        sums[0] += fold_rows(d_pre.astype(f32))

    edge_back(0)
    for m in order:
        sum_n.cross_y(m)
    edge_back(1)
    edges_all = edges[...]

    def edge_grads(k, into):
        at = slice(k * (D // 2), (k + 1) * (D // 2))
        d_pre = dpre[:, at]
        into.put(0, inner(edges_all, d_pre))
        for half in range(2):
            nodes_at = slice(half * N, (half + 1) * N)
            seg[nodes_at, at] = mm(spread[nodes_at, :], d_pre).astype(bf16)
            into.put((1 + half) * D, inner(nodes_all, seg[nodes_at, at]))
        into.start()

    sums_w = {"a": sum1a, "b": sum1b, "c": sum2, "n": sum_n}
    gm = []
    node_sum = NodeSum(pb_n, yr_n, zs_n, zr_n)

    def step_w(which, _):
        if which == "c":
            sum2.put(0, inner(hidden[...], dout[...]))
            sum2.start()
        else:
            edge_grads("ab".index(which), sums_w[which])

    def step_t(which, _):
        if which == "N":
            ngrad_out[...] = (node_part + node_sum.total()).astype(bf16)
            return
        result = sums_w[which].total()
        if which == "n":
            g3_out[...] = result[0:r3]
            g4_out[...] = result[r3 : r3 + r4]
        elif which == "c":
            g2_out[...] = result
        else:
            k = "ab".index(which)
            g1_out[:, k * (D // 2) : (k + 1) * (D // 2)] = result

    def step_n(which, k):
        if which == "s":
            total = times_t(seg[0:N, :], w1[D : 2 * D, :])
            total = total + times_t(seg[N : 2 * N, :], w1[2 * D : 3 * D, :])
            pf[...] = total.reshape(pf.shape)
            pb_n[...] = total.astype(bf16).reshape(pf.shape)
            for m in order:
                for h in range(2):
                    node_sum.y[m, h] = push(pb_n.at[zx(m), yp, h], yr_n.at[m, h], y_dev)
        elif which in "gh":
            node_sum.turn(k, "gh".index(which))
        else:
            node_sum.merge(k, "mo".index(which))

    def step_e(*_):
        for i in range(2):
            at = slice(i * R, (i + 1) * R)
            egrad[at, :] = (dedge[at, :] + times_t(dpre[at, :], w1[0:D, :])).astype(bf16)

    def step_g(_, k):
        if k == 0:
            for row in range(4):
                gsm[row : row + 1, :] = jnp.sum(sums[row], axis=0, keepdims=True)
            for zz in range(Z):
                gm_tile[zz] = gsm[:, zz * wide : (zz + 1) * wide]
            gm.extend(
                push(gm_tile.at[zx(m)], gm_tile.at[Z + m - 1], z_dev(m)) for m in range(1, Z)
            )
        elif k == 1:
            tile = gm_tile[z]
            for m in range(1, Z):
                gm[m - 1].wait_recv()
                tile = tile + gm_tile[Z + m - 1]
            gm_src[0] = tile
            gm.append(push(gm_src.at[0], gm_rcv.at[0], y_dev))
        else:
            small_sum(gm_src, gm_rcv, k - 2, gm[-1])
            if k < 4:
                gm.append(push(gm_src.at[k - 1], gm_rcv.at[k - 1], (x_dev, c_dev)[k - 2]))
                return
            take = (
                lax.broadcasted_iota(jnp.int32, (wide, ws), 0)
                == lax.broadcasted_iota(jnp.int32, (wide, ws), 1) + first
            )
            gs_out[...] = jnp.dot(
                gm_src[3],
                jnp.where(take, 1.0, 0.0),
                preferred_element_type=f32,
                precision=lax.Precision.HIGHEST,
            )

    tail = {
        "w": step_w,
        "x": lambda which, k: sums_w[which].cross_x(k),
        "y": lambda which, m: sums_w[which].cross_y(m),
        "z": lambda which, m: sums_w[which].cross_z(m),
        "m": lambda which, m: sums_w[which].merge(m),
        "t": step_t,
        "n": step_n,
        "e": step_e,
        "g": step_g,
    }
    for step in geo["tail"]:
        kind, which, k = step[0], step[1:2], int(step[2:] or 0)
        if kind not in "yzmn" or k < Z:
            tail[kind](which, k)
    for copy in started:
        copy.wait_send()


def update_kernel(*refs):
    passed, weights, firsts, seconds = refs[0:9], refs[9:14], refs[14:19], refs[19:24]
    outs, new_v, new_w, smalls, sem = refs[24:43], refs[43:47], refs[47:51], refs[51:54], refs[54]
    enew, egrad, nnew, ngrad, *grads = passed
    copies = []

    def put(src, dst):
        copies.append(pltpu.make_async_copy(src, dst, sem.at[len(copies)]))
        copies[-1].start()

    for src, dst in zip((weights[4], firsts[4], seconds[4]), smalls):
        put(src, dst)
    for src, dst in zip((enew, nnew, egrad, ngrad), outs[:4]):
        put(src, dst.at[0])
    for k in range(4):
        put(grads[k], outs[4 + k])
    outs[8][...] = grads[4][...]
    for k in range(4):
        new_w[k][...], new_v[k][...] = adamw(
            weights[k][...], grads[k][...], firsts[k][...], seconds[k][...], 0.03
        )
        put(new_v[k], outs[9 + k])
        put(new_w[k], outs[14 + k])
    for copy in copies[:3]:
        copy.wait()
    small, first, second = (ref[...] for ref in smalls)
    outs[18][...], outs[13][...] = adamw(small, grads[4][...], first, second, 0.2)
    for copy in copies[3:]:
        copy.wait()


def on_device(n_edge, n_grp, *args):
    (
        edge_lat,
        node_lat,
        edge_cot,
        node_cot,
        senders,
        receivers,
        edge_count,
        *state,
    ) = args
    weights, firsts, seconds = state[0:5], state[5:10], state[10:15]
    rows, D = edge_lat.shape[1:]
    n = node_lat.shape[1]
    N = n * n_edge
    n_dev = n_edge * n_grp
    shards = [w.shape[0] for w in weights[:4]]
    fits = (
        n_edge % 2 == 0
        and n_grp == 4
        and all(r % 16 == 0 for r in shards)
        and n_edge // 2 in (2, 4)
        and D % (128 * (n_edge // 2)) == 0
        and D % 256 == 0
        and N % 128 == 0
        and n % 32 == 0
        and (shards[0] + shards[1]) % 32 == 0
        and rows % 256 == 0
        and rows * N <= 1024 * 1024
    )
    if not fits:
        return native(*args)
    Z, Y, X, C = n_edge // 2, 2, 2, 2
    n_sem = 240

    def vm(shape, dtype=bf16):
        return pltpu.VMEM(shape, dtype)

    ins = [edge_lat[0], edge_cot[0], node_lat[0], node_cot[0], senders, receivers, edge_count, *weights]
    scratch = [
        *[vm(a.shape, a.dtype) for a in ins if a is not edge_count],
        vm((Z, Y, n, D)),
        vm((Z, Y, n, D)),
        *[vm((r * n_dev, D)) for r in shards],
        vm((Z, Y, X, C, shards[0] + shards[1], D)),
        vm((Z, Y, X, C, shards[2] + shards[3], D)),
        vm((rows, 2 * N)),
        vm((2 * N, rows)),
        vm((2 * N, D)),
        vm((rows, D), f32),
        vm((rows, D)),
        vm((rows, D), f32),
        vm((rows, 128), f32),
        vm((rows, D)),
        vm((rows, D), f32),
        vm((rows, D)),
        vm((rows, D)),
        vm((4, 8, D), f32),
        vm((Z, Y, 2, n // 2, D), f32),
        vm((Z, Y, 2, n // 2, D)),
        vm((Z, Y, 2, n // 2, D)),
        vm((Z, 2, n // 2, D)),
        vm((Z, 2, n // 2, D)),
        *[vm((Z - 1, 2, n // 2, D))] * 4,
        vm((2 * N, D)),
        vm((4, 8, D // Z), f32),
        vm((3, 8, D // Z), f32),
        vm((Z, 8, D // Z), f32),
        vm((8, D), f32),
        vm((4, 8, D // Z), f32),
        vm((3, 8, D // Z), f32),
        vm((2 * Z - 1, 8, D // Z), f32),
        vm((8, D), f32),
    ]
    blocks = ((shards[0], D // 2), (shards[0], D // 2), (shards[1], D), (shards[2] + shards[3], D))
    for r, cols in blocks:
        scratch += [
            vm((Z, Y, X, C, r, cols)),
            vm((4, Z, r, cols)),
            vm((2, Z, r, cols)),
            vm((2, Z, r, cols)),
            vm((2, Z, r, cols), f32),
            vm((Z, r, cols)),
            vm((Z, r, cols)),
            vm((Z - 1, r, cols)),
            vm((Z - 1, r, cols)),
        ]
    scratch += [
        pltpu.SemaphoreType.DMA((len(ins),)),
        pltpu.SemaphoreType.DMA((n_sem,)),
        pltpu.SemaphoreType.DMA((n_sem,)),
    ]
    hbm = pl.BlockSpec(memory_space=pltpu.HBM)
    anyspace = pl.BlockSpec(memory_space=pl.ANY)
    vmem = pl.BlockSpec(memory_space=pltpu.VMEM)
    results = pl.pallas_call(
        functools.partial(layer_kernel, dict(GEO, dims=(Z, Y, X, C), n_sem=n_sem)),
        out_shape=[vm((rows, D))] * 2 + [vm((n, D))] * 2 + [vm(w.shape, f32) for w in weights],
        in_specs=[hbm] * 6 + [pl.BlockSpec(memory_space=pltpu.SMEM)] + [hbm] * 5,
        out_specs=[vmem] * 9,
        scratch_shapes=scratch,
        compiler_params=pltpu.CompilerParams(
            collective_id=0, has_side_effects=True, vmem_limit_bytes=52 * 1024 * 1024
        ),
        name="layer",
    )(*ins)
    sds = jax.ShapeDtypeStruct
    state_out = [sds(w.shape, f32) for w in weights]
    kept = [vm(w.shape, f32) for w in weights[:4]]
    return tuple(
        pl.pallas_call(
            update_kernel,
            out_shape=[
                sds((1, rows, D), bf16),
                sds((1, n, D), bf16),
                sds((1, rows, D), bf16),
                sds((1, n, D), bf16),
                *state_out,
                *state_out,
                *state_out,
            ],
            in_specs=[vmem] * 9 + ([vmem] * 4 + [hbm]) * 3,
            out_specs=[anyspace] * 4 + ([anyspace] * 4 + [vmem]) * 3,
            scratch_shapes=[
                *kept,
                *kept,
                *[vm(weights[4].shape, f32)] * 3,
                pltpu.SemaphoreType.DMA((19,)),
            ],
            compiler_params=pltpu.CompilerParams(vmem_limit_bytes=8 * 1024 * 1024),
            name="update",
        )(*results, *weights, *firsts, *seconds)
    )


def solution(mesh):
    in_specs = (
        P("grp", "edge", None),
        P("grp", "edge", None),
        P("grp", "edge", None),
        P("grp", "edge", None),
        P("grp", "edge"),
        P("grp", "edge"),
        P("grp", "edge"),
        P(("edge", "grp"), None),
        P(("edge", "grp"), None),
        P(("edge", "grp"), None),
        P(("edge", "grp"), None),
        P(None, ("edge", "grp")),
        P(("edge", "grp"), None),
        P(("edge", "grp"), None),
        P(("edge", "grp"), None),
        P(("edge", "grp"), None),
        P(None, ("edge", "grp")),
        P(("edge", "grp"), None),
        P(("edge", "grp"), None),
        P(("edge", "grp"), None),
        P(("edge", "grp"), None),
        P(None, ("edge", "grp")),
    )
    out_specs = (
        P("grp", "edge", None),
        P("grp", "edge", None),
        P("grp", "edge", None),
        P("grp", "edge", None),
        P(("edge", "grp"), None),
        P(("edge", "grp"), None),
        P(("edge", "grp"), None),
        P(("edge", "grp"), None),
        P(None, ("edge", "grp")),
        P(("edge", "grp"), None),
        P(("edge", "grp"), None),
        P(("edge", "grp"), None),
        P(("edge", "grp"), None),
        P(None, ("edge", "grp")),
        P(("edge", "grp"), None),
        P(("edge", "grp"), None),
        P(("edge", "grp"), None),
        P(("edge", "grp"), None),
        P(None, ("edge", "grp")),
    )
    return jax.shard_map(
        functools.partial(on_device, mesh.shape["edge"], mesh.shape["grp"]),
        mesh=mesh, in_specs=in_specs, out_specs=out_specs, check_vma=False
    )
```

```python
import functools

import jax
import jax.numpy as jnp
from jax import lax
from jax.experimental import pallas as pl
from jax.experimental.pallas import tpu as pltpu
from jax.sharding import PartitionSpec as P

step_count = 10.0


def inner(left, right):
    return lax.dot_general(
        left, right, (((0,), (0,)), ((), ())), preferred_element_type=jnp.float32
    )


def times_t(left, right):
    return lax.dot_general(
        left, right, (((1,), (1,)), ((), ())), preferred_element_type=jnp.float32
    )


def norm_stats(values):
    mean = jnp.mean(values, axis=-1, keepdims=True)
    centred = values - mean
    var = jnp.mean(centred * centred, axis=-1, keepdims=True)
    rstd = lax.rsqrt(var + 1e-05)
    return (centred * rstd, rstd)


def norm_back(grad_out, normed, rstd, gain):
    scaled = grad_out * gain
    return rstd * (
        scaled
        - jnp.mean(scaled, axis=-1, keepdims=True)
        - normed * jnp.mean(scaled * normed, axis=-1, keepdims=True)
    )


def silu_slope(values):
    sig = jax.nn.sigmoid(values)
    return sig * (1.0 + values * (1.0 - sig))


def adamw(weight, grad, first, second, rate):
    first_new = 0.9 * first + 0.1 * grad
    second_new = 0.999 * second + 0.001 * grad * grad
    mhat = first_new / (1.0 - 0.9**step_count)
    vhat = second_new / (1.0 - 0.999**step_count)
    return (weight - rate * (mhat / (jnp.sqrt(vhat) + 1e-08) + 0.1 * weight), second_new)


def native(
    edge_lat,
    node_lat,
    edge_cot,
    node_cot,
    senders,
    receivers,
    edge_count,
    w_edge_in,
    w_edge_out,
    w_node_in,
    w_node_out,
    small_params,
    first_edge_in,
    first_edge_out,
    first_node_in,
    first_node_out,
    first_small,
    second_edge_in,
    second_edge_out,
    second_node_in,
    second_node_out,
    second_small,
):
    bf = jnp.bfloat16
    edges = edge_lat[0]
    nodes = node_lat[0]
    send = senders[0]
    recv = receivers[0]
    rows = edges.shape[0]
    width = edges.shape[1]
    maskf = (jnp.arange(rows, dtype=jnp.int32) < edge_count[0, 0]).astype(jnp.float32)[:, None]
    w1e, w2e, w1n, w2n, small = (
        lax.all_gather(w_edge_in.astype(bf), ("edge", "grp"), axis=0, tiled=True),
        lax.all_gather(w_edge_out.astype(bf), ("edge", "grp"), axis=0, tiled=True),
        lax.all_gather(w_node_in.astype(bf), ("edge", "grp"), axis=0, tiled=True),
        lax.all_gather(w_node_out.astype(bf), ("edge", "grp"), axis=0, tiled=True),
        lax.all_gather(small_params.astype(bf), ("edge", "grp"), axis=1, tiled=True),
    )
    params = small.astype(jnp.float32)
    whole = lax.all_gather(nodes, "edge", axis=0, tiled=True)
    node_total = whole.shape[0]
    joined = jnp.concatenate([edges, whole[send], whole[recv]], axis=1)
    pre = jnp.dot(joined, w1e, preferred_element_type=jnp.float32) + params[0]
    hidden = jax.nn.silu(pre).astype(bf)
    out = jnp.dot(hidden, w2e, preferred_element_type=jnp.float32) + params[1]
    normed, rstd = norm_stats(out)
    edge_new = edges.astype(jnp.float32) + maskf * (normed * params[2] + params[3])
    dense = jnp.zeros((node_total, width), jnp.float32).at[recv].add(maskf * edge_new)
    agg = lax.psum_scatter(dense, "edge", scatter_dimension=0, tiled=True)
    node_in = jnp.concatenate([nodes, agg.astype(bf)], axis=1)
    pre_n = jnp.dot(node_in, w1n, preferred_element_type=jnp.float32) + params[4]
    hidden_n = jax.nn.silu(pre_n).astype(bf)
    out_n = jnp.dot(hidden_n, w2n, preferred_element_type=jnp.float32) + params[5]
    normed_n, rstd_n = norm_stats(out_n)
    node_new = nodes.astype(jnp.float32) + normed_n * params[6] + params[7]
    grad_node_out_f = node_cot[0].astype(jnp.float32)
    d_out_n = norm_back(grad_node_out_f, normed_n, rstd_n, params[6]).astype(bf)
    gain_n = jnp.sum(grad_node_out_f * normed_n, axis=0)
    shift_n = jnp.sum(grad_node_out_f, axis=0)
    g_w2n = inner(hidden_n, d_out_n)
    g_b2n = jnp.sum(d_out_n.astype(jnp.float32), axis=0)
    d_pre_n = (times_t(d_out_n, w2n) * silu_slope(pre_n)).astype(bf)
    g_w1n = inner(node_in, d_pre_n)
    g_b1n = jnp.sum(d_pre_n.astype(jnp.float32), axis=0)
    d_node_in = times_t(d_pre_n, w1n)
    node_part = grad_node_out_f + d_node_in[:, :width]
    d_agg = d_node_in[:, width:].astype(bf)
    agg_rows = lax.all_gather(d_agg, "edge", axis=0, tiled=True)
    d_edge = edge_cot[0].astype(jnp.float32) + maskf * agg_rows[recv].astype(jnp.float32)
    masked = maskf * d_edge
    d_out = norm_back(masked, normed, rstd, params[2]).astype(bf)
    gain_e = jnp.sum(masked * normed, axis=0)
    shift_e = jnp.sum(masked, axis=0)
    g_w2e = inner(hidden, d_out)
    g_b2e = jnp.sum(d_out.astype(jnp.float32), axis=0)
    d_pre = (times_t(d_out, w2e) * silu_slope(pre)).astype(bf)
    g_w1e = inner(joined, d_pre)
    g_b1e = jnp.sum(d_pre.astype(jnp.float32), axis=0)
    d_joined = times_t(d_pre, w1e)
    edge_grad = (d_edge + d_joined[:, :width]).astype(bf)
    dense_grad = jnp.zeros((node_total, width), jnp.float32)
    dense_grad = (
        dense_grad.at[send]
        .add(d_joined[:, width : 2 * width])
        .at[recv]
        .add(d_joined[:, 2 * width :])
    )
    node_sum = lax.psum_scatter(dense_grad, "edge", scatter_dimension=0, tiled=True)
    node_grad = (node_part + node_sum).astype(bf)
    g_small = jnp.stack([g_b1e, g_b2e, gain_e, shift_e, g_b1n, g_b2n, gain_n, shift_n])
    grads = (
        lax.psum_scatter(g_w1e, ("edge", "grp"), scatter_dimension=0, tiled=True),
        lax.psum_scatter(g_w2e, ("edge", "grp"), scatter_dimension=0, tiled=True),
        lax.psum_scatter(g_w1n, ("edge", "grp"), scatter_dimension=0, tiled=True),
        lax.psum_scatter(g_w2n, ("edge", "grp"), scatter_dimension=0, tiled=True),
        lax.psum_scatter(g_small, ("edge", "grp"), scatter_dimension=1, tiled=True),
    )
    weights = (w_edge_in, w_edge_out, w_node_in, w_node_out, small_params)
    firsts = (first_edge_in, first_edge_out, first_node_in, first_node_out, first_small)
    seconds = (second_edge_in, second_edge_out, second_node_in, second_node_out, second_small)
    rates = (0.03, 0.03, 0.03, 0.03, 0.2)
    updated = [
        adamw(w, g, m, v, r) for w, g, m, v, r in zip(weights, grads, firsts, seconds, rates)
    ]
    return (
        edge_new.astype(bf)[None],
        node_new.astype(bf)[None],
        edge_grad[None],
        node_grad[None],
        grads[0],
        grads[1],
        grads[2],
        grads[3],
        grads[4],
        updated[0][1],
        updated[1][1],
        updated[2][1],
        updated[3][1],
        updated[4][1],
        updated[0][0],
        updated[1][0],
        updated[2][0],
        updated[3][0],
        updated[4][0],
    )


bf16 = jnp.bfloat16
f32 = jnp.float32
MESH = pl.DeviceIdType.MESH


def mm(left, right):
    return jnp.dot(left, right, preferred_element_type=f32)


def fold_rows(values):
    count, width = values.shape
    return jnp.sum(values.reshape(count // 8, 8, width), axis=0)


GEO = {
    "x_first": (True, True, False, True),
    "diagonal": (),
    "bits_a": True,
    "bits_n": True,
    "bits_b": True,
    "bits_d": True,
    "bits_agg": True,
    "bits_node": False,
    "bits_w": False,
    "gather": (
        200, 700, 100, 10, 101, 20, 11, 21, 120, 110, 600, 30, 111, 31, 610, 220, 121, 210, 130,
        300, 131, 230, 620
    ),
    "late": (
        310, 320, 400, 410, 420
    ),
    "mid": (
        330, 430
    ),
    "agg": (
        30, 300, 20, 10, 0, 130, 131, 121, 310, 120, 110, 220, 221, 320, 100, 111, 101, 330, 200,
        201
    ),
    "back": (
        100, 110, 10, 20, 21, 11, 30, 120, 130, 31
    ),
    "tail": (
        0, 8050, 10, 3032, 5060, 3033, 1000, 1012, 1010, 1002, 1001, 3030, 4032, 5073, 20, 5083,
        2002, 1011, 1022, 5082, 1013, 1003, 3031, 2003, 5081, 1020, 2012, 8051, 2001, 5072, 3003,
        2013, 4030, 5070, 5092, 2023, 1023, 3002, 2011, 5080, 1021, 2020, 2021, 2000, 2010, 2022,
        5071, 3012, 3013, 5090, 4002, 3001, 3011, 5100, 7050, 3023, 8052, 3022, 4012, 3021, 5102,
        3020, 8053, 8054, 3010, 6040, 4010, 3000, 6030, 4000, 6000, 4022, 6010, 4020, 6020
    ),
}


def decode(step, unit):
    return step // (10 * unit), step // 10 % unit, step % 10


def layer_kernel(geo, *refs):
    Z, Y, X, C = geo["dims"]
    n_sem = geo["n_sem"]
    (
        edges_hbm,
        cot_hbm,
        nodes_hbm,
        ncot_hbm,
        send_hbm,
        recv_hbm,
        count_in,
        w1_hbm,
        w2_hbm,
        w3_hbm,
        w4_hbm,
        small_hbm,
        *rest,
    ) = refs
    moments_hbm, rest = rest[:10], rest[10:]
    enew, nnew_out, egrad, ngrad_out, *rest = rest
    grads_out, seconds_out, weights_out, rest = rest[0:5], rest[5:10], rest[10:15], rest[15:]
    g1_out, g2_out, g3_out, g4_out, gs_out = grads_out
    moments_in, rest = rest[:10], rest[10:]
    (
        edges,
        cot,
        nodes_in,
        ncot_in,
        send_in,
        recv_in,
        w1_in,
        w2_in,
        w3_in,
        w4_in,
        small_in,
        nbuf,
        dbuf,
        w1,
        w2,
        w3,
        w4,
        wa,
        wb,
        pick,
        spread,
        proj,
        slope,
        hidden,
        normed,
        rstd,
        term,
        dedge,
        dout,
        dpre,
        sums,
        pf,
        pb_a,
        pb_n,
        yr_a,
        yr_n,
        zs_a,
        zs_n,
        zr_a,
        zr_n,
        seg,
        sm_src,
        sm_rcv,
        sm_tile,
        par_all,
        gm_src,
        gm_rcv,
        gm_tile,
        gsm,
        *grad_refs,
    ) = rest
    local_sem, ssem, rsem = grad_refs[-3:]
    grad_refs = grad_refs[:-3]
    rows, D = edges.shape
    n = nodes_in.shape[0]
    N = Z * Y * n
    R = rows // 2

    e_id = lax.axis_index("edge")
    g_id = lax.axis_index("grp")
    z = e_id // Y
    y = e_id % Y
    x = g_id // C
    c = g_id % C
    yp, xp, cp = 1 - y, 1 - x, 1 - c
    me = e_id * (X * C) + g_id
    y_dev = (z * Y + yp, g_id)
    x_dev = (e_id, xp * C + c)
    c_dev = (e_id, x * C + cp)
    xy_dev = (z * Y + yp, xp * C + c)

    def zx(m):
        place = z
        for j in range(m.bit_length()):
            if m >> j & 1:
                place = place + (1 << j) - (2 << j) * (z // (1 << j) % 2)
        return place

    def z_dev(m):
        return (zx(m) * Y + y, g_id)

    started = []

    def push(src, dst, dev):
        k = len(started)
        assert k < n_sem
        copy = pltpu.make_async_remote_copy(
            src_ref=src,
            dst_ref=dst,
            send_sem=ssem.at[k],
            recv_sem=rsem.at[k],
            device_id=dev,
            device_id_type=MESH,
        )
        copy.start()
        started.append(copy)
        return copy

    barrier = pltpu.get_barrier_semaphore()
    peers = [z_dev(m) for m in range(1, Z)] + [y_dev, x_dev, c_dev, xy_dev]
    for dev in peers:
        pl.semaphore_signal(barrier, inc=1, device_id=dev, device_id_type=MESH)
    loads = [
        (w1_hbm, w1_in),
        (w2_hbm, w2_in),
        (w3_hbm, w3_in),
        (w4_hbm, w4_in),
        (small_hbm, small_in),
        (nodes_hbm, nodes_in),
        (send_hbm, send_in),
        (recv_hbm, recv_in),
        (ncot_hbm, ncot_in),
        (edges_hbm, edges),
        (cot_hbm, cot),
        *zip(moments_hbm, moments_in),
    ]
    loads = [pltpu.make_async_copy(*pair, local_sem.at[k]) for k, pair in enumerate(loads)]
    for load in loads:
        load.start()
    for load in loads[0:6]:
        load.wait()
    r1, r2, r3, r4 = (own.shape[0] for own in (w1_in, w2_in, w3_in, w4_in))
    ra = r1 + r2
    wa[z, y, x, c, 0:r1, :] = w1_in[...].astype(bf16)
    wa[z, y, x, c, r1:ra, :] = w2_in[...].astype(bf16)
    wb[z, y, x, c, 0:r3, :] = w3_in[...].astype(bf16)
    wb[z, y, x, c, r3 : r3 + r4, :] = w4_in[...].astype(bf16)
    nbuf[z, y] = nodes_in[...]
    ws = small_in.shape[1]
    wide = ws * Y * X * C
    first = me % (Y * X * C) * ws
    place = (
        lax.broadcasted_iota(jnp.int32, (ws, wide), 1)
        == lax.broadcasted_iota(jnp.int32, (ws, wide), 0) + first
    )
    sm_src[0] = mm(small_in[...].astype(bf16), jnp.where(place, 1.0, 0.0).astype(bf16))

    def update(k):
        weight = (w1_in, w2_in, w3_in, w4_in, small_in)[k]
        weights_out[k][...], seconds_out[k][...] = adamw(
            weight[...],
            grads_out[k][...],
            moments_in[k][...],
            moments_in[5 + k][...],
            0.2 if k == 4 else 0.03,
        )

    pl.semaphore_wait(barrier, len(peers))

    def along_z(own, by_bits):
        to = [1 << j for j in range((Z - 1).bit_length())] if by_bits else range(1, Z)
        return {m: push(own, own, z_dev(m)) for m in reversed(to)}

    def arrive_z(copies, m, block):
        copies[m].wait_recv()
        j = 0 if len(copies) < Z - 1 else Z
        while not m >> j & 1 and j < Z:
            copies[m | 1 << j] = push(block, block, z_dev(1 << j))
            j += 1

    halves = ra // 2

    def part(zz, yy, xx, h):
        return wa.at[zz, yy, xx, c, h * halves : (h + 1) * halves, :]

    def send(block, dev):
        return push(block, block, dev)

    def settle(zz, yy, xx, cc):
        k = ((zz * Y + yy) * X + xx) * C + cc
        w1[pl.ds(pl.multiple_of(k * r1, 16), r1), :] = wa[zz, yy, xx, cc, 0:r1, :]
        w2[pl.ds(pl.multiple_of(k * r2, 16), r2), :] = wa[zz, yy, xx, cc, r1:ra, :]

    def small_sum(src, rcv, stage, copy):
        copy.wait_recv()
        src[stage + 1] = src[stage] + rcv[stage]

    small = [push(sm_src.at[0], sm_rcv.at[0], c_dev)]
    a_z, a_y, a_x, a_c, x_order = ({}, {}), {}, [], [], []
    n_z, n_y, b_z, b_y, b_x = {}, [], {}, [], []
    for h in range(2):
        own = part(z, y, x, h)
        a_z[h].update(along_z(own, geo["bits_a"]))
        a_y[0, h] = send(own, y_dev)
        a_x.append(send(own, x_dev))
        x_order.append((0, 0, h))
    a_c.append(send(wa.at[z, y, x, c], c_dev))

    def across(m, flip, h):
        yy = yp if flip else y
        straight = m in geo["diagonal"]
        if not (flip and straight):
            a_x.append(send(part(zx(m), yy, x, h), x_dev))
            x_order.append((m, flip, h))
        if straight and not flip:
            a_x.append(send(part(zx(m), yy, x, h), xy_dev))
            x_order.append((m, 1, h))
        if h == 1:
            a_c.append(send(wa.at[zx(m), yy, x, c], c_dev))
            settle(zx(m), yy, x, c)

    def on_z(m, h):
        block = part(zx(m), y, x, h)
        arrive_z(a_z[h], m, block)
        a_y[m, h] = send(block, y_dev)
        across(m, 0, h)

    def on_y(m, h):
        a_y[m, h].wait_recv()
        across(m, 1, h)

    def on_n(m, _):
        block = nbuf.at[zx(m), y]
        if m == 0:
            n_z.update(along_z(block, geo["bits_n"]))
        else:
            arrive_z(n_z, m, block)
        n_y.append(send(block, y_dev))

    def on_b(m, _):
        block = wb.at[zx(m), y, x, c]
        if m == 0:
            b_z.update(along_z(block, geo["bits_b"]))
        else:
            arrive_z(b_z, m, block)

    def line_b(m, _):
        block = wb.at[zx(m), y, x, c]
        b_y.append(send(block, y_dev))
        b_x.append(send(block, x_dev))

    def on_x(first, last):
        for k in range(first, last):
            m, flip, h = x_order[k]
            a_x[k].wait_recv()
            if h == 1:
                yy = yp if flip else y
                a_c.append(send(wa.at[zx(m), yy, xp, c], c_dev))
                settle(zx(m), yy, xp, c)

    def on_small(k, _):
        small_sum(sm_src, sm_rcv, k, small[k])
        if k < 2:
            small.append(push(sm_src.at[k + 1], sm_rcv.at[k + 1], (y_dev, x_dev)[k]))
        else:
            sm_tile[z] = sm_src[3]
            small.extend(push(sm_src.at[3], sm_tile.at[z], z_dev(m)) for m in range(1, Z))

    settle(z, y, x, c)
    def on_hot(*_):
        for load in loads[6:9]:
            load.wait()
        lane = lax.broadcasted_iota(jnp.int32, (128, N), 1)
        sub = lax.broadcasted_iota(jnp.int32, (N, 128), 0)

        @pl.loop(0, rows // 128)
        def _(k):
            at = pl.ds(pl.multiple_of(k * 128, 128), 128)
            for half, ids in enumerate((send_in, recv_in)):
                row = jnp.broadcast_to(ids[0:1, at], (128, 128))
                col = jnp.tile(row.T, (1, N // 128))
                pick[at, half * N : (half + 1) * N] = jnp.where(lane == col, 1.0, 0.0).astype(bf16)
                flat = jnp.broadcast_to(ids[0:1, at], (N, 128))
                spread[half * N : (half + 1) * N, at] = jnp.where(sub == flat, 1.0, 0.0).astype(bf16)

    steps = (on_z, on_y, on_n, on_b, line_b, on_x, on_small, on_hot)

    def gather(name):
        for step in geo[name]:
            kind, m, h = decode(step, 10)
            if kind > 5 or m < Z:
                steps[kind](m, h)

    gather("gather")
    on_x(0, len(x_order))
    for copy in n_y:
        copy.wait_recv()
    loads[9].wait()
    for copy in a_c:
        copy.wait_recv()
    gather("late")
    for zz in range(Z):
        for yy in range(Y):
            for xx in range(X):
                settle(zz, yy, xx, cp)
    for copy in small[3:]:
        copy.wait_recv()
    for zz in range(Z):
        par_all[:, zz * wide : (zz + 1) * wide] = sm_tile[zz]

    nodes_all = nbuf[...].reshape(N, D)
    proj[0:N, :] = mm(nodes_all, w1[D : 2 * D, :]).astype(bf16)
    proj[N : 2 * N, :] = mm(nodes_all, w1[2 * D : 3 * D, :]).astype(bf16)
    count = count_in[0, 0]
    row_id = lax.broadcasted_iota(jnp.int32, (R, D), 0)

    def edge_forward(i):
        at = slice(i * R, (i + 1) * R)
        live = row_id < count - i * R
        own = edges[at, :]
        pre = mm(own, w1[0:D, :]) + mm(pick[at, :], proj[...]) + par_all[0:1, :]
        sig = jax.nn.sigmoid(pre)
        act = (pre * sig).astype(bf16)
        hidden[at, :] = act
        slope[at, :] = sig * (1.0 + pre * (1.0 - sig))
        out = mm(act, w2[...]) + par_all[1:2, :]
        norm, inv = norm_stats(out)
        normed[at, :] = norm
        rstd[at, :] = jnp.broadcast_to(inv, (R, 128))
        new = own.astype(f32) + jnp.where(live, norm * par_all[2:3, :] + par_all[3:4, :], 0.0)
        enew[at, :] = new.astype(bf16)
        term[at, :] = jnp.where(live, new, 0.0).astype(bf16)

    edge_forward(0)
    gather("mid")
    edge_forward(1)

    order = tuple(reversed(range(Z)))

    class NodeSum:
        def __init__(self, by_bits, pb, yr, zs, zr):
            self.by_bits = by_bits
            self.pb, self.yr, self.zs, self.zr = pb, yr, zs, zr
            self.y, self.z = {}, {}

        def put(self, m, values):
            pf[zx(m)] = values.reshape(Y, 2, n // 2, D)
            self.pb[zx(m)] = values.astype(bf16).reshape(Y, 2, n // 2, D)
            for h in range(2):
                self.y[m, h] = push(self.pb.at[zx(m), yp, h], self.yr.at[m, h], y_dev)

        def over(self, m, h, low):
            self.zs[m - 1, h] = pf[zx(m), y, h].astype(bf16)
            self.z[m, h] = push(self.zs.at[m - 1, h], self.zr.at[m - 1, h], z_dev(low))

        def turn(self, m, h):
            self.y[m, h].wait_recv()
            pf[zx(m), y, h] = pf[zx(m), y, h] + self.yr[m, h].astype(f32)
            if not self.by_bits and m:
                self.over(m, h, m)
            elif m % 2:
                self.over(m, h, 1)

        def merge(self, m, h):
            if not self.by_bits:
                return
            self.z[m + 1, h].wait_recv()
            pf[zx(m), y, h] = pf[zx(m), y, h] + self.zr[m, h].astype(f32)
            if m:
                self.over(m, h, 2)

        def total(self):
            sums = []
            for h in range(2):
                part = pf[z, y, h]
                for m in range(2, Z, 2) if self.by_bits else range(1, Z):
                    self.z[m, h].wait_recv()
                    part = part + self.zr[m - 1, h].astype(f32)
                sums.append(part)
            return jnp.concatenate(sums, axis=0)

    agg_sum = NodeSum(geo["bits_agg"], pb_a, yr_a, zs_a, zr_a)
    b_c, early = [], {}

    def step_p(m, _):
        first_row = pl.multiple_of(N + zx(m) * (Y * n), Y * n)
        agg_sum.put(m, mm(spread[pl.ds(first_row, Y * n), :], term[...]))

    def step_b(k, _):
        if k == 0:
            for copy in b_y:
                copy.wait_recv()
            b_x.append(send(wb.at[:, yp, x, c], x_dev))
            b_c.extend(send(wb.at[:, yy, x, c], c_dev) for yy in (y, yp))
        elif k == 1:
            for copy in b_x[:-1]:
                copy.wait_recv()
            b_c.append(send(wb.at[:, y, xp, c], c_dev))
        elif k == 2:
            b_x[-1].wait_recv()
            b_c.append(send(wb.at[:, yp, xp, c], c_dev))
        else:
            for copy in b_c:
                copy.wait_recv()
            w3[...] = wb[:, :, :, :, 0:r3, :].reshape(w3.shape)
            w4[...] = wb[:, :, :, :, r3 : r3 + r4, :].reshape(w4.shape)
            early["pre"] = mm(nodes_in[...], w3[0:D, :])

    for step in geo["agg"]:
        kind, m, h = decode(step, 10)
        if kind == 3 or m < Z:
            (step_p, agg_sum.turn, agg_sum.merge, step_b)[kind](m, h)
    own_nodes = nodes_in[...]
    agg = agg_sum.total()

    def par(k):
        return par_all[k : k + 1, :]

    agg_low = agg.astype(bf16)
    pre_n = early["pre"] + mm(agg_low, w3[D : 2 * D, :]) + par(4)
    sig_n = jax.nn.sigmoid(pre_n)
    hidden_n = (pre_n * sig_n).astype(bf16)
    out_n = mm(hidden_n, w4[...]) + par(5)
    normed_n, rstd_n = norm_stats(out_n)
    ncot = ncot_in[...].astype(f32)
    d_out_n = norm_back(ncot, normed_n, rstd_n, par(6)).astype(bf16)
    slope_n = sig_n * (1.0 + pre_n * (1.0 - sig_n))
    d_pre_n = (times_t(d_out_n, w4[...]) * slope_n).astype(bf16)
    dbuf[z, y] = times_t(d_pre_n, w3[D : 2 * D, :]).astype(bf16)
    d_z, d_y = {}, []

    def d_part(m, h):
        return dbuf.at[zx(m), y, h * (n // 2) : (h + 1) * (n // 2), :]

    def step_d(m, h):
        block = d_part(m, h)
        if m == 0:
            d_z[h] = along_z(block, geo["bits_d"])
        else:
            arrive_z(d_z[h], m, block)
        d_y.append(send(block, y_dev))

    for h in range(2):
        step_d(0, h)
    class WeightSum:
        def __init__(self, x_first, grad, crecv, xs, xrecv, ks, ys, yrecv, zs, zrecv):
            self.first, self.second = (x_dev, y_dev) if x_first else (y_dev, x_dev)
            side = ((y, xp), (yp, x)) if x_first else ((yp, x), (y, xp))
            self.groups = ((yp, xp), side[0], side[1], (y, x))
            self.grad, self.crecv, self.xs, self.xrecv, self.ks = grad, crecv, xs, xrecv, ks
            self.ys, self.yrecv, self.zs, self.zrecv = ys, yrecv, zs, zrecv

        def put(self, first, values, lane_rows=None, base=0):
            low, r = values.astype(bf16), lane_rows or self.grad.shape[4]
            row = 0
            while row < values.shape[0]:
                k, off = divmod(first + row, r)
                size = min(r - off, values.shape[0] - row)
                at = (k // (Y * X * C), k // (X * C) % Y, k // C % X, k % C)
                self.grad[(*at, slice(base + off, base + off + size))] = low[row : row + size]
                row += size

        def start(self):
            self.c = [
                push(self.grad.at[:, yy, xx, cp], self.crecv.at[k], c_dev)
                for k, (yy, xx) in enumerate(self.groups)
            ]

            self.x, self.y, self.z = {}, {}, {}

        def cross_x(self, k):
            self.c[k].wait_recv()
            for m in order:
                part = self.grad[(zx(m), *self.groups[k], c)].astype(f32)
                part = part + self.crecv[k, zx(m)].astype(f32)
                if k < 2:
                    self.xs[k, m] = part.astype(bf16)
                    self.x[k, m] = push(self.xs.at[k, m], self.xrecv.at[k, m], self.first)
                else:
                    self.ks[k - 2, m] = part

        def cross_y(self, m):
            self.x[0, m].wait_recv()
            self.ys[m] = (self.ks[0, m] + self.xrecv[0, m].astype(f32)).astype(bf16)
            self.y[m] = push(self.ys.at[m], self.yrecv.at[m], self.second)

        def cross_z(self, m):
            self.x[1, m].wait_recv()
            self.y[m].wait_recv()
            part = self.ks[1, m] + self.xrecv[1, m].astype(f32) + self.yrecv[m].astype(f32)
            if not geo["bits_w"] and m:
                self.over(part, m, m)
            elif m % 2:
                self.over(part, m, 1)
            else:
                self.ks[1, m] = part

        def over(self, part, m, low):
            self.zs[m - 1] = part.astype(bf16)
            self.z[m] = push(self.zs.at[m - 1], self.zrecv.at[m - 1], z_dev(low))

        def merge(self, m):
            if not geo["bits_w"]:
                return
            self.z[m + 1].wait_recv()
            part = self.ks[1, m] + self.zrecv[m].astype(f32)
            if m:
                self.over(part, m, 2)
            else:
                self.ks[1, 0] = part

        def total(self):
            result = self.ks[1, 0]
            for m in range(2, Z, 2) if geo["bits_w"] else range(1, Z):
                self.z[m].wait_recv()
                result = result + self.zrecv[m - 1].astype(f32)
            return result

    per = len(grad_refs) // 4
    sum1a, sum1b, sum2, sum_n = [
        WeightSum(geo["x_first"][k], *grad_refs[k * per : (k + 1) * per]) for k in range(4)
    ]

    sum_n.put(0, inner(own_nodes, d_pre_n), r3)
    sum_n.put(D, inner(agg_low, d_pre_n), r3)
    sum_n.put(0, inner(hidden_n, d_out_n), r4, r3)
    sum_n.start()
    nnew_out[...] = (own_nodes.astype(f32) + normed_n * par(6) + par(7)).astype(bf16)
    node_part = ncot + times_t(d_pre_n, w3[0:D, :])
    gsm[4:5, :] = jnp.sum(d_pre_n.astype(f32), axis=0, keepdims=True)
    gsm[5:6, :] = jnp.sum(d_out_n.astype(f32), axis=0, keepdims=True)
    gsm[6:7, :] = jnp.sum(ncot * normed_n, axis=0, keepdims=True)
    gsm[7:8, :] = jnp.sum(ncot, axis=0, keepdims=True)
    for step in geo["back"]:
        kind, m, h = decode(step, 10)
        if kind == 1:
            sum_n.cross_x(m)
        elif m < Z:
            step_d(m, h)
    for load in loads[10:]:
        load.wait()
    for copy in d_y:
        copy.wait_recv()

    sums[...] = jnp.zeros_like(sums)
    d_all = dbuf[...].reshape(N, D)

    def edge_back(i):
        at = slice(i * R, (i + 1) * R)
        live = row_id < count - i * R
        d_edge = cot[at, :].astype(f32) + jnp.where(live, mm(pick[at, N : 2 * N], d_all), 0.0)
        dedge[at, :] = d_edge
        masked = jnp.where(live, d_edge, 0.0)
        norm = normed[at, :]
        inv = rstd[at, 0:1]
        weighted = masked * norm
        sums[2] += fold_rows(weighted)
        sums[3] += fold_rows(masked)
        d_out = norm_back(masked, norm, inv, par(2)).astype(bf16)
        dout[at, :] = d_out
        sums[1] += fold_rows(d_out.astype(f32))
        d_pre = (times_t(d_out, w2[...]) * slope[at, :]).astype(bf16)
        dpre[at, :] = d_pre
        sums[0] += fold_rows(d_pre.astype(f32))

    edge_back(0)
    for m in order:
        sum_n.cross_y(m)
    edge_back(1)
    edges_all = edges[...]

    def edge_grads(k, into):
        at = slice(k * (D // 2), (k + 1) * (D // 2))
        d_pre = dpre[:, at]
        into.put(0, inner(edges_all, d_pre))
        for half in range(2):
            nodes_at = slice(half * N, (half + 1) * N)
            seg[nodes_at, at] = mm(spread[nodes_at, :], d_pre).astype(bf16)
            into.put((1 + half) * D, inner(nodes_all, seg[nodes_at, at]))
        into.start()

    sums_w = (sum1a, sum1b, sum2, sum_n)
    gm = []
    node_sum = NodeSum(geo["bits_node"], pb_n, yr_n, zs_n, zr_n)

    def step_w(which, _):
        if which == 2:
            sum2.put(0, inner(hidden[...], dout[...]))
            sum2.start()
        else:
            edge_grads(which, sums_w[which])

    def step_t(which, _):
        if which == 4:
            ngrad_out[...] = (node_part + node_sum.total()).astype(bf16)
            return
        result = sums_w[which].total()
        if which == 3:
            g3_out[...] = result[0:r3]
            g4_out[...] = result[r3 : r3 + r4]
            update(2)
            update(3)
        elif which == 2:
            g2_out[...] = result
            update(1)
        else:
            g1_out[:, which * (D // 2) : (which + 1) * (D // 2)] = result

    def step_n(which, k):
        if which == 6:
            total = times_t(seg[0:N, :], w1[D : 2 * D, :])
            total = total + times_t(seg[N : 2 * N, :], w1[2 * D : 3 * D, :])
            pf[...] = total.reshape(pf.shape)
            pb_n[...] = total.astype(bf16).reshape(pf.shape)
            for m in order:
                for h in range(2):
                    node_sum.y[m, h] = push(pb_n.at[zx(m), yp, h], yr_n.at[m, h], y_dev)
        elif which < 9:
            node_sum.turn(k, which - 7)
        else:
            node_sum.merge(k, which - 9)

    def step_e(*_):
        for i in range(2):
            at = slice(i * R, (i + 1) * R)
            egrad[at, :] = (dedge[at, :] + times_t(dpre[at, :], w1[0:D, :])).astype(bf16)

    def step_g(_, k):
        if k == 0:
            for row in range(4):
                gsm[row : row + 1, :] = jnp.sum(sums[row], axis=0, keepdims=True)
            for zz in range(Z):
                gm_tile[zz] = gsm[:, zz * wide : (zz + 1) * wide]
            gm.extend(
                push(gm_tile.at[zx(m)], gm_tile.at[Z + m - 1], z_dev(m)) for m in range(1, Z)
            )
        elif k == 1:
            tile = gm_tile[z]
            for m in range(1, Z):
                gm[m - 1].wait_recv()
                tile = tile + gm_tile[Z + m - 1]
            gm_src[0] = tile
            gm.append(push(gm_src.at[0], gm_rcv.at[0], y_dev))
        else:
            small_sum(gm_src, gm_rcv, k - 2, gm[-1])
            if k < 4:
                gm.append(push(gm_src.at[k - 1], gm_rcv.at[k - 1], (x_dev, c_dev)[k - 2]))
                return
            take = (
                lax.broadcasted_iota(jnp.int32, (wide, ws), 0)
                == lax.broadcasted_iota(jnp.int32, (wide, ws), 1) + first
            )
            gs_out[...] = jnp.dot(
                gm_src[3],
                jnp.where(take, 1.0, 0.0),
                preferred_element_type=f32,
                precision=lax.Precision.HIGHEST,
            )
            update(4)

    tail = (
        step_w,
        lambda which, k: sums_w[which].cross_x(k),
        lambda which, m: sums_w[which].cross_y(m),
        lambda which, m: sums_w[which].cross_z(m),
        lambda which, m: sums_w[which].merge(m),
        step_n,
        step_t,
        step_e,
        step_g,
    )
    for step in geo["tail"]:
        kind, which, k = decode(step, 100)
        if not 2 <= kind <= 5 or k < Z:
            tail[kind](which, k)
    update(0)
    for copy in started:
        copy.wait_send()


def deliver_kernel(*refs):
    count = len(refs) // 2
    copies = []
    for k in range(count):
        dst = refs[count + k]
        dst = dst.at[0] if k < 4 else dst
        copies.append(pltpu.make_async_copy(refs[k], dst, refs[-1].at[k]))
    for copy in copies:
        copy.start()
    for copy in copies:
        copy.wait()


def on_device(n_edge, n_grp, *args):
    (
        edge_lat,
        node_lat,
        edge_cot,
        node_cot,
        senders,
        receivers,
        edge_count,
        *state,
    ) = args
    weights, firsts, seconds = state[0:5], state[5:10], state[10:15]
    rows, D = edge_lat.shape[1:]
    n = node_lat.shape[1]
    N = n * n_edge
    n_dev = n_edge * n_grp
    shards = [w.shape[0] for w in weights[:4]]
    fits = (
        n_edge % 2 == 0
        and n_grp == 4
        and all(r % 16 == 0 for r in shards)
        and n_edge // 2 in (2, 4)
        and D % (128 * (n_edge // 2)) == 0
        and D % 256 == 0
        and N % 128 == 0
        and n % 32 == 0
        and (shards[0] + shards[1]) % 32 == 0
        and rows % 256 == 0
        and rows * N <= 1024 * 1024
    )
    if not fits:
        return native(*args)
    Z, Y, X, C = n_edge // 2, 2, 2, 2
    n_sem = 240

    def vm(shape, dtype=bf16):
        return pltpu.VMEM(shape, dtype)

    ins = [edge_lat[0], edge_cot[0], node_lat[0], node_cot[0], senders, receivers, edge_count]
    ins += [*weights, *firsts, *seconds]
    moments = [vm(m.shape, f32) for m in (*firsts, *seconds)]
    scratch = [
        *moments,
        *[vm(a.shape, a.dtype) for a in ins[:12] if a is not edge_count],
        vm((Z, Y, n, D)),
        vm((Z, Y, n, D)),
        *[vm((r * n_dev, D)) for r in shards],
        vm((Z, Y, X, C, shards[0] + shards[1], D)),
        vm((Z, Y, X, C, shards[2] + shards[3], D)),
        vm((rows, 2 * N)),
        vm((2 * N, rows)),
        vm((2 * N, D)),
        vm((rows, D), f32),
        vm((rows, D)),
        vm((rows, D), f32),
        vm((rows, 128), f32),
        vm((rows, D)),
        vm((rows, D), f32),
        vm((rows, D)),
        vm((rows, D)),
        vm((4, 8, D), f32),
        vm((Z, Y, 2, n // 2, D), f32),
        vm((Z, Y, 2, n // 2, D)),
        vm((Z, Y, 2, n // 2, D)),
        vm((Z, 2, n // 2, D)),
        vm((Z, 2, n // 2, D)),
        *[vm((Z - 1, 2, n // 2, D))] * 4,
        vm((2 * N, D)),
        vm((4, 8, D // Z), f32),
        vm((3, 8, D // Z), f32),
        vm((Z, 8, D // Z), f32),
        vm((8, D), f32),
        vm((4, 8, D // Z), f32),
        vm((3, 8, D // Z), f32),
        vm((2 * Z - 1, 8, D // Z), f32),
        vm((8, D), f32),
    ]
    blocks = ((shards[0], D // 2), (shards[0], D // 2), (shards[1], D), (shards[2] + shards[3], D))
    for r, cols in blocks:
        scratch += [
            vm((Z, Y, X, C, r, cols)),
            vm((4, Z, r, cols)),
            vm((2, Z, r, cols)),
            vm((2, Z, r, cols)),
            vm((2, Z, r, cols), f32),
            vm((Z, r, cols)),
            vm((Z, r, cols)),
            vm((Z - 1, r, cols)),
            vm((Z - 1, r, cols)),
        ]
    scratch += [
        pltpu.SemaphoreType.DMA((len(ins),)),
        pltpu.SemaphoreType.DMA((n_sem,)),
        pltpu.SemaphoreType.DMA((n_sem,)),
    ]
    hbm = pl.BlockSpec(memory_space=pltpu.HBM)
    anyspace = pl.BlockSpec(memory_space=pl.ANY)
    vmem = pl.BlockSpec(memory_space=pltpu.VMEM)
    state_out = [vm(w.shape, f32) for w in weights]
    results = pl.pallas_call(
        functools.partial(layer_kernel, dict(GEO, dims=(Z, Y, X, C), n_sem=n_sem)),
        out_shape=[vm((rows, D)), vm((n, D))] * 2 + state_out * 3,
        in_specs=[hbm] * 6 + [pl.BlockSpec(memory_space=pltpu.SMEM)] + [hbm] * 15,
        out_specs=[vmem] * 19,
        scratch_shapes=scratch,
        compiler_params=pltpu.CompilerParams(
            collective_id=0, has_side_effects=True, vmem_limit_bytes=52 * 1024 * 1024
        ),
        name="layer",
    )(*ins)
    sds = jax.ShapeDtypeStruct
    shapes = [sds((1, *r.shape) if k < 4 else r.shape, r.dtype) for k, r in enumerate(results)]
    return tuple(
        pl.pallas_call(
            deliver_kernel,
            out_shape=shapes,
            in_specs=[vmem] * 19,
            out_specs=[anyspace] * 19,
            scratch_shapes=[pltpu.SemaphoreType.DMA((19,))],
            compiler_params=pltpu.CompilerParams(vmem_limit_bytes=8 * 1024 * 1024),
            name="deliver",
        )(*results)
    )


def solution(mesh):
    in_specs = (
        P("grp", "edge", None),
        P("grp", "edge", None),
        P("grp", "edge", None),
        P("grp", "edge", None),
        P("grp", "edge"),
        P("grp", "edge"),
        P("grp", "edge"),
        P(("edge", "grp"), None),
        P(("edge", "grp"), None),
        P(("edge", "grp"), None),
        P(("edge", "grp"), None),
        P(None, ("edge", "grp")),
        P(("edge", "grp"), None),
        P(("edge", "grp"), None),
        P(("edge", "grp"), None),
        P(("edge", "grp"), None),
        P(None, ("edge", "grp")),
        P(("edge", "grp"), None),
        P(("edge", "grp"), None),
        P(("edge", "grp"), None),
        P(("edge", "grp"), None),
        P(None, ("edge", "grp")),
    )
    out_specs = (
        P("grp", "edge", None),
        P("grp", "edge", None),
        P("grp", "edge", None),
        P("grp", "edge", None),
        P(("edge", "grp"), None),
        P(("edge", "grp"), None),
        P(("edge", "grp"), None),
        P(("edge", "grp"), None),
        P(None, ("edge", "grp")),
        P(("edge", "grp"), None),
        P(("edge", "grp"), None),
        P(("edge", "grp"), None),
        P(("edge", "grp"), None),
        P(None, ("edge", "grp")),
        P(("edge", "grp"), None),
        P(("edge", "grp"), None),
        P(("edge", "grp"), None),
        P(("edge", "grp"), None),
        P(None, ("edge", "grp")),
    )
    return jax.shard_map(
        functools.partial(on_device, mesh.shape["edge"], mesh.shape["grp"]),
        mesh=mesh, in_specs=in_specs, out_specs=out_specs, check_vma=False
    )
```

```python
import functools

import jax
import jax.numpy as jnp
from jax import lax
from jax.experimental import pallas as pl
from jax.experimental.pallas import tpu as pltpu
from jax.sharding import PartitionSpec as P

step_count = 10.0


def inner(left, right):
    return lax.dot_general(
        left, right, (((0,), (0,)), ((), ())), preferred_element_type=jnp.float32
    )


def times_t(left, right):
    return lax.dot_general(
        left, right, (((1,), (1,)), ((), ())), preferred_element_type=jnp.float32
    )


def norm_stats(values):
    mean = jnp.mean(values, axis=-1, keepdims=True)
    centred = values - mean
    var = jnp.mean(centred * centred, axis=-1, keepdims=True)
    rstd = lax.rsqrt(var + 1e-05)
    return (centred * rstd, rstd)


def norm_back(grad_out, normed, rstd, gain):
    scaled = grad_out * gain
    return rstd * (
        scaled
        - jnp.mean(scaled, axis=-1, keepdims=True)
        - normed * jnp.mean(scaled * normed, axis=-1, keepdims=True)
    )


def silu_slope(values):
    sig = jax.nn.sigmoid(values)
    return sig * (1.0 + values * (1.0 - sig))


def adamw(weight, grad, first, second, rate):
    first_new = 0.9 * first + 0.1 * grad
    second_new = 0.999 * second + 0.001 * grad * grad
    mhat = first_new / (1.0 - 0.9**step_count)
    vhat = second_new / (1.0 - 0.999**step_count)
    return (weight - rate * (mhat / (jnp.sqrt(vhat) + 1e-08) + 0.1 * weight), second_new)


def native(
    edge_lat,
    node_lat,
    edge_cot,
    node_cot,
    senders,
    receivers,
    edge_count,
    w_edge_in,
    w_edge_out,
    w_node_in,
    w_node_out,
    small_params,
    first_edge_in,
    first_edge_out,
    first_node_in,
    first_node_out,
    first_small,
    second_edge_in,
    second_edge_out,
    second_node_in,
    second_node_out,
    second_small,
):
    bf = jnp.bfloat16
    edges = edge_lat[0]
    nodes = node_lat[0]
    send = senders[0]
    recv = receivers[0]
    rows = edges.shape[0]
    width = edges.shape[1]
    maskf = (jnp.arange(rows, dtype=jnp.int32) < edge_count[0, 0]).astype(jnp.float32)[:, None]
    w1e, w2e, w1n, w2n, small = (
        lax.all_gather(w_edge_in.astype(bf), ("edge", "grp"), axis=0, tiled=True),
        lax.all_gather(w_edge_out.astype(bf), ("edge", "grp"), axis=0, tiled=True),
        lax.all_gather(w_node_in.astype(bf), ("edge", "grp"), axis=0, tiled=True),
        lax.all_gather(w_node_out.astype(bf), ("edge", "grp"), axis=0, tiled=True),
        lax.all_gather(small_params.astype(bf), ("edge", "grp"), axis=1, tiled=True),
    )
    params = small.astype(jnp.float32)
    whole = lax.all_gather(nodes, "edge", axis=0, tiled=True)
    node_total = whole.shape[0]
    joined = jnp.concatenate([edges, whole[send], whole[recv]], axis=1)
    pre = jnp.dot(joined, w1e, preferred_element_type=jnp.float32) + params[0]
    hidden = jax.nn.silu(pre).astype(bf)
    out = jnp.dot(hidden, w2e, preferred_element_type=jnp.float32) + params[1]
    normed, rstd = norm_stats(out)
    edge_new = edges.astype(jnp.float32) + maskf * (normed * params[2] + params[3])
    dense = jnp.zeros((node_total, width), jnp.float32).at[recv].add(maskf * edge_new)
    agg = lax.psum_scatter(dense, "edge", scatter_dimension=0, tiled=True)
    node_in = jnp.concatenate([nodes, agg.astype(bf)], axis=1)
    pre_n = jnp.dot(node_in, w1n, preferred_element_type=jnp.float32) + params[4]
    hidden_n = jax.nn.silu(pre_n).astype(bf)
    out_n = jnp.dot(hidden_n, w2n, preferred_element_type=jnp.float32) + params[5]
    normed_n, rstd_n = norm_stats(out_n)
    node_new = nodes.astype(jnp.float32) + normed_n * params[6] + params[7]
    grad_node_out_f = node_cot[0].astype(jnp.float32)
    d_out_n = norm_back(grad_node_out_f, normed_n, rstd_n, params[6]).astype(bf)
    gain_n = jnp.sum(grad_node_out_f * normed_n, axis=0)
    shift_n = jnp.sum(grad_node_out_f, axis=0)
    g_w2n = inner(hidden_n, d_out_n)
    g_b2n = jnp.sum(d_out_n.astype(jnp.float32), axis=0)
    d_pre_n = (times_t(d_out_n, w2n) * silu_slope(pre_n)).astype(bf)
    g_w1n = inner(node_in, d_pre_n)
    g_b1n = jnp.sum(d_pre_n.astype(jnp.float32), axis=0)
    d_node_in = times_t(d_pre_n, w1n)
    node_part = grad_node_out_f + d_node_in[:, :width]
    d_agg = d_node_in[:, width:].astype(bf)
    agg_rows = lax.all_gather(d_agg, "edge", axis=0, tiled=True)
    d_edge = edge_cot[0].astype(jnp.float32) + maskf * agg_rows[recv].astype(jnp.float32)
    masked = maskf * d_edge
    d_out = norm_back(masked, normed, rstd, params[2]).astype(bf)
    gain_e = jnp.sum(masked * normed, axis=0)
    shift_e = jnp.sum(masked, axis=0)
    g_w2e = inner(hidden, d_out)
    g_b2e = jnp.sum(d_out.astype(jnp.float32), axis=0)
    d_pre = (times_t(d_out, w2e) * silu_slope(pre)).astype(bf)
    g_w1e = inner(joined, d_pre)
    g_b1e = jnp.sum(d_pre.astype(jnp.float32), axis=0)
    d_joined = times_t(d_pre, w1e)
    edge_grad = (d_edge + d_joined[:, :width]).astype(bf)
    dense_grad = jnp.zeros((node_total, width), jnp.float32)
    dense_grad = (
        dense_grad.at[send]
        .add(d_joined[:, width : 2 * width])
        .at[recv]
        .add(d_joined[:, 2 * width :])
    )
    node_sum = lax.psum_scatter(dense_grad, "edge", scatter_dimension=0, tiled=True)
    node_grad = (node_part + node_sum).astype(bf)
    g_small = jnp.stack([g_b1e, g_b2e, gain_e, shift_e, g_b1n, g_b2n, gain_n, shift_n])
    grads = (
        lax.psum_scatter(g_w1e, ("edge", "grp"), scatter_dimension=0, tiled=True),
        lax.psum_scatter(g_w2e, ("edge", "grp"), scatter_dimension=0, tiled=True),
        lax.psum_scatter(g_w1n, ("edge", "grp"), scatter_dimension=0, tiled=True),
        lax.psum_scatter(g_w2n, ("edge", "grp"), scatter_dimension=0, tiled=True),
        lax.psum_scatter(g_small, ("edge", "grp"), scatter_dimension=1, tiled=True),
    )
    weights = (w_edge_in, w_edge_out, w_node_in, w_node_out, small_params)
    firsts = (first_edge_in, first_edge_out, first_node_in, first_node_out, first_small)
    seconds = (second_edge_in, second_edge_out, second_node_in, second_node_out, second_small)
    rates = (0.03, 0.03, 0.03, 0.03, 0.2)
    updated = [
        adamw(w, g, m, v, r) for w, g, m, v, r in zip(weights, grads, firsts, seconds, rates)
    ]
    return (
        edge_new.astype(bf)[None],
        node_new.astype(bf)[None],
        edge_grad[None],
        node_grad[None],
        grads[0],
        grads[1],
        grads[2],
        grads[3],
        grads[4],
        updated[0][1],
        updated[1][1],
        updated[2][1],
        updated[3][1],
        updated[4][1],
        updated[0][0],
        updated[1][0],
        updated[2][0],
        updated[3][0],
        updated[4][0],
    )


bf16 = jnp.bfloat16
f32 = jnp.float32
MESH = pl.DeviceIdType.MESH


def mm(left, right):
    return jnp.dot(left, right, preferred_element_type=f32)


def fold_rows(values):
    count, width = values.shape
    return jnp.sum(values.reshape(count // 8, 8, width), axis=0)


GEO = {
    "x_first": (True, True, False, True),
    "diagonal": (),
    "bits_a": True,
    "bits_n": True,
    "bits_b": True,
    "bits_d": True,
    "bits_agg": False,
    "bits_node": False,
    "bits_w": (False, False, False, False),
    "gather": (
        200, 700, 100, 10, 101, 20, 11, 21, 120, 110, 600, 30, 111, 31, 610, 220, 121, 210, 130,
        300, 131, 230, 620
    ),
    "late": (
        310, 320, 400, 410, 420
    ),
    "mid": (
        330, 430
    ),
    "agg": (
        30, 600, 10, 20, 111, 121, 131, 230, 0, 210, 101, 220, 221, 610, 620, 231, 211, 200, 630,
        201, 300, 301, 700, 701, 320, 800, 420, 410, 321, 421, 500, 411, 510, 520, 430, 530, 431
    ),
    "tail": (
        2032, 9050, 2031, 2033, 9051, 10051, 10050, 0, 3032, 2030, 10, 5060, 8050, 1000, 1010, 3033,
        3030, 1012, 1001, 1002, 20, 5073, 5083, 1022, 3031, 8051, 1003, 5082, 2003, 2002, 2013,
        1020, 5072, 5081, 2011, 5071, 1011, 1013, 2012, 2001, 7050, 5070, 1021, 1023, 5080, 5102,
        3003, 2023, 3013, 2021, 3002, 5090, 5092, 4030, 2022, 8052, 4002, 3011, 3012, 2010, 3001,
        2000, 4032, 2020, 4012, 3023, 5100, 3022, 3021, 3020, 8053, 3010, 6040, 4010, 3000, 8054,
        6030, 4000, 6000, 4020, 6010, 4022, 6020
    ),
}


def decode(step, unit):
    return step // (10 * unit), step // 10 % unit, step % 10


def layer_kernel(geo, *refs):
    Z, Y, X, C = geo["dims"]
    n_sem = geo["n_sem"]
    (
        edges_hbm,
        cot_hbm,
        nodes_hbm,
        ncot_hbm,
        send_hbm,
        recv_hbm,
        count_in,
        w1_hbm,
        w2_hbm,
        w3_hbm,
        w4_hbm,
        small_hbm,
        *rest,
    ) = refs
    moments_hbm, rest = rest[:10], rest[10:]
    enew, nnew_out, egrad, ngrad_out, *rest = rest
    grads_out, seconds_out, weights_out, rest = rest[0:5], rest[5:10], rest[10:15], rest[15:]
    g1_out, g2_out, g3_out, g4_out, gs_out = grads_out
    moments_in, rest = rest[:10], rest[10:]
    (
        edges,
        cot,
        nodes_in,
        ncot_in,
        send_in,
        recv_in,
        w1_in,
        w2_in,
        w3_in,
        w4_in,
        small_in,
        nbuf,
        dbuf,
        w1,
        w2,
        w3,
        w4,
        wa,
        wb,
        pick,
        spread,
        proj,
        slope,
        hidden,
        normed,
        rstd,
        term,
        dedge,
        dout,
        dpre,
        sums,
        pf,
        pb_a,
        pb_n,
        yr_a,
        yr_n,
        zs_a,
        zs_n,
        zr_a,
        zr_n,
        seg,
        pre_own,
        norm_n,
        node_part,
        agg_low,
        hidden_n,
        dout_n,
        dpre_n,
        sm_src,
        sm_rcv,
        sm_tile,
        par_all,
        gm_src,
        gm_rcv,
        gm_tile,
        gsm,
        *grad_refs,
    ) = rest
    local_sem, ssem, rsem = grad_refs[-3:]
    grad_refs = grad_refs[:-3]
    rows, D = edges.shape
    n = nodes_in.shape[0]
    N = Z * Y * n
    R = rows // 2

    e_id = lax.axis_index("edge")
    g_id = lax.axis_index("grp")
    z = e_id // Y
    y = e_id % Y
    x = g_id // C
    c = g_id % C
    yp, xp, cp = 1 - y, 1 - x, 1 - c
    me = e_id * (X * C) + g_id
    y_dev = (z * Y + yp, g_id)
    x_dev = (e_id, xp * C + c)
    c_dev = (e_id, x * C + cp)
    xy_dev = (z * Y + yp, xp * C + c)

    def zx(m):
        place = z
        for j in range(m.bit_length()):
            if m >> j & 1:
                place = place + (1 << j) - (2 << j) * (z // (1 << j) % 2)
        return place

    def z_dev(m):
        return (zx(m) * Y + y, g_id)

    started = []

    def push(src, dst, dev):
        k = len(started)
        assert k < n_sem
        copy = pltpu.make_async_remote_copy(
            src_ref=src,
            dst_ref=dst,
            send_sem=ssem.at[k],
            recv_sem=rsem.at[k],
            device_id=dev,
            device_id_type=MESH,
        )
        copy.start()
        started.append(copy)
        return copy

    barrier = pltpu.get_barrier_semaphore()
    peers = [z_dev(m) for m in range(1, Z)] + [y_dev, x_dev, c_dev, xy_dev]
    for dev in peers:
        pl.semaphore_signal(barrier, inc=1, device_id=dev, device_id_type=MESH)
    loads = [
        (w1_hbm, w1_in),
        (w2_hbm, w2_in),
        (w3_hbm, w3_in),
        (w4_hbm, w4_in),
        (small_hbm, small_in),
        (nodes_hbm, nodes_in),
        (send_hbm, send_in),
        (recv_hbm, recv_in),
        (ncot_hbm, ncot_in),
        (edges_hbm, edges),
        (cot_hbm, cot),
        *zip(moments_hbm, moments_in),
    ]
    loads = [pltpu.make_async_copy(*pair, local_sem.at[k]) for k, pair in enumerate(loads)]
    for load in loads:
        load.start()
    for load in loads[0:6]:
        load.wait()
    r1, r2, r3, r4 = (own.shape[0] for own in (w1_in, w2_in, w3_in, w4_in))
    ra = r1 + r2
    wa[z, y, x, c, 0:r1, :] = w1_in[...].astype(bf16)
    wa[z, y, x, c, r1:ra, :] = w2_in[...].astype(bf16)
    wb[z, y, x, c, 0:r3, :] = w3_in[...].astype(bf16)
    wb[z, y, x, c, r3 : r3 + r4, :] = w4_in[...].astype(bf16)
    nbuf[z, y] = nodes_in[...]
    ws = small_in.shape[1]
    wide = ws * Y * X * C
    first = me % (Y * X * C) * ws
    place = (
        lax.broadcasted_iota(jnp.int32, (ws, wide), 1)
        == lax.broadcasted_iota(jnp.int32, (ws, wide), 0) + first
    )
    sm_src[0] = mm(small_in[...].astype(bf16), jnp.where(place, 1.0, 0.0).astype(bf16))

    def update(k):
        weight = (w1_in, w2_in, w3_in, w4_in, small_in)[k]
        weights_out[k][...], seconds_out[k][...] = adamw(
            weight[...],
            grads_out[k][...],
            moments_in[k][...],
            moments_in[5 + k][...],
            0.2 if k == 4 else 0.03,
        )

    pl.semaphore_wait(barrier, len(peers))

    def along_z(own, by_bits):
        to = [1 << j for j in range((Z - 1).bit_length())] if by_bits else range(1, Z)
        return {m: push(own, own, z_dev(m)) for m in reversed(to)}

    def arrive_z(copies, m, block):
        copies[m].wait_recv()
        j = 0 if len(copies) < Z - 1 else Z
        while not m >> j & 1 and j < Z:
            copies[m | 1 << j] = push(block, block, z_dev(1 << j))
            j += 1

    halves = ra // 2

    def part(zz, yy, xx, h):
        return wa.at[zz, yy, xx, c, h * halves : (h + 1) * halves, :]

    def send(block, dev):
        return push(block, block, dev)

    def settle(zz, yy, xx, cc):
        k = ((zz * Y + yy) * X + xx) * C + cc
        w1[pl.ds(pl.multiple_of(k * r1, 16), r1), :] = wa[zz, yy, xx, cc, 0:r1, :]
        w2[pl.ds(pl.multiple_of(k * r2, 16), r2), :] = wa[zz, yy, xx, cc, r1:ra, :]

    def small_sum(src, rcv, stage, copy):
        copy.wait_recv()
        src[stage + 1] = src[stage] + rcv[stage]

    small = [push(sm_src.at[0], sm_rcv.at[0], c_dev)]
    a_z, a_y, a_x, a_c, x_order = ({}, {}), {}, [], [], []
    n_z, n_y, b_z, b_y, b_x = {}, [], {}, [], []
    for h in range(2):
        own = part(z, y, x, h)
        a_z[h].update(along_z(own, geo["bits_a"]))
        a_y[0, h] = send(own, y_dev)
        a_x.append(send(own, x_dev))
        x_order.append((0, 0, h))
    a_c.append(send(wa.at[z, y, x, c], c_dev))

    def across(m, flip, h):
        yy = yp if flip else y
        straight = m in geo["diagonal"]
        if not (flip and straight):
            a_x.append(send(part(zx(m), yy, x, h), x_dev))
            x_order.append((m, flip, h))
        if straight and not flip:
            a_x.append(send(part(zx(m), yy, x, h), xy_dev))
            x_order.append((m, 1, h))
        if h == 1:
            a_c.append(send(wa.at[zx(m), yy, x, c], c_dev))
            settle(zx(m), yy, x, c)

    def on_z(m, h):
        block = part(zx(m), y, x, h)
        arrive_z(a_z[h], m, block)
        a_y[m, h] = send(block, y_dev)
        across(m, 0, h)

    def on_y(m, h):
        a_y[m, h].wait_recv()
        across(m, 1, h)

    def on_n(m, _):
        block = nbuf.at[zx(m), y]
        if m == 0:
            n_z.update(along_z(block, geo["bits_n"]))
        else:
            arrive_z(n_z, m, block)
        n_y.append(send(block, y_dev))

    def on_b(m, _):
        block = wb.at[zx(m), y, x, c]
        if m == 0:
            b_z.update(along_z(block, geo["bits_b"]))
        else:
            arrive_z(b_z, m, block)

    def line_b(m, _):
        block = wb.at[zx(m), y, x, c]
        b_y.append(send(block, y_dev))
        b_x.append(send(block, x_dev))

    def on_x(first, last):
        for k in range(first, last):
            m, flip, h = x_order[k]
            a_x[k].wait_recv()
            if h == 1:
                yy = yp if flip else y
                a_c.append(send(wa.at[zx(m), yy, xp, c], c_dev))
                settle(zx(m), yy, xp, c)

    def on_small(k, _):
        small_sum(sm_src, sm_rcv, k, small[k])
        if k < 2:
            small.append(push(sm_src.at[k + 1], sm_rcv.at[k + 1], (y_dev, x_dev)[k]))
        else:
            sm_tile[z] = sm_src[3]
            small.extend(push(sm_src.at[3], sm_tile.at[z], z_dev(m)) for m in range(1, Z))

    settle(z, y, x, c)
    def on_hot(*_):
        for load in loads[6:9]:
            load.wait()
        lane = lax.broadcasted_iota(jnp.int32, (128, N), 1)
        sub = lax.broadcasted_iota(jnp.int32, (N, 128), 0)

        @pl.loop(0, rows // 128)
        def _(k):
            at = pl.ds(pl.multiple_of(k * 128, 128), 128)
            for half, ids in enumerate((send_in, recv_in)):
                row = jnp.broadcast_to(ids[0:1, at], (128, 128))
                col = jnp.tile(row.T, (1, N // 128))
                pick[at, half * N : (half + 1) * N] = jnp.where(lane == col, 1.0, 0.0).astype(bf16)
                flat = jnp.broadcast_to(ids[0:1, at], (N, 128))
                spread[half * N : (half + 1) * N, at] = jnp.where(sub == flat, 1.0, 0.0).astype(bf16)

    steps = (on_z, on_y, on_n, on_b, line_b, on_x, on_small, on_hot)

    def gather(name):
        for step in geo[name]:
            kind, m, h = decode(step, 10)
            if kind > 5 or m < Z:
                steps[kind](m, h)

    gather("gather")
    on_x(0, len(x_order))
    for copy in n_y:
        copy.wait_recv()
    loads[9].wait()
    for copy in a_c:
        copy.wait_recv()
    gather("late")
    for zz in range(Z):
        for yy in range(Y):
            for xx in range(X):
                settle(zz, yy, xx, cp)
    for copy in small[3:]:
        copy.wait_recv()
    for zz in range(Z):
        par_all[:, zz * wide : (zz + 1) * wide] = sm_tile[zz]

    nodes_all = nbuf[...].reshape(N, D)
    proj[0:N, :] = mm(nodes_all, w1[D : 2 * D, :]).astype(bf16)
    proj[N : 2 * N, :] = mm(nodes_all, w1[2 * D : 3 * D, :]).astype(bf16)
    count = count_in[0, 0]
    row_id = lax.broadcasted_iota(jnp.int32, (R, D), 0)

    def edge_forward(i):
        at = slice(i * R, (i + 1) * R)
        live = row_id < count - i * R
        own = edges[at, :]
        pre = mm(own, w1[0:D, :]) + mm(pick[at, :], proj[...]) + par_all[0:1, :]
        sig = jax.nn.sigmoid(pre)
        act = (pre * sig).astype(bf16)
        hidden[at, :] = act
        slope[at, :] = sig * (1.0 + pre * (1.0 - sig))
        out = mm(act, w2[...]) + par_all[1:2, :]
        norm, inv = norm_stats(out)
        normed[at, :] = norm
        rstd[at, :] = jnp.broadcast_to(inv, (R, 128))
        new = own.astype(f32) + jnp.where(live, norm * par_all[2:3, :] + par_all[3:4, :], 0.0)
        enew[at, :] = new.astype(bf16)
        term[at, :] = jnp.where(live, new, 0.0).astype(bf16)

    edge_forward(0)
    gather("mid")
    edge_forward(1)

    order = tuple(reversed(range(Z)))

    class NodeSum:
        def __init__(self, by_bits, pb, yr, zs, zr):
            self.by_bits = by_bits
            self.pb, self.yr, self.zs, self.zr = pb, yr, zs, zr
            self.y, self.z = {}, {}

        def put(self, m, values):
            pf[zx(m)] = values.reshape(Y, 2, n // 2, D)
            self.pb[zx(m)] = values.astype(bf16).reshape(Y, 2, n // 2, D)

        def go(self, m, h):
            self.y[m, h] = push(self.pb.at[zx(m), yp, h], self.yr.at[m, h], y_dev)

        def over(self, m, h, low):
            self.zs[m - 1, h] = pf[zx(m), y, h].astype(bf16)
            self.z[m, h] = push(self.zs.at[m - 1, h], self.zr.at[m - 1, h], z_dev(low))

        def turn(self, m, h):
            self.y[m, h].wait_recv()
            pf[zx(m), y, h] = pf[zx(m), y, h] + self.yr[m, h].astype(f32)
            if not self.by_bits and m:
                self.over(m, h, m)
            elif m % 2:
                self.over(m, h, 1)

        def merge(self, m, h):
            if not self.by_bits:
                return
            self.z[m + 1, h].wait_recv()
            pf[zx(m), y, h] = pf[zx(m), y, h] + self.zr[m, h].astype(f32)
            if m:
                self.over(m, h, 2)

        def total(self, h):
            part = pf[z, y, h]
            for m in range(2, Z, 2) if self.by_bits else range(1, Z):
                self.z[m, h].wait_recv()
                part = part + self.zr[m - 1, h].astype(f32)
            return part

    class WeightSum:
        def __init__(self, x_first, by_bits, grad, crecv, xs, xrecv, ks, ys, yrecv, zs, zrecv):
            self.by_bits = by_bits
            self.first, self.second = (x_dev, y_dev) if x_first else (y_dev, x_dev)
            side = ((y, xp), (yp, x)) if x_first else ((yp, x), (y, xp))
            self.groups = ((yp, xp), side[0], side[1], (y, x))
            self.grad, self.crecv, self.xs, self.xrecv, self.ks = grad, crecv, xs, xrecv, ks
            self.ys, self.yrecv, self.zs, self.zrecv = ys, yrecv, zs, zrecv

        def put(self, first, values, lane_rows=None, base=0):
            low, r = values.astype(bf16), lane_rows or self.grad.shape[4]
            row = 0
            while row < values.shape[0]:
                k, off = divmod(first + row, r)
                size = min(r - off, values.shape[0] - row)
                at = (k // (Y * X * C), k // (X * C) % Y, k // C % X, k % C)
                self.grad[(*at, slice(base + off, base + off + size))] = low[row : row + size]
                row += size

        def start(self):
            self.c = [
                push(self.grad.at[:, yy, xx, cp], self.crecv.at[k], c_dev)
                for k, (yy, xx) in enumerate(self.groups)
            ]

            self.x, self.y, self.z = {}, {}, {}

        def cross_x(self, k):
            self.c[k].wait_recv()
            for m in order:
                part = self.grad[(zx(m), *self.groups[k], c)].astype(f32)
                part = part + self.crecv[k, zx(m)].astype(f32)
                if k < 2:
                    self.xs[k, m] = part.astype(bf16)
                    self.x[k, m] = push(self.xs.at[k, m], self.xrecv.at[k, m], self.first)
                else:
                    self.ks[k - 2, m] = part

        def cross_y(self, m):
            self.x[0, m].wait_recv()
            self.ys[m] = (self.ks[0, m] + self.xrecv[0, m].astype(f32)).astype(bf16)
            self.y[m] = push(self.ys.at[m], self.yrecv.at[m], self.second)

        def cross_z(self, m):
            self.x[1, m].wait_recv()
            self.y[m].wait_recv()
            part = self.ks[1, m] + self.xrecv[1, m].astype(f32) + self.yrecv[m].astype(f32)
            if not self.by_bits and m:
                self.over(part, m, m)
            elif m % 2:
                self.over(part, m, 1)
            else:
                self.ks[1, m] = part

        def over(self, part, m, low):
            self.zs[m - 1] = part.astype(bf16)
            self.z[m] = push(self.zs.at[m - 1], self.zrecv.at[m - 1], z_dev(low))

        def merge(self, m):
            if not self.by_bits:
                return
            self.z[m + 1].wait_recv()
            part = self.ks[1, m] + self.zrecv[m].astype(f32)
            if m:
                self.over(part, m, 2)
            else:
                self.ks[1, 0] = part

        def total(self):
            result = self.ks[1, 0]
            for m in range(2, Z, 2) if self.by_bits else range(1, Z):
                self.z[m].wait_recv()
                result = result + self.zrecv[m - 1].astype(f32)
            return result

    per = len(grad_refs) // 4
    sum1a, sum1b, sum2, sum_n = [
        WeightSum(geo["x_first"][k], geo["bits_w"][k], *grad_refs[k * per : (k + 1) * per]) for k in range(4)
    ]

    agg_sum = NodeSum(geo["bits_agg"], pb_a, yr_a, zs_a, zr_a)
    b_c = []

    def step_p(m, _):
        first_row = pl.multiple_of(N + zx(m) * (Y * n), Y * n)
        agg_sum.put(m, mm(spread[pl.ds(first_row, Y * n), :], term[...]))
        agg_sum.go(m, 0)

    def step_b(k, _):
        if k == 0:
            for copy in b_y:
                copy.wait_recv()
            b_x.append(send(wb.at[:, yp, x, c], x_dev))
            b_c.extend(send(wb.at[:, yy, x, c], c_dev) for yy in (y, yp))
        elif k == 1:
            for copy in b_x[:-1]:
                copy.wait_recv()
            b_c.append(send(wb.at[:, y, xp, c], c_dev))
        elif k == 2:
            b_x[-1].wait_recv()
            b_c.append(send(wb.at[:, yp, xp, c], c_dev))
        else:
            for copy in b_c:
                copy.wait_recv()
            w3[...] = wb[:, :, :, :, 0:r3, :].reshape(w3.shape)
            w4[...] = wb[:, :, :, :, r3 : r3 + r4, :].reshape(w4.shape)
            pre_own[...] = mm(nodes_in[...], w3[0:D, :])

    def par(k):
        return par_all[k : k + 1, :]

    def step_node(_, h):
        at = slice(h * (n // 2), (h + 1) * (n // 2))
        low = agg_sum.total(h).astype(bf16)
        agg_low[at, :] = low
        pre_n = pre_own[at, :] + mm(low, w3[D : 2 * D, :]) + par(4)
        sig_n = jax.nn.sigmoid(pre_n)
        act_n = (pre_n * sig_n).astype(bf16)
        hidden_n[at, :] = act_n
        normed_n, rstd_n = norm_stats(mm(act_n, w4[...]) + par(5))
        ncot = ncot_in[at, :].astype(f32)
        d_out_n = norm_back(ncot, normed_n, rstd_n, par(6)).astype(bf16)
        dout_n[at, :] = d_out_n
        slope_n = sig_n * (1.0 + pre_n * (1.0 - sig_n))
        d_pre_n = (times_t(d_out_n, w4[...]) * slope_n).astype(bf16)
        dpre_n[at, :] = d_pre_n
        dbuf[z, y, at, :] = times_t(d_pre_n, w3[D : 2 * D, :]).astype(bf16)
        step_d(0, h)
        norm_n[at, :] = normed_n

    d_z, d_y = {}, []

    def d_part(m, h):
        return dbuf.at[zx(m), y, h * (n // 2) : (h + 1) * (n // 2), :]

    def step_d(m, h):
        block = d_part(m, h)
        if m == 0:
            d_z[h] = along_z(block, geo["bits_d"])
        else:
            arrive_z(d_z[h], m, block)
        d_y.append(send(block, y_dev))

    def step_wn(*_):
        own_nodes, ncot = nodes_in[...], ncot_in[...].astype(f32)
        normed_n, d_pre_n, d_out_n = norm_n[...], dpre_n[...], dout_n[...]
        sum_n.put(0, inner(own_nodes, d_pre_n), r3)
        sum_n.put(D, inner(agg_low[...], d_pre_n), r3)
        sum_n.put(0, inner(hidden_n[...], d_out_n), r4, r3)
        sum_n.start()
        nnew_out[...] = (own_nodes.astype(f32) + normed_n * par(6) + par(7)).astype(bf16)
        node_part[...] = ncot + times_t(d_pre_n, w3[0:D, :])
        gsm[4:5, :] = jnp.sum(d_pre_n.astype(f32), axis=0, keepdims=True)
        gsm[5:6, :] = jnp.sum(d_out_n.astype(f32), axis=0, keepdims=True)
        gsm[6:7, :] = jnp.sum(ncot * normed_n, axis=0, keepdims=True)
        gsm[7:8, :] = jnp.sum(ncot, axis=0, keepdims=True)

    steps_n = (
        step_p,
        agg_sum.go,
        agg_sum.turn,
        agg_sum.merge,
        step_d,
        lambda k, _: sum_n.cross_x(k),
        step_b,
        step_node,
        step_wn,
    )
    for step in geo["agg"]:
        kind, m, h = decode(step, 10)
        if kind > 4 or m < Z:
            steps_n[kind](m, h)
    for load in loads[10:]:
        load.wait()
    for copy in d_y:
        copy.wait_recv()

    sums[...] = jnp.zeros_like(sums)

    def add_sums(k, at, values):
        sums[k, :, at] += fold_rows(values)

    d_all = dbuf[...].reshape(N, D)

    def step_v(_, i):
        at = slice(i * R, (i + 1) * R)
        live = row_id < count - i * R
        d_edge = cot[at, :].astype(f32) + jnp.where(live, mm(pick[at, N : 2 * N], d_all), 0.0)
        dedge[at, :] = d_edge
        masked = jnp.where(live, d_edge, 0.0)
        norm = normed[at, :]
        inv = rstd[at, 0:1]
        weighted = masked * norm
        add_sums(2, slice(0, D), weighted)
        add_sums(3, slice(0, D), masked)
        d_out = norm_back(masked, norm, inv, par(2)).astype(bf16)
        dout[at, :] = d_out
        add_sums(1, slice(0, D), d_out.astype(f32))

    def step_d(_, k):
        at = slice(k * (D // 2), (k + 1) * (D // 2))
        d_pre = (times_t(dout[...], w2[at, :]) * slope[:, at]).astype(bf16)
        dpre[:, at] = d_pre
        add_sums(0, at, d_pre.astype(f32))

    edges_all = edges[...]

    def edge_grads(k, into):
        at = slice(k * (D // 2), (k + 1) * (D // 2))
        d_pre = dpre[:, at]
        into.put(0, inner(edges_all, d_pre))
        for half in range(2):
            nodes_at = slice(half * N, (half + 1) * N)
            seg[nodes_at, at] = mm(spread[nodes_at, :], d_pre).astype(bf16)
            into.put((1 + half) * D, inner(nodes_all, seg[nodes_at, at]))
        into.start()

    sums_w = (sum1a, sum1b, sum2, sum_n)
    gm = []
    node_sum = NodeSum(geo["bits_node"], pb_n, yr_n, zs_n, zr_n)

    def step_w(which, _):
        if which == 2:
            sum2.put(0, inner(hidden[...], dout[...]))
            sum2.start()
        else:
            edge_grads(which, sums_w[which])

    def step_t(which, _):
        if which == 4:
            for h in range(2):
                at = slice(h * (n // 2), (h + 1) * (n // 2))
                ngrad_out[at, :] = (node_part[at, :] + node_sum.total(h)).astype(bf16)
            return
        result = sums_w[which].total()
        if which == 3:
            g3_out[...] = result[0:r3]
            g4_out[...] = result[r3 : r3 + r4]
            update(2)
            update(3)
        elif which == 2:
            g2_out[...] = result
            update(1)
        else:
            g1_out[:, which * (D // 2) : (which + 1) * (D // 2)] = result

    def step_n(which, k):
        if which == 6:
            total = times_t(seg[0:N, :], w1[D : 2 * D, :])
            total = total + times_t(seg[N : 2 * N, :], w1[2 * D : 3 * D, :])
            pf[...] = total.reshape(pf.shape)
            pb_n[...] = total.astype(bf16).reshape(pf.shape)
            for m in order:
                for h in range(2):
                    node_sum.go(m, h)
        elif which < 9:
            node_sum.turn(k, which - 7)
        else:
            node_sum.merge(k, which - 9)

    def step_e(*_):
        for i in range(2):
            at = slice(i * R, (i + 1) * R)
            egrad[at, :] = (dedge[at, :] + times_t(dpre[at, :], w1[0:D, :])).astype(bf16)

    def step_g(_, k):
        if k == 0:
            for row in range(4):
                gsm[row : row + 1, :] = jnp.sum(sums[row], axis=0, keepdims=True)
            for zz in range(Z):
                gm_tile[zz] = gsm[:, zz * wide : (zz + 1) * wide]
            gm.extend(
                push(gm_tile.at[zx(m)], gm_tile.at[Z + m - 1], z_dev(m)) for m in range(1, Z)
            )
        elif k == 1:
            tile = gm_tile[z]
            for m in range(1, Z):
                gm[m - 1].wait_recv()
                tile = tile + gm_tile[Z + m - 1]
            gm_src[0] = tile
            gm.append(push(gm_src.at[0], gm_rcv.at[0], y_dev))
        else:
            small_sum(gm_src, gm_rcv, k - 2, gm[-1])
            if k < 4:
                gm.append(push(gm_src.at[k - 1], gm_rcv.at[k - 1], (x_dev, c_dev)[k - 2]))
                return
            take = (
                lax.broadcasted_iota(jnp.int32, (wide, ws), 0)
                == lax.broadcasted_iota(jnp.int32, (wide, ws), 1) + first
            )
            gs_out[...] = jnp.dot(
                gm_src[3],
                jnp.where(take, 1.0, 0.0),
                preferred_element_type=f32,
                precision=lax.Precision.HIGHEST,
            )
            update(4)

    tail = (
        step_w,
        lambda which, k: sums_w[which].cross_x(k),
        lambda which, m: sums_w[which].cross_y(m),
        lambda which, m: sums_w[which].cross_z(m),
        lambda which, m: sums_w[which].merge(m),
        step_n,
        step_t,
        step_e,
        step_g,
        step_v,
        step_d,
    )
    for step in geo["tail"]:
        kind, which, k = decode(step, 100)
        if not 2 <= kind <= 5 or k < Z:
            tail[kind](which, k)
    update(0)
    for copy in started:
        copy.wait_send()


def deliver_kernel(*refs):
    count = len(refs) // 2
    copies = []
    for k in range(count):
        dst = refs[count + k]
        dst = dst.at[0] if k < 4 else dst
        copies.append(pltpu.make_async_copy(refs[k], dst, refs[-1].at[k]))
    for copy in copies:
        copy.start()
    for copy in copies:
        copy.wait()


def on_device(n_edge, n_grp, *args):
    (
        edge_lat,
        node_lat,
        edge_cot,
        node_cot,
        senders,
        receivers,
        edge_count,
        *state,
    ) = args
    weights, firsts, seconds = state[0:5], state[5:10], state[10:15]
    rows, D = edge_lat.shape[1:]
    n = node_lat.shape[1]
    N = n * n_edge
    n_dev = n_edge * n_grp
    shards = [w.shape[0] for w in weights[:4]]
    fits = (
        n_edge % 2 == 0
        and n_grp == 4
        and all(r % 16 == 0 for r in shards)
        and n_edge // 2 in (2, 4)
        and D % (128 * (n_edge // 2)) == 0
        and D % 256 == 0
        and N % 128 == 0
        and n % 32 == 0
        and (shards[0] + shards[1]) % 32 == 0
        and rows % 256 == 0
        and rows * N <= 1024 * 1024
    )
    if not fits:
        return native(*args)
    Z, Y, X, C = n_edge // 2, 2, 2, 2
    n_sem = 240

    def vm(shape, dtype=bf16):
        return pltpu.VMEM(shape, dtype)

    ins = [edge_lat[0], edge_cot[0], node_lat[0], node_cot[0], senders, receivers, edge_count]
    ins += [*weights, *firsts, *seconds]
    moments = [vm(m.shape, f32) for m in (*firsts, *seconds)]
    scratch = [
        *moments,
        *[vm(a.shape, a.dtype) for a in ins[:12] if a is not edge_count],
        vm((Z, Y, n, D)),
        vm((Z, Y, n, D)),
        *[vm((r * n_dev, D)) for r in shards],
        vm((Z, Y, X, C, shards[0] + shards[1], D)),
        vm((Z, Y, X, C, shards[2] + shards[3], D)),
        vm((rows, 2 * N)),
        vm((2 * N, rows)),
        vm((2 * N, D)),
        vm((rows, D), f32),
        vm((rows, D)),
        vm((rows, D), f32),
        vm((rows, 128), f32),
        vm((rows, D)),
        vm((rows, D), f32),
        vm((rows, D)),
        vm((rows, D)),
        vm((4, 8, D), f32),
        vm((Z, Y, 2, n // 2, D), f32),
        vm((Z, Y, 2, n // 2, D)),
        vm((Z, Y, 2, n // 2, D)),
        vm((Z, 2, n // 2, D)),
        vm((Z, 2, n // 2, D)),
        *[vm((Z - 1, 2, n // 2, D))] * 4,
        vm((2 * N, D)),
        *[vm((n, D), f32)] * 3,
        *[vm((n, D))] * 4,
        vm((4, 8, D // Z), f32),
        vm((3, 8, D // Z), f32),
        vm((Z, 8, D // Z), f32),
        vm((8, D), f32),
        vm((4, 8, D // Z), f32),
        vm((3, 8, D // Z), f32),
        vm((2 * Z - 1, 8, D // Z), f32),
        vm((8, D), f32),
    ]
    blocks = ((shards[0], D // 2), (shards[0], D // 2), (shards[1], D), (shards[2] + shards[3], D))
    for r, cols in blocks:
        scratch += [
            vm((Z, Y, X, C, r, cols)),
            vm((4, Z, r, cols)),
            vm((2, Z, r, cols)),
            vm((2, Z, r, cols)),
            vm((2, Z, r, cols), f32),
            vm((Z, r, cols)),
            vm((Z, r, cols)),
            vm((Z - 1, r, cols)),
            vm((Z - 1, r, cols)),
        ]
    scratch += [
        pltpu.SemaphoreType.DMA((len(ins),)),
        pltpu.SemaphoreType.DMA((n_sem,)),
        pltpu.SemaphoreType.DMA((n_sem,)),
    ]
    hbm = pl.BlockSpec(memory_space=pltpu.HBM)
    anyspace = pl.BlockSpec(memory_space=pl.ANY)
    vmem = pl.BlockSpec(memory_space=pltpu.VMEM)
    state_out = [vm(w.shape, f32) for w in weights]
    results = pl.pallas_call(
        functools.partial(layer_kernel, dict(GEO, dims=(Z, Y, X, C), n_sem=n_sem)),
        out_shape=[vm((rows, D)), vm((n, D))] * 2 + state_out * 3,
        in_specs=[hbm] * 6 + [pl.BlockSpec(memory_space=pltpu.SMEM)] + [hbm] * 15,
        out_specs=[vmem] * 19,
        scratch_shapes=scratch,
        compiler_params=pltpu.CompilerParams(
            collective_id=0, has_side_effects=True, vmem_limit_bytes=52 * 1024 * 1024
        ),
        name="layer",
    )(*ins)
    sds = jax.ShapeDtypeStruct
    shapes = [sds((1, *r.shape) if k < 4 else r.shape, r.dtype) for k, r in enumerate(results)]
    return tuple(
        pl.pallas_call(
            deliver_kernel,
            out_shape=shapes,
            in_specs=[vmem] * 19,
            out_specs=[anyspace] * 19,
            scratch_shapes=[pltpu.SemaphoreType.DMA((19,))],
            compiler_params=pltpu.CompilerParams(vmem_limit_bytes=8 * 1024 * 1024),
            name="deliver",
        )(*results)
    )


def solution(mesh):
    in_specs = (
        P("grp", "edge", None),
        P("grp", "edge", None),
        P("grp", "edge", None),
        P("grp", "edge", None),
        P("grp", "edge"),
        P("grp", "edge"),
        P("grp", "edge"),
        P(("edge", "grp"), None),
        P(("edge", "grp"), None),
        P(("edge", "grp"), None),
        P(("edge", "grp"), None),
        P(None, ("edge", "grp")),
        P(("edge", "grp"), None),
        P(("edge", "grp"), None),
        P(("edge", "grp"), None),
        P(("edge", "grp"), None),
        P(None, ("edge", "grp")),
        P(("edge", "grp"), None),
        P(("edge", "grp"), None),
        P(("edge", "grp"), None),
        P(("edge", "grp"), None),
        P(None, ("edge", "grp")),
    )
    out_specs = (
        P("grp", "edge", None),
        P("grp", "edge", None),
        P("grp", "edge", None),
        P("grp", "edge", None),
        P(("edge", "grp"), None),
        P(("edge", "grp"), None),
        P(("edge", "grp"), None),
        P(("edge", "grp"), None),
        P(None, ("edge", "grp")),
        P(("edge", "grp"), None),
        P(("edge", "grp"), None),
        P(("edge", "grp"), None),
        P(("edge", "grp"), None),
        P(None, ("edge", "grp")),
        P(("edge", "grp"), None),
        P(("edge", "grp"), None),
        P(("edge", "grp"), None),
        P(("edge", "grp"), None),
        P(None, ("edge", "grp")),
    )
    return jax.shard_map(
        functools.partial(on_device, mesh.shape["edge"], mesh.shape["grp"]),
        mesh=mesh, in_specs=in_specs, out_specs=out_specs, check_vma=False
    )
```

```python
import functools

import jax
import jax.numpy as jnp
from jax import lax
from jax.experimental import pallas as pl
from jax.experimental.pallas import tpu as pltpu
from jax.sharding import PartitionSpec as P

step_count = 10.0


def inner(left, right):
    return lax.dot_general(
        left, right, (((0,), (0,)), ((), ())), preferred_element_type=jnp.float32
    )


def times_t(left, right):
    return lax.dot_general(
        left, right, (((1,), (1,)), ((), ())), preferred_element_type=jnp.float32
    )


def norm_stats(values):
    mean = jnp.mean(values, axis=-1, keepdims=True)
    centred = values - mean
    var = jnp.mean(centred * centred, axis=-1, keepdims=True)
    rstd = lax.rsqrt(var + 1e-05)
    return (centred * rstd, rstd)


def norm_back(grad_out, normed, rstd, gain):
    scaled = grad_out * gain
    return rstd * (
        scaled
        - jnp.mean(scaled, axis=-1, keepdims=True)
        - normed * jnp.mean(scaled * normed, axis=-1, keepdims=True)
    )


def silu_slope(values):
    sig = jax.nn.sigmoid(values)
    return sig * (1.0 + values * (1.0 - sig))


def adamw(weight, grad, first, second, rate):
    first_new = 0.9 * first + 0.1 * grad
    second_new = 0.999 * second + 0.001 * grad * grad
    mhat = first_new / (1.0 - 0.9**step_count)
    vhat = second_new / (1.0 - 0.999**step_count)
    return (weight - rate * (mhat / (jnp.sqrt(vhat) + 1e-08) + 0.1 * weight), second_new)


def native(
    edge_lat,
    node_lat,
    edge_cot,
    node_cot,
    senders,
    receivers,
    edge_count,
    w_edge_in,
    w_edge_out,
    w_node_in,
    w_node_out,
    small_params,
    first_edge_in,
    first_edge_out,
    first_node_in,
    first_node_out,
    first_small,
    second_edge_in,
    second_edge_out,
    second_node_in,
    second_node_out,
    second_small,
):
    bf = jnp.bfloat16
    edges = edge_lat[0]
    nodes = node_lat[0]
    send = senders[0]
    recv = receivers[0]
    rows = edges.shape[0]
    width = edges.shape[1]
    maskf = (jnp.arange(rows, dtype=jnp.int32) < edge_count[0, 0]).astype(jnp.float32)[:, None]
    w1e, w2e, w1n, w2n, small = (
        lax.all_gather(w_edge_in.astype(bf), ("edge", "grp"), axis=0, tiled=True),
        lax.all_gather(w_edge_out.astype(bf), ("edge", "grp"), axis=0, tiled=True),
        lax.all_gather(w_node_in.astype(bf), ("edge", "grp"), axis=0, tiled=True),
        lax.all_gather(w_node_out.astype(bf), ("edge", "grp"), axis=0, tiled=True),
        lax.all_gather(small_params.astype(bf), ("edge", "grp"), axis=1, tiled=True),
    )
    params = small.astype(jnp.float32)
    whole = lax.all_gather(nodes, "edge", axis=0, tiled=True)
    node_total = whole.shape[0]
    joined = jnp.concatenate([edges, whole[send], whole[recv]], axis=1)
    pre = jnp.dot(joined, w1e, preferred_element_type=jnp.float32) + params[0]
    hidden = jax.nn.silu(pre).astype(bf)
    out = jnp.dot(hidden, w2e, preferred_element_type=jnp.float32) + params[1]
    normed, rstd = norm_stats(out)
    edge_new = edges.astype(jnp.float32) + maskf * (normed * params[2] + params[3])
    dense = jnp.zeros((node_total, width), jnp.float32).at[recv].add(maskf * edge_new)
    agg = lax.psum_scatter(dense, "edge", scatter_dimension=0, tiled=True)
    node_in = jnp.concatenate([nodes, agg.astype(bf)], axis=1)
    pre_n = jnp.dot(node_in, w1n, preferred_element_type=jnp.float32) + params[4]
    hidden_n = jax.nn.silu(pre_n).astype(bf)
    out_n = jnp.dot(hidden_n, w2n, preferred_element_type=jnp.float32) + params[5]
    normed_n, rstd_n = norm_stats(out_n)
    node_new = nodes.astype(jnp.float32) + normed_n * params[6] + params[7]
    grad_node_out_f = node_cot[0].astype(jnp.float32)
    d_out_n = norm_back(grad_node_out_f, normed_n, rstd_n, params[6]).astype(bf)
    gain_n = jnp.sum(grad_node_out_f * normed_n, axis=0)
    shift_n = jnp.sum(grad_node_out_f, axis=0)
    g_w2n = inner(hidden_n, d_out_n)
    g_b2n = jnp.sum(d_out_n.astype(jnp.float32), axis=0)
    d_pre_n = (times_t(d_out_n, w2n) * silu_slope(pre_n)).astype(bf)
    g_w1n = inner(node_in, d_pre_n)
    g_b1n = jnp.sum(d_pre_n.astype(jnp.float32), axis=0)
    d_node_in = times_t(d_pre_n, w1n)
    node_part = grad_node_out_f + d_node_in[:, :width]
    d_agg = d_node_in[:, width:].astype(bf)
    agg_rows = lax.all_gather(d_agg, "edge", axis=0, tiled=True)
    d_edge = edge_cot[0].astype(jnp.float32) + maskf * agg_rows[recv].astype(jnp.float32)
    masked = maskf * d_edge
    d_out = norm_back(masked, normed, rstd, params[2]).astype(bf)
    gain_e = jnp.sum(masked * normed, axis=0)
    shift_e = jnp.sum(masked, axis=0)
    g_w2e = inner(hidden, d_out)
    g_b2e = jnp.sum(d_out.astype(jnp.float32), axis=0)
    d_pre = (times_t(d_out, w2e) * silu_slope(pre)).astype(bf)
    g_w1e = inner(joined, d_pre)
    g_b1e = jnp.sum(d_pre.astype(jnp.float32), axis=0)
    d_joined = times_t(d_pre, w1e)
    edge_grad = (d_edge + d_joined[:, :width]).astype(bf)
    dense_grad = jnp.zeros((node_total, width), jnp.float32)
    dense_grad = (
        dense_grad.at[send]
        .add(d_joined[:, width : 2 * width])
        .at[recv]
        .add(d_joined[:, 2 * width :])
    )
    node_sum = lax.psum_scatter(dense_grad, "edge", scatter_dimension=0, tiled=True)
    node_grad = (node_part + node_sum).astype(bf)
    g_small = jnp.stack([g_b1e, g_b2e, gain_e, shift_e, g_b1n, g_b2n, gain_n, shift_n])
    grads = (
        lax.psum_scatter(g_w1e, ("edge", "grp"), scatter_dimension=0, tiled=True),
        lax.psum_scatter(g_w2e, ("edge", "grp"), scatter_dimension=0, tiled=True),
        lax.psum_scatter(g_w1n, ("edge", "grp"), scatter_dimension=0, tiled=True),
        lax.psum_scatter(g_w2n, ("edge", "grp"), scatter_dimension=0, tiled=True),
        lax.psum_scatter(g_small, ("edge", "grp"), scatter_dimension=1, tiled=True),
    )
    weights = (w_edge_in, w_edge_out, w_node_in, w_node_out, small_params)
    firsts = (first_edge_in, first_edge_out, first_node_in, first_node_out, first_small)
    seconds = (second_edge_in, second_edge_out, second_node_in, second_node_out, second_small)
    rates = (0.03, 0.03, 0.03, 0.03, 0.2)
    updated = [
        adamw(w, g, m, v, r) for w, g, m, v, r in zip(weights, grads, firsts, seconds, rates)
    ]
    return (
        edge_new.astype(bf)[None],
        node_new.astype(bf)[None],
        edge_grad[None],
        node_grad[None],
        grads[0],
        grads[1],
        grads[2],
        grads[3],
        grads[4],
        updated[0][1],
        updated[1][1],
        updated[2][1],
        updated[3][1],
        updated[4][1],
        updated[0][0],
        updated[1][0],
        updated[2][0],
        updated[3][0],
        updated[4][0],
    )


bf16 = jnp.bfloat16
f32 = jnp.float32
MESH = pl.DeviceIdType.MESH


def mm(left, right):
    return jnp.dot(left, right, preferred_element_type=f32)


def fold_rows(values):
    count, width = values.shape
    return jnp.sum(values.reshape(count // 8, 8, width), axis=0)


GEO = {
    "x_first": (True, True, False, True),
    "diagonal": (),
    "bits_a": True,
    "bits_n": True,
    "bits_b": False,
    "bits_d": True,
    "bits_agg": False,
    "bits_node": False,
    "bits_w": (False, False, False, False),
    "gather": (
        200, 700, 100, 10, 101, 20, 11, 21, 120, 110, 600, 30, 111, 31, 610, 220, 121, 210, 130,
        300, 131, 230, 620
    ),
    "late": (
        310, 320, 400, 410, 420
    ),
    "mid": (
        330, 430
    ),
    "agg": (
        30, 600, 10, 20, 111, 121, 131, 230, 0, 210, 101, 220, 221, 610, 620, 231, 211, 200, 630,
        201, 300, 301, 700, 701, 320, 800, 420, 410, 321, 421, 500, 411, 510, 520, 430, 530, 431
    ),
    "tail": (
        2032, 9050, 2031, 2033, 9051, 10051, 10050, 0, 3032, 2030, 10, 5060, 8050, 1000, 1010, 3033,
        3030, 1012, 1001, 1002, 20, 5073, 5083, 1022, 3031, 8051, 1003, 5082, 2003, 2002, 2013,
        1020, 5072, 5081, 2011, 5071, 1011, 1013, 2012, 2001, 7050, 5070, 1021, 1023, 5080, 5102,
        3003, 2023, 3013, 2021, 3002, 5090, 5092, 4030, 2022, 8052, 4002, 3011, 3012, 2010, 3001,
        2000, 4032, 2020, 4012, 3023, 5100, 3022, 3021, 3020, 8053, 3010, 6040, 4010, 3000, 8054,
        6030, 4000, 6000, 4020, 6010, 4022, 6020
    ),
}


def decode(step, unit):
    return step // (10 * unit), step // 10 % unit, step % 10


def layer_kernel(geo, *refs):
    Z, Y, X, C = geo["dims"]
    n_sem = geo["n_sem"]
    (
        edges_hbm,
        cot_hbm,
        nodes_hbm,
        ncot_hbm,
        send_hbm,
        recv_hbm,
        count_in,
        w1_hbm,
        w2_hbm,
        w3_hbm,
        w4_hbm,
        small_hbm,
        *rest,
    ) = refs
    moments_hbm, rest = rest[:10], rest[10:]
    enew, nnew_out, egrad, ngrad_out, *rest = rest
    grads_out, seconds_out, weights_out, rest = rest[0:5], rest[5:10], rest[10:15], rest[15:]
    g1_out, g2_out, g3_out, g4_out, gs_out = grads_out
    moments_in, rest = rest[:10], rest[10:]
    (
        edges,
        cot,
        nodes_in,
        ncot_in,
        send_in,
        recv_in,
        w1_in,
        w2_in,
        w3_in,
        w4_in,
        small_in,
        nbuf,
        dbuf,
        w1,
        w2,
        w3,
        w4,
        wa,
        wb,
        pick,
        spread,
        proj,
        slope,
        hidden,
        normed,
        rstd,
        term,
        dedge,
        dout,
        dpre,
        sums,
        pf,
        pb_a,
        pb_n,
        yr_a,
        yr_n,
        zs_a,
        zs_n,
        zr_a,
        zr_n,
        seg,
        pre_own,
        norm_n,
        node_part,
        agg_low,
        hidden_n,
        dout_n,
        dpre_n,
        sm_src,
        sm_rcv,
        sm_tile,
        par_all,
        gm_src,
        gm_rcv,
        gm_tile,
        gsm,
        *grad_refs,
    ) = rest
    local_sem, ssem, rsem = grad_refs[-3:]
    grad_refs = grad_refs[:-3]
    rows, D = edges.shape
    n = nodes_in.shape[0]
    N = Z * Y * n
    R = rows // 2

    e_id = lax.axis_index("edge")
    g_id = lax.axis_index("grp")
    z = e_id // Y
    y = e_id % Y
    x = g_id // C
    c = g_id % C
    yp, xp, cp = 1 - y, 1 - x, 1 - c
    me = e_id * (X * C) + g_id
    y_dev = (z * Y + yp, g_id)
    x_dev = (e_id, xp * C + c)
    c_dev = (e_id, x * C + cp)
    xy_dev = (z * Y + yp, xp * C + c)

    def zx(m):
        place = z
        for j in range(m.bit_length()):
            if m >> j & 1:
                place = place + (1 << j) - (2 << j) * (z // (1 << j) % 2)
        return place

    def z_dev(m):
        return (zx(m) * Y + y, g_id)

    started = []

    def push(src, dst, dev):
        k = len(started)
        assert k < n_sem
        copy = pltpu.make_async_remote_copy(
            src_ref=src,
            dst_ref=dst,
            send_sem=ssem.at[k],
            recv_sem=rsem.at[k],
            device_id=dev,
            device_id_type=MESH,
        )
        copy.start()
        started.append(copy)
        return copy

    barrier = pltpu.get_barrier_semaphore()
    peers = [z_dev(m) for m in range(1, Z)] + [y_dev, x_dev, c_dev, xy_dev]
    for dev in peers:
        pl.semaphore_signal(barrier, inc=1, device_id=dev, device_id_type=MESH)
    loads = [
        (w1_hbm, w1_in),
        (w2_hbm, w2_in),
        (w3_hbm, w3_in),
        (w4_hbm, w4_in),
        (small_hbm, small_in),
        (nodes_hbm, nodes_in),
        (send_hbm, send_in),
        (recv_hbm, recv_in),
        (ncot_hbm, ncot_in),
        (edges_hbm, edges),
        (cot_hbm, cot),
        *zip(moments_hbm, moments_in),
    ]
    loads = [pltpu.make_async_copy(*pair, local_sem.at[k]) for k, pair in enumerate(loads)]
    for load in loads:
        load.start()
    for load in loads[0:6]:
        load.wait()
    r1, r2, r3, r4 = (own.shape[0] for own in (w1_in, w2_in, w3_in, w4_in))
    ra = r1 + r2
    wa[z, y, x, c, 0:r1, :] = w1_in[...].astype(bf16)
    wa[z, y, x, c, r1:ra, :] = w2_in[...].astype(bf16)
    wb[z, y, x, c, 0:r3, :] = w3_in[...].astype(bf16)
    wb[z, y, x, c, r3 : r3 + r4, :] = w4_in[...].astype(bf16)
    nbuf[z, y] = nodes_in[...]
    ws = small_in.shape[1]
    wide = ws * Y * X * C
    first = me % (Y * X * C) * ws
    place = (
        lax.broadcasted_iota(jnp.int32, (ws, wide), 1)
        == lax.broadcasted_iota(jnp.int32, (ws, wide), 0) + first
    )
    sm_src[0] = mm(small_in[...].astype(bf16), jnp.where(place, 1.0, 0.0).astype(bf16))

    def update(k):
        weight = (w1_in, w2_in, w3_in, w4_in, small_in)[k]
        weights_out[k][...], seconds_out[k][...] = adamw(
            weight[...],
            grads_out[k][...],
            moments_in[k][...],
            moments_in[5 + k][...],
            0.2 if k == 4 else 0.03,
        )

    pl.semaphore_wait(barrier, len(peers))

    def along_z(own, by_bits):
        to = [1 << j for j in range((Z - 1).bit_length())] if by_bits else range(1, Z)
        return {m: push(own, own, z_dev(m)) for m in reversed(to)}

    def arrive_z(copies, m, block):
        copies[m].wait_recv()
        j = 0 if len(copies) < Z - 1 else Z
        while not m >> j & 1 and j < Z:
            copies[m | 1 << j] = push(block, block, z_dev(1 << j))
            j += 1

    halves = ra // 2

    def part(zz, yy, xx, h):
        return wa.at[zz, yy, xx, c, h * halves : (h + 1) * halves, :]

    def send(block, dev):
        return push(block, block, dev)

    def settle(zz, yy, xx, cc):
        k = ((zz * Y + yy) * X + xx) * C + cc
        w1[pl.ds(pl.multiple_of(k * r1, 16), r1), :] = wa[zz, yy, xx, cc, 0:r1, :]
        w2[pl.ds(pl.multiple_of(k * r2, 16), r2), :] = wa[zz, yy, xx, cc, r1:ra, :]

    def small_sum(src, rcv, stage, copy):
        copy.wait_recv()
        src[stage + 1] = src[stage] + rcv[stage]

    small = [push(sm_src.at[0], sm_rcv.at[0], c_dev)]
    a_z, a_y, a_x, a_c, x_order = ({}, {}), {}, [], [], []
    n_z, n_y, b_z, b_y, b_x = {}, [], {}, [], []
    for h in range(2):
        own = part(z, y, x, h)
        a_z[h].update(along_z(own, geo["bits_a"]))
        a_y[0, h] = send(own, y_dev)
        a_x.append(send(own, x_dev))
        x_order.append((0, 0, h))
    a_c.append(send(wa.at[z, y, x, c], c_dev))

    def across(m, flip, h):
        yy = yp if flip else y
        straight = m in geo["diagonal"]
        if not (flip and straight):
            a_x.append(send(part(zx(m), yy, x, h), x_dev))
            x_order.append((m, flip, h))
        if straight and not flip:
            a_x.append(send(part(zx(m), yy, x, h), xy_dev))
            x_order.append((m, 1, h))
        if h == 1:
            a_c.append(send(wa.at[zx(m), yy, x, c], c_dev))
            settle(zx(m), yy, x, c)

    def on_z(m, h):
        block = part(zx(m), y, x, h)
        arrive_z(a_z[h], m, block)
        a_y[m, h] = send(block, y_dev)
        across(m, 0, h)

    def on_y(m, h):
        a_y[m, h].wait_recv()
        across(m, 1, h)

    def on_n(m, _):
        block = nbuf.at[zx(m), y]
        if m == 0:
            n_z.update(along_z(block, geo["bits_n"]))
        else:
            arrive_z(n_z, m, block)
        n_y.append(send(block, y_dev))

    def on_b(m, _):
        block = wb.at[zx(m), y, x, c]
        if m == 0:
            b_z.update(along_z(block, geo["bits_b"]))
        else:
            arrive_z(b_z, m, block)

    def line_b(m, _):
        block = wb.at[zx(m), y, x, c]
        b_y.append(send(block, y_dev))
        b_x.append(send(block, x_dev))

    def on_x(first, last):
        for k in range(first, last):
            m, flip, h = x_order[k]
            a_x[k].wait_recv()
            if h == 1:
                yy = yp if flip else y
                a_c.append(send(wa.at[zx(m), yy, xp, c], c_dev))
                settle(zx(m), yy, xp, c)

    def on_small(k, _):
        small_sum(sm_src, sm_rcv, k, small[k])
        if k < 2:
            small.append(push(sm_src.at[k + 1], sm_rcv.at[k + 1], (y_dev, x_dev)[k]))
        else:
            sm_tile[z] = sm_src[3]
            small.extend(push(sm_src.at[3], sm_tile.at[z], z_dev(m)) for m in range(1, Z))

    settle(z, y, x, c)
    def on_hot(*_):
        for load in loads[6:9]:
            load.wait()
        lane = lax.broadcasted_iota(jnp.int32, (128, N), 1)
        sub = lax.broadcasted_iota(jnp.int32, (N, 128), 0)

        @pl.loop(0, rows // 128)
        def _(k):
            at = pl.ds(pl.multiple_of(k * 128, 128), 128)
            for half, ids in enumerate((send_in, recv_in)):
                row = jnp.broadcast_to(ids[0:1, at], (128, 128))
                col = jnp.tile(row.T, (1, N // 128))
                pick[at, half * N : (half + 1) * N] = jnp.where(lane == col, 1.0, 0.0).astype(bf16)
                flat = jnp.broadcast_to(ids[0:1, at], (N, 128))
                spread[half * N : (half + 1) * N, at] = jnp.where(sub == flat, 1.0, 0.0).astype(bf16)

    steps = (on_z, on_y, on_n, on_b, line_b, on_x, on_small, on_hot)

    def gather(name):
        for step in geo[name]:
            kind, m, h = decode(step, 10)
            if kind > 5 or m < Z:
                steps[kind](m, h)

    gather("gather")
    on_x(0, len(x_order))
    for copy in n_y:
        copy.wait_recv()
    loads[9].wait()
    for copy in a_c:
        copy.wait_recv()
    gather("late")
    for zz in range(Z):
        for yy in range(Y):
            for xx in range(X):
                settle(zz, yy, xx, cp)
    for copy in small[3:]:
        copy.wait_recv()
    for zz in range(Z):
        par_all[:, zz * wide : (zz + 1) * wide] = sm_tile[zz]

    nodes_all = nbuf[...].reshape(N, D)
    proj[0:N, :] = mm(nodes_all, w1[D : 2 * D, :]).astype(bf16)
    proj[N : 2 * N, :] = mm(nodes_all, w1[2 * D : 3 * D, :]).astype(bf16)
    count = count_in[0, 0]
    row_id = lax.broadcasted_iota(jnp.int32, (R, D), 0)

    def edge_forward(i):
        at = slice(i * R, (i + 1) * R)
        live = row_id < count - i * R
        own = edges[at, :]
        pre = mm(own, w1[0:D, :]) + mm(pick[at, :], proj[...]) + par_all[0:1, :]
        sig = jax.nn.sigmoid(pre)
        act = (pre * sig).astype(bf16)
        hidden[at, :] = act
        slope[at, :] = sig * (1.0 + pre * (1.0 - sig))
        out = mm(act, w2[...]) + par_all[1:2, :]
        norm, inv = norm_stats(out)
        normed[at, :] = norm
        rstd[at, :] = jnp.broadcast_to(inv, (R, 128))
        new = own.astype(f32) + jnp.where(live, norm * par_all[2:3, :] + par_all[3:4, :], 0.0)
        enew[at, :] = new.astype(bf16)
        term[at, :] = jnp.where(live, new, 0.0).astype(bf16)

    edge_forward(0)
    gather("mid")
    edge_forward(1)

    order = tuple(reversed(range(Z)))

    class NodeSum:
        def __init__(self, by_bits, pb, yr, zs, zr):
            self.by_bits = by_bits
            self.pb, self.yr, self.zs, self.zr = pb, yr, zs, zr
            self.y, self.z = {}, {}

        def put(self, m, values):
            pf[zx(m)] = values.reshape(Y, 2, n // 2, D)
            self.pb[zx(m)] = values.astype(bf16).reshape(Y, 2, n // 2, D)

        def go(self, m, h):
            self.y[m, h] = push(self.pb.at[zx(m), yp, h], self.yr.at[m, h], y_dev)

        def over(self, m, h, low):
            self.zs[m - 1, h] = pf[zx(m), y, h].astype(bf16)
            self.z[m, h] = push(self.zs.at[m - 1, h], self.zr.at[m - 1, h], z_dev(low))

        def turn(self, m, h):
            self.y[m, h].wait_recv()
            pf[zx(m), y, h] = pf[zx(m), y, h] + self.yr[m, h].astype(f32)
            if not self.by_bits and m:
                self.over(m, h, m)
            elif m % 2:
                self.over(m, h, 1)

        def merge(self, m, h):
            if not self.by_bits:
                return
            self.z[m + 1, h].wait_recv()
            pf[zx(m), y, h] = pf[zx(m), y, h] + self.zr[m, h].astype(f32)
            if m:
                self.over(m, h, 2)

        def total(self, h):
            part = pf[z, y, h]
            for m in range(2, Z, 2) if self.by_bits else range(1, Z):
                self.z[m, h].wait_recv()
                part = part + self.zr[m - 1, h].astype(f32)
            return part

    class WeightSum:
        def __init__(self, x_first, by_bits, grad, crecv, xs, xrecv, ks, ys, yrecv, zs, zrecv):
            self.by_bits = by_bits
            self.first, self.second = (x_dev, y_dev) if x_first else (y_dev, x_dev)
            side = ((y, xp), (yp, x)) if x_first else ((yp, x), (y, xp))
            self.groups = ((yp, xp), side[0], side[1], (y, x))
            self.grad, self.crecv, self.xs, self.xrecv, self.ks = grad, crecv, xs, xrecv, ks
            self.ys, self.yrecv, self.zs, self.zrecv = ys, yrecv, zs, zrecv

        def put(self, first, values, lane_rows=None, base=0):
            low, r = values.astype(bf16), lane_rows or self.grad.shape[4]
            row = 0
            while row < values.shape[0]:
                k, off = divmod(first + row, r)
                size = min(r - off, values.shape[0] - row)
                at = (k // (Y * X * C), k // (X * C) % Y, k // C % X, k % C)
                self.grad[(*at, slice(base + off, base + off + size))] = low[row : row + size]
                row += size

        def start(self):
            self.c = [
                push(self.grad.at[:, yy, xx, cp], self.crecv.at[k], c_dev)
                for k, (yy, xx) in enumerate(self.groups)
            ]

            self.x, self.y, self.z = {}, {}, {}

        def cross_x(self, k):
            self.c[k].wait_recv()
            for m in order:
                part = self.grad[(zx(m), *self.groups[k], c)].astype(f32)
                part = part + self.crecv[k, zx(m)].astype(f32)
                if k < 2:
                    self.xs[k, m] = part.astype(bf16)
                    self.x[k, m] = push(self.xs.at[k, m], self.xrecv.at[k, m], self.first)
                else:
                    self.ks[k - 2, m] = part

        def cross_y(self, m):
            self.x[0, m].wait_recv()
            self.ys[m] = (self.ks[0, m] + self.xrecv[0, m].astype(f32)).astype(bf16)
            self.y[m] = push(self.ys.at[m], self.yrecv.at[m], self.second)

        def cross_z(self, m):
            self.x[1, m].wait_recv()
            self.y[m].wait_recv()
            part = self.ks[1, m] + self.xrecv[1, m].astype(f32) + self.yrecv[m].astype(f32)
            if not self.by_bits and m:
                self.over(part, m, m)
            elif m % 2:
                self.over(part, m, 1)
            else:
                self.ks[1, m] = part

        def over(self, part, m, low):
            self.zs[m - 1] = part.astype(bf16)
            self.z[m] = push(self.zs.at[m - 1], self.zrecv.at[m - 1], z_dev(low))

        def merge(self, m):
            if not self.by_bits:
                return
            self.z[m + 1].wait_recv()
            part = self.ks[1, m] + self.zrecv[m].astype(f32)
            if m:
                self.over(part, m, 2)
            else:
                self.ks[1, 0] = part

        def total(self):
            result = self.ks[1, 0]
            for m in range(2, Z, 2) if self.by_bits else range(1, Z):
                self.z[m].wait_recv()
                result = result + self.zrecv[m - 1].astype(f32)
            return result

    per = len(grad_refs) // 4
    sum1a, sum1b, sum2, sum_n = [
        WeightSum(geo["x_first"][k], geo["bits_w"][k], *grad_refs[k * per : (k + 1) * per]) for k in range(4)
    ]

    agg_sum = NodeSum(geo["bits_agg"], pb_a, yr_a, zs_a, zr_a)
    b_c = []

    def step_p(m, _):
        first_row = pl.multiple_of(N + zx(m) * (Y * n), Y * n)
        agg_sum.put(m, mm(spread[pl.ds(first_row, Y * n), :], term[...]))
        agg_sum.go(m, 0)

    def step_b(k, _):
        if k == 0:
            for copy in b_y:
                copy.wait_recv()
            b_x.append(send(wb.at[:, yp, x, c], x_dev))
            b_c.extend(send(wb.at[:, yy, x, c], c_dev) for yy in (y, yp))
        elif k == 1:
            for copy in b_x[:-1]:
                copy.wait_recv()
            b_c.append(send(wb.at[:, y, xp, c], c_dev))
        elif k == 2:
            b_x[-1].wait_recv()
            b_c.append(send(wb.at[:, yp, xp, c], c_dev))
        else:
            for copy in b_c:
                copy.wait_recv()
            w3[...] = wb[:, :, :, :, 0:r3, :].reshape(w3.shape)
            w4[...] = wb[:, :, :, :, r3 : r3 + r4, :].reshape(w4.shape)
            pre_own[...] = mm(nodes_in[...], w3[0:D, :])

    def par(k):
        return par_all[k : k + 1, :]

    def step_node(_, h):
        at = slice(h * (n // 2), (h + 1) * (n // 2))
        low = agg_sum.total(h).astype(bf16)
        agg_low[at, :] = low
        pre_n = pre_own[at, :] + mm(low, w3[D : 2 * D, :]) + par(4)
        sig_n = jax.nn.sigmoid(pre_n)
        act_n = (pre_n * sig_n).astype(bf16)
        hidden_n[at, :] = act_n
        normed_n, rstd_n = norm_stats(mm(act_n, w4[...]) + par(5))
        ncot = ncot_in[at, :].astype(f32)
        d_out_n = norm_back(ncot, normed_n, rstd_n, par(6)).astype(bf16)
        dout_n[at, :] = d_out_n
        slope_n = sig_n * (1.0 + pre_n * (1.0 - sig_n))
        d_pre_n = (times_t(d_out_n, w4[...]) * slope_n).astype(bf16)
        dpre_n[at, :] = d_pre_n
        dbuf[z, y, at, :] = times_t(d_pre_n, w3[D : 2 * D, :]).astype(bf16)
        step_d(0, h)
        norm_n[at, :] = normed_n

    d_z, d_y = {}, []

    def d_part(m, h):
        return dbuf.at[zx(m), y, h * (n // 2) : (h + 1) * (n // 2), :]

    def step_d(m, h):
        block = d_part(m, h)
        if m == 0:
            d_z[h] = along_z(block, geo["bits_d"])
        else:
            arrive_z(d_z[h], m, block)
        d_y.append(send(block, y_dev))

    def step_wn(*_):
        own_nodes, ncot = nodes_in[...], ncot_in[...].astype(f32)
        normed_n, d_pre_n, d_out_n = norm_n[...], dpre_n[...], dout_n[...]
        sum_n.put(0, inner(own_nodes, d_pre_n), r3)
        sum_n.put(D, inner(agg_low[...], d_pre_n), r3)
        sum_n.put(0, inner(hidden_n[...], d_out_n), r4, r3)
        sum_n.start()
        nnew_out[...] = (own_nodes.astype(f32) + normed_n * par(6) + par(7)).astype(bf16)
        node_part[...] = ncot + times_t(d_pre_n, w3[0:D, :])
        gsm[4:5, :] = jnp.sum(d_pre_n.astype(f32), axis=0, keepdims=True)
        gsm[5:6, :] = jnp.sum(d_out_n.astype(f32), axis=0, keepdims=True)
        gsm[6:7, :] = jnp.sum(ncot * normed_n, axis=0, keepdims=True)
        gsm[7:8, :] = jnp.sum(ncot, axis=0, keepdims=True)

    steps_n = (
        step_p,
        agg_sum.go,
        agg_sum.turn,
        agg_sum.merge,
        step_d,
        lambda k, _: sum_n.cross_x(k),
        step_b,
        step_node,
        step_wn,
    )
    for step in geo["agg"]:
        kind, m, h = decode(step, 10)
        if kind > 4 or m < Z:
            steps_n[kind](m, h)
    for load in loads[10:]:
        load.wait()
    for copy in d_y:
        copy.wait_recv()

    sums[...] = jnp.zeros_like(sums)

    def add_sums(k, at, values):
        sums[k, :, at] += fold_rows(values)

    d_all = dbuf[...].reshape(N, D)

    def step_v(_, i):
        at = slice(i * R, (i + 1) * R)
        live = row_id < count - i * R
        d_edge = cot[at, :].astype(f32) + jnp.where(live, mm(pick[at, N : 2 * N], d_all), 0.0)
        dedge[at, :] = d_edge
        masked = jnp.where(live, d_edge, 0.0)
        norm = normed[at, :]
        inv = rstd[at, 0:1]
        weighted = masked * norm
        add_sums(2, slice(0, D), weighted)
        add_sums(3, slice(0, D), masked)
        d_out = norm_back(masked, norm, inv, par(2)).astype(bf16)
        dout[at, :] = d_out
        add_sums(1, slice(0, D), d_out.astype(f32))

    def step_d(_, k):
        at = slice(k * (D // 2), (k + 1) * (D // 2))
        d_pre = (times_t(dout[...], w2[at, :]) * slope[:, at]).astype(bf16)
        dpre[:, at] = d_pre
        add_sums(0, at, d_pre.astype(f32))

    edges_all = edges[...]

    def edge_grads(k, into):
        at = slice(k * (D // 2), (k + 1) * (D // 2))
        d_pre = dpre[:, at]
        into.put(0, inner(edges_all, d_pre))
        for half in range(2):
            nodes_at = slice(half * N, (half + 1) * N)
            seg[nodes_at, at] = mm(spread[nodes_at, :], d_pre).astype(bf16)
            into.put((1 + half) * D, inner(nodes_all, seg[nodes_at, at]))
        into.start()

    sums_w = (sum1a, sum1b, sum2, sum_n)
    gm = []
    node_sum = NodeSum(geo["bits_node"], pb_n, yr_n, zs_n, zr_n)

    def step_w(which, _):
        if which == 2:
            sum2.put(0, inner(hidden[...], dout[...]))
            sum2.start()
        else:
            edge_grads(which, sums_w[which])

    def step_t(which, _):
        if which == 4:
            for h in range(2):
                at = slice(h * (n // 2), (h + 1) * (n // 2))
                ngrad_out[at, :] = (node_part[at, :] + node_sum.total(h)).astype(bf16)
            return
        result = sums_w[which].total()
        if which == 3:
            g3_out[...] = result[0:r3]
            g4_out[...] = result[r3 : r3 + r4]
            update(2)
            update(3)
        elif which == 2:
            g2_out[...] = result
            update(1)
        else:
            g1_out[:, which * (D // 2) : (which + 1) * (D // 2)] = result

    def step_n(which, k):
        if which == 6:
            total = times_t(seg[0:N, :], w1[D : 2 * D, :])
            total = total + times_t(seg[N : 2 * N, :], w1[2 * D : 3 * D, :])
            pf[...] = total.reshape(pf.shape)
            pb_n[...] = total.astype(bf16).reshape(pf.shape)
            for m in order:
                for h in range(2):
                    node_sum.go(m, h)
        elif which < 9:
            node_sum.turn(k, which - 7)
        else:
            node_sum.merge(k, which - 9)

    def step_e(*_):
        for i in range(2):
            at = slice(i * R, (i + 1) * R)
            egrad[at, :] = (dedge[at, :] + times_t(dpre[at, :], w1[0:D, :])).astype(bf16)

    def step_g(_, k):
        if k == 0:
            for row in range(4):
                gsm[row : row + 1, :] = jnp.sum(sums[row], axis=0, keepdims=True)
            for zz in range(Z):
                gm_tile[zz] = gsm[:, zz * wide : (zz + 1) * wide]
            gm.extend(
                push(gm_tile.at[zx(m)], gm_tile.at[Z + m - 1], z_dev(m)) for m in range(1, Z)
            )
        elif k == 1:
            tile = gm_tile[z]
            for m in range(1, Z):
                gm[m - 1].wait_recv()
                tile = tile + gm_tile[Z + m - 1]
            gm_src[0] = tile
            gm.append(push(gm_src.at[0], gm_rcv.at[0], y_dev))
        else:
            small_sum(gm_src, gm_rcv, k - 2, gm[-1])
            if k < 4:
                gm.append(push(gm_src.at[k - 1], gm_rcv.at[k - 1], (x_dev, c_dev)[k - 2]))
                return
            take = (
                lax.broadcasted_iota(jnp.int32, (wide, ws), 0)
                == lax.broadcasted_iota(jnp.int32, (wide, ws), 1) + first
            )
            gs_out[...] = jnp.dot(
                gm_src[3],
                jnp.where(take, 1.0, 0.0),
                preferred_element_type=f32,
                precision=lax.Precision.HIGHEST,
            )
            update(4)

    tail = (
        step_w,
        lambda which, k: sums_w[which].cross_x(k),
        lambda which, m: sums_w[which].cross_y(m),
        lambda which, m: sums_w[which].cross_z(m),
        lambda which, m: sums_w[which].merge(m),
        step_n,
        step_t,
        step_e,
        step_g,
        step_v,
        step_d,
    )
    for step in geo["tail"]:
        kind, which, k = decode(step, 100)
        if not 2 <= kind <= 5 or k < Z:
            tail[kind](which, k)
    update(0)
    for copy in started:
        copy.wait_send()


def deliver_kernel(*refs):
    count = len(refs) // 2
    copies = []
    for k in range(count):
        dst = refs[count + k]
        dst = dst.at[0] if k < 4 else dst
        copies.append(pltpu.make_async_copy(refs[k], dst, refs[-1].at[k]))
    for copy in copies:
        copy.start()
    for copy in copies:
        copy.wait()


def on_device(n_edge, n_grp, *args):
    (
        edge_lat,
        node_lat,
        edge_cot,
        node_cot,
        senders,
        receivers,
        edge_count,
        *state,
    ) = args
    weights, firsts, seconds = state[0:5], state[5:10], state[10:15]
    rows, D = edge_lat.shape[1:]
    n = node_lat.shape[1]
    N = n * n_edge
    n_dev = n_edge * n_grp
    shards = [w.shape[0] for w in weights[:4]]
    fits = (
        n_edge % 2 == 0
        and n_grp == 4
        and all(r % 16 == 0 for r in shards)
        and n_edge // 2 in (2, 4)
        and D % (128 * (n_edge // 2)) == 0
        and D % 256 == 0
        and N % 128 == 0
        and n % 32 == 0
        and (shards[0] + shards[1]) % 32 == 0
        and rows % 256 == 0
        and rows * N <= 1024 * 1024
    )
    if not fits:
        return native(*args)
    Z, Y, X, C = n_edge // 2, 2, 2, 2
    n_sem = 240

    def vm(shape, dtype=bf16):
        return pltpu.VMEM(shape, dtype)

    ins = [edge_lat[0], edge_cot[0], node_lat[0], node_cot[0], senders, receivers, edge_count]
    ins += [*weights, *firsts, *seconds]
    moments = [vm(m.shape, f32) for m in (*firsts, *seconds)]
    scratch = [
        *moments,
        *[vm(a.shape, a.dtype) for a in ins[:12] if a is not edge_count],
        vm((Z, Y, n, D)),
        vm((Z, Y, n, D)),
        *[vm((r * n_dev, D)) for r in shards],
        vm((Z, Y, X, C, shards[0] + shards[1], D)),
        vm((Z, Y, X, C, shards[2] + shards[3], D)),
        vm((rows, 2 * N)),
        vm((2 * N, rows)),
        vm((2 * N, D)),
        vm((rows, D), f32),
        vm((rows, D)),
        vm((rows, D), f32),
        vm((rows, 128), f32),
        vm((rows, D)),
        vm((rows, D), f32),
        vm((rows, D)),
        vm((rows, D)),
        vm((4, 8, D), f32),
        vm((Z, Y, 2, n // 2, D), f32),
        vm((Z, Y, 2, n // 2, D)),
        vm((Z, Y, 2, n // 2, D)),
        vm((Z, 2, n // 2, D)),
        vm((Z, 2, n // 2, D)),
        *[vm((Z - 1, 2, n // 2, D))] * 4,
        vm((2 * N, D)),
        *[vm((n, D), f32)] * 3,
        *[vm((n, D))] * 4,
        vm((4, 8, D // Z), f32),
        vm((3, 8, D // Z), f32),
        vm((Z, 8, D // Z), f32),
        vm((8, D), f32),
        vm((4, 8, D // Z), f32),
        vm((3, 8, D // Z), f32),
        vm((2 * Z - 1, 8, D // Z), f32),
        vm((8, D), f32),
    ]
    blocks = ((shards[0], D // 2), (shards[0], D // 2), (shards[1], D), (shards[2] + shards[3], D))
    for r, cols in blocks:
        scratch += [
            vm((Z, Y, X, C, r, cols)),
            vm((4, Z, r, cols)),
            vm((2, Z, r, cols)),
            vm((2, Z, r, cols)),
            vm((2, Z, r, cols), f32),
            vm((Z, r, cols)),
            vm((Z, r, cols)),
            vm((Z - 1, r, cols)),
            vm((Z - 1, r, cols)),
        ]
    scratch += [
        pltpu.SemaphoreType.DMA((len(ins),)),
        pltpu.SemaphoreType.DMA((n_sem,)),
        pltpu.SemaphoreType.DMA((n_sem,)),
    ]
    hbm = pl.BlockSpec(memory_space=pltpu.HBM)
    anyspace = pl.BlockSpec(memory_space=pl.ANY)
    vmem = pl.BlockSpec(memory_space=pltpu.VMEM)
    state_out = [vm(w.shape, f32) for w in weights]
    results = pl.pallas_call(
        functools.partial(layer_kernel, dict(GEO, dims=(Z, Y, X, C), n_sem=n_sem)),
        out_shape=[vm((rows, D)), vm((n, D))] * 2 + state_out * 3,
        in_specs=[hbm] * 6 + [pl.BlockSpec(memory_space=pltpu.SMEM)] + [hbm] * 15,
        out_specs=[vmem] * 19,
        scratch_shapes=scratch,
        compiler_params=pltpu.CompilerParams(
            collective_id=0, has_side_effects=True, vmem_limit_bytes=52 * 1024 * 1024
        ),
        name="layer",
    )(*ins)
    sds = jax.ShapeDtypeStruct
    shapes = [sds((1, *r.shape) if k < 4 else r.shape, r.dtype) for k, r in enumerate(results)]
    return tuple(
        pl.pallas_call(
            deliver_kernel,
            out_shape=shapes,
            in_specs=[vmem] * 19,
            out_specs=[anyspace] * 19,
            scratch_shapes=[pltpu.SemaphoreType.DMA((19,))],
            compiler_params=pltpu.CompilerParams(vmem_limit_bytes=8 * 1024 * 1024),
            name="deliver",
        )(*results)
    )


def solution(mesh):
    in_specs = (
        P("grp", "edge", None),
        P("grp", "edge", None),
        P("grp", "edge", None),
        P("grp", "edge", None),
        P("grp", "edge"),
        P("grp", "edge"),
        P("grp", "edge"),
        P(("edge", "grp"), None),
        P(("edge", "grp"), None),
        P(("edge", "grp"), None),
        P(("edge", "grp"), None),
        P(None, ("edge", "grp")),
        P(("edge", "grp"), None),
        P(("edge", "grp"), None),
        P(("edge", "grp"), None),
        P(("edge", "grp"), None),
        P(None, ("edge", "grp")),
        P(("edge", "grp"), None),
        P(("edge", "grp"), None),
        P(("edge", "grp"), None),
        P(("edge", "grp"), None),
        P(None, ("edge", "grp")),
    )
    out_specs = (
        P("grp", "edge", None),
        P("grp", "edge", None),
        P("grp", "edge", None),
        P("grp", "edge", None),
        P(("edge", "grp"), None),
        P(("edge", "grp"), None),
        P(("edge", "grp"), None),
        P(("edge", "grp"), None),
        P(None, ("edge", "grp")),
        P(("edge", "grp"), None),
        P(("edge", "grp"), None),
        P(("edge", "grp"), None),
        P(("edge", "grp"), None),
        P(None, ("edge", "grp")),
        P(("edge", "grp"), None),
        P(("edge", "grp"), None),
        P(("edge", "grp"), None),
        P(("edge", "grp"), None),
        P(None, ("edge", "grp")),
    )
    return jax.shard_map(
        functools.partial(on_device, mesh.shape["edge"], mesh.shape["grp"]),
        mesh=mesh, in_specs=in_specs, out_specs=out_specs, check_vma=False
    )
```
